32 devices in a mesh: tier: 4 (over z), aux: 8 (over y, x, core).
Axes of the slice: x: 2, y: 2, z: 4, core: 2. Of those that a mesh axis runs over, the one named last changes fastest.
Arguments:
- section_state: float32 [256, 18432], P(('tier', 'aux')), may hold values from -6 to 6
- coupling: float32 [96, 96], replicated, may hold values from -0.625 to 0.625
- site_energy: float32 [96], replicated, may hold values from -1 to 1
- bath_rate: float32 [96], replicated, may hold values from 0.3 to 3
- bath_strength: float32 [96], replicated, may hold values from 0.1 to 1
- bath_of_site: int32 [96], replicated, may hold values from 0 to 95, each once
- quanta: int32 [256, 4], P(('tier', 'aux')), may hold values from -1 to 95, as said below
- send_list: int32 [32, 48], P(('tier', 'aux')), may hold values from -1 to 31, as said below
- dest_slot: int32 [32, 48], P(('tier', 'aux')), may hold values from 0 to 7
Outputs:
- derivative: float32 [256, 18432], P(('tier', 'aux'))
The draws below stay inside these ranges and needn't reach their ends.
Inputs may be any that keep to these rules, and one draw needn't show every extreme that they name: Row a lists the sites of auxiliary a's quanta, 1 to 4 of them with repeats allowed, in ascending order, then -1 in the empty places. `send_list`: entry [d, l] is slot * 4 + place for an auxiliary slot of device d, or -1. The first place of every distinct site of every auxiliary stands in exactly one lane of its device, and no other place stands anywhere. On every device the 3 lanes of group 0 towards one aux index are all used.
All inputs are finite; a program needn't handle non-finite values.
Results may differ from the reference program's by a relative error of at most 0.00005.
Values sent between devices are 32-bit elements; how exact they have to be, the bound alone decides.
No kernel may reach another device: no remote copies, remote signals or barrier semaphores. Data moves between devices by JAX's collectives and lax.ppermute only.
A program may use at most 64 MiB of HBM per device.

```python
import math
import jax
import jax.numpy as jnp
from jax import lax

SITES = 96
DEPTH = 4
AUX_DEV = 8
PEERS = 8
HOLDERS = 32
AUX = 256
CAP = 3
LANES = 48


def edge_tables(key):
    base = jax.random.fold_in(key, 41)
    tier_key, site_key, peer_key, order_key = jax.random.split(base, 4)
    tier_counts = jax.random.randint(tier_key, (AUX,), 1, DEPTH + 1)
    places = jnp.arange(DEPTH)
    drawn_sites = jax.random.randint(site_key, (AUX, DEPTH), 0, SITES)
    drawn_sites = jnp.where(places[None, :] < tier_counts[:, None], drawn_sites, SITES)
    ordered = jnp.sort(drawn_sites, axis=1)
    quanta = jnp.where(ordered < SITES, ordered, -1).astype(jnp.int32)
    previous = jnp.concatenate([jnp.full((AUX, 1), -2, jnp.int32), quanta[:, :-1]], axis=1)
    firsts = (quanta >= 0) & (quanta != previous)
    per_holder = firsts.reshape(HOLDERS, AUX_DEV * DEPTH)
    edge_rank = jnp.cumsum(per_holder.astype(jnp.int32), axis=1) - 1
    first_peer = jax.random.randint(peer_key, (HOLDERS, 1), 0, PEERS)
    first_lane = first_peer * CAP
    shuffles = jax.vmap(lambda subkey: jax.random.permutation(subkey, LANES - CAP))(jax.random.split(order_key, HOLDERS))
    other_lanes = jnp.take_along_axis(shuffles, jnp.clip(edge_rank - CAP, 0, LANES - CAP - 1), axis=1)
    other_lanes = jnp.where(other_lanes >= first_lane, other_lanes + CAP, other_lanes)
    lane_of_edge = jnp.where(edge_rank < CAP, first_lane + edge_rank, other_lanes)
    lane_of_edge = jnp.where(per_holder, lane_of_edge, LANES).astype(jnp.int32)
    edge_ids = jnp.broadcast_to(jnp.arange(AUX_DEV * DEPTH, dtype=jnp.int32)[None, :], (HOLDERS, AUX_DEV * DEPTH))
    holder_ids = jnp.broadcast_to(jnp.arange(HOLDERS, dtype=jnp.int32)[:, None], (HOLDERS, AUX_DEV * DEPTH))
    table = jnp.full((HOLDERS, LANES), -1, jnp.int32).at[holder_ids, lane_of_edge].set(edge_ids, mode='drop')
    return (quanta, table)


def draw_quanta(key, part):
    return edge_tables(key)[0]


def draw_send_list(key, part):
    return edge_tables(key)[1]


def plant(drawn, own_key, smallest, largest):
    spot = [jax.random.randint(jax.random.fold_in(own_key, axis), (), 0, length) for axis, length in enumerate(drawn.shape)]
    main_axis = drawn.shape.index(max(drawn.shape))
    neighbour = spot[:main_axis] + [(spot[main_axis] + 1) % drawn.shape[main_axis]] + spot[main_axis + 1:]
    return drawn.at[tuple(spot)].set(smallest).at[tuple(neighbour)].set(largest)


def block_levels(rng, dims, cuts, smallest, largest):
    factor_of, own = 1.0, jax.random.fold_in(rng, 6)
    for axis_at, blocks in cuts:
        steps = jnp.exp(jax.random.uniform(jax.random.fold_in(own, axis_at), (blocks,), jnp.float32, smallest / len(cuts), largest / len(cuts)))
        factor_of = factor_of * jnp.repeat(steps, dims[axis_at] // blocks).reshape([-1 if axis == axis_at else 1 for axis in range(len(dims))])
    return factor_of


def noise(key, extent, width, reach, cuts=(), kind=jnp.bfloat16):
    values = width * jax.random.normal(key, extent, jnp.float32)
    if cuts:
        values = values * block_levels(key, extent, cuts, -0.22, 0.18)
    return jnp.clip(values, -reach, reach).astype(kind)


def setup_inputs(seed: int = 0) -> dict:
    arg_keys = jax.random.split(jax.random.key(seed), 10)
    section_state = noise(arg_keys[0], (AUX, 2 * SITES * SITES), 1.0, 6.0, ((0, 32),), jnp.float32)
    coupling = noise(arg_keys[1], (SITES, SITES), SITES ** -0.5, 0.625, (), jnp.float32)
    site_energy = jnp.clip(jax.random.uniform(arg_keys[2], (SITES,), jnp.float32, -1.0, 1.0), -1.0, 1.0)
    bath_rate = jnp.clip(jnp.exp(jax.random.uniform(arg_keys[3], (SITES,), jnp.float32, math.log(0.3), math.log(3.0))), 0.3, 3.0)
    bath_strength = jnp.clip(jnp.exp(jax.random.uniform(arg_keys[4], (SITES,), jnp.float32, math.log(0.1), math.log(1.0))), 0.1, 1.0)
    bath_of_site = jax.random.permutation(arg_keys[5], SITES).astype(jnp.int32)
    quanta = draw_quanta(jax.random.fold_in(arg_keys[9], 71), 0)
    send_list = draw_send_list(jax.random.fold_in(arg_keys[9], 71), 0)
    dest_slot = plant(jax.random.randint(arg_keys[8], (HOLDERS, LANES), 0, AUX_DEV), jax.random.fold_in(arg_keys[8], 1), 0, AUX_DEV - 1).astype(jnp.int32)
    return dict(section_state=section_state, coupling=coupling, site_energy=site_energy, bath_rate=bath_rate, bath_strength=bath_strength, bath_of_site=bath_of_site, quanta=quanta, send_list=send_list, dest_slot=dest_slot)


thermal = 0.5
highest = lax.Precision.HIGHEST


def local_block(hamilton, paired, holder_block, damp_block):
    site_count = hamilton.shape[0]
    left_product = jnp.einsum("ij,ajc->aic", hamilton, holder_block, precision=highest)
    right_product = jnp.dot(holder_block.reshape(-1, 2 * site_count), paired, precision=highest).reshape(holder_block.shape)
    commutator = left_product - right_product
    coherent = jnp.concatenate([commutator[..., site_count:], -commutator[..., :site_count]], axis=-1)
    return coherent - damp_block[:, None, None] * holder_block


def slice_pairs(states, holders, columns):
    site_count = states.shape[1]
    positions = jnp.arange(site_count).astype(jnp.int32)
    row_part = states[holders, columns, :]
    column_real = states[holders[:, None], positions[None, :], columns[:, None]]
    column_imag = states[holders[:, None], positions[None, :], columns[:, None] + site_count]
    return row_part, column_real, column_imag


def reference(section_state, coupling, site_energy, bath_rate, bath_strength, bath_of_site, quanta, send_list, dest_slot):
    float_type = section_state.dtype
    flat_shape = section_state.shape
    section_state = section_state.reshape(AUX, SITES, 2 * SITES)
    positions = jnp.arange(SITES).astype(jnp.int32)
    hamilton = (coupling + coupling.T) * 0.5 + jnp.diag(site_energy)
    zero_block = jnp.zeros_like(hamilton)
    paired = jnp.concatenate([jnp.concatenate([hamilton, zero_block], 1), jnp.concatenate([zero_block, hamilton], 1)], 0)
    chooser = (bath_of_site[:, None] == positions[None, :]).astype(float_type)
    site_rate = jnp.dot(chooser, bath_rate, precision=highest)
    site_strength = jnp.dot(chooser, bath_strength, precision=highest)
    real_coef = 2.0 * thermal * site_strength
    imag_coef = site_strength * site_rate
    matches = (quanta[:, :, None] == positions[None, None, :]).astype(float_type)
    multiple = jnp.sum(matches, axis=1)
    damping = jnp.dot(multiple, site_rate, precision=highest)
    blocks = section_state.reshape(HOLDERS, AUX_DEV, SITES, 2 * SITES)
    damp_blocks = damping.reshape(HOLDERS, AUX_DEV)
    derivative = lax.map(lambda pieces: local_block(hamilton, paired, pieces[0], pieces[1]), (blocks, damp_blocks)).reshape(section_state.shape)

    holder_ids = jnp.arange(HOLDERS).astype(jnp.int32)[:, None]
    lane_ids = jnp.arange(LANES).astype(jnp.int32)[None, :]
    band_ids = holder_ids // PEERS
    lane_group = lane_ids // (PEERS * CAP)
    target_peer = (lane_ids // CAP) % PEERS
    clipped = jnp.maximum(send_list, 0)
    sources = holder_ids * AUX_DEV + clipped // DEPTH
    lane_sites = quanta[sources, clipped % DEPTH]
    target_band = band_ids - lane_group
    usable = (send_list >= 0) & (lane_sites >= 0) & (target_band >= 0)
    targets = (jnp.maximum(target_band, 0) * PEERS + target_peer) * AUX_DEV + dest_slot
    sources = sources.reshape(-1).astype(jnp.int32)
    targets = targets.reshape(-1).astype(jnp.int32)
    columns = jnp.maximum(lane_sites, 0).reshape(-1).astype(jnp.int32)
    mask = usable.reshape(-1).astype(float_type)[:, None]

    upper_row, upper_creal, upper_cimag = slice_pairs(section_state, sources, columns)
    lower_row, lower_creal, lower_cimag = slice_pairs(section_state, targets, columns)

    up_row = jnp.concatenate([upper_row[:, SITES:], -upper_row[:, :SITES]], axis=-1)
    derivative = derivative.at[targets, columns, :].add(mask * up_row)
    derivative = derivative.at[targets[:, None], positions[None, :], columns[:, None]].add(mask * (-upper_cimag))
    derivative = derivative.at[targets[:, None], positions[None, :], columns[:, None] + SITES].add(mask * upper_creal)

    weights = multiple[sources, columns]
    shared = (-weights * imag_coef[columns])[:, None]
    row_turn = (-weights * real_coef[columns])[:, None]
    column_turn = (weights * real_coef[columns])[:, None]
    lower_rreal = lower_row[:, :SITES]
    lower_rimag = lower_row[:, SITES:]
    down_row = jnp.concatenate([shared * lower_rreal - row_turn * lower_rimag, shared * lower_rimag + row_turn * lower_rreal], axis=-1)
    down_creal = shared * lower_creal - column_turn * lower_cimag
    down_cimag = shared * lower_cimag + column_turn * lower_creal
    derivative = derivative.at[sources, columns, :].add(mask * down_row)
    derivative = derivative.at[sources[:, None], positions[None, :], columns[:, None]].add(mask * down_creal)
    derivative = derivative.at[sources[:, None], positions[None, :], columns[:, None] + SITES].add(mask * down_cimag)
    return derivative.reshape(flat_shape)
```

```python
import functools

import jax
import jax.numpy as jnp
from jax import lax
from jax.experimental import pallas as pl
from jax.experimental.pallas import tpu as pltpu
from jax.sharding import PartitionSpec as P

thermal = 0.5
LANES = 128
SUB = 8
FIELDS = 4
VMEM = pltpu.VMEM
SMEM = pltpu.SMEM


def spec(space):
    return pl.BlockSpec(memory_space=space)


def lane_index(shape):
    return lax.broadcasted_iota(jnp.int32, shape, 1)


def pack_kernel(
    sizes, band_ref, send_ref, quanta_ref, slot_ref, state_ref, store_ref, payload_ref
):
    sites, aux, depth, peers, capacity, tiers = sizes
    tiles = 4 * sites // LANES
    pair_blocks = sites // (2 * SUB)
    rows = aux * sites
    lane = lane_index((SUB, LANES))
    store_ref[:, pl.ds(rows, LANES - sites), :] = jnp.zeros((4, LANES - sites, LANES), jnp.float32)
    for a in range(aux):
        for block in range(pair_blocks):
            parts = [
                state_ref[pl.ds(a + aux * (tiles * SUB * block + u), SUB, stride=aux * tiles), :]
                for u in range(tiles)
            ]
            first, middle, last = parts
            even_imag = jnp.where(lane < 32, pltpu.roll(first, 32, 1), pltpu.roll(middle, 32, 1))
            odd_real = jnp.where(lane < 64, pltpu.roll(middle, 64, 1), pltpu.roll(last, 64, 1))
            odd_imag = pltpu.roll(last, 96, 1)
            base = a * sites + 2 * SUB * block
            store_ref[0, pl.ds(base, SUB, stride=2), :] = first
            store_ref[1, pl.ds(base, SUB, stride=2), :] = even_imag
            store_ref[0, pl.ds(base + 1, SUB, stride=2), :] = odd_real
            store_ref[1, pl.ds(base + 1, SUB, stride=2), :] = odd_imag
    for a in range(aux):
        for c in range(2):
            block = store_ref[c, pl.ds(a * sites, LANES), :]
            store_ref[2 + c, pl.ds(a * sites, sites), :] = block.T[:sites, :]
    band = band_ref[0]
    row_lane = lane_index((1, LANES))
    for g in (1, 0):
        target = jnp.maximum(band - g, 0)
        for q in range(peers):
            at_row = target * peers + q
            tags = []
            for j in range(capacity):
                l = (g * peers + q) * capacity + j
                entry = send_ref[0, l]
                clipped = jnp.maximum(entry, 0)
                source = clipped // depth
                site = quanta_ref[source, clipped % depth]
                usable = (entry >= 0) & (site >= 0) & (band - g >= 0)
                row = source * sites + jnp.maximum(site, 0)
                tags.append(slot_ref[0, l].astype(jnp.float32))
                tags.append(jnp.where(usable, site, -1).astype(jnp.float32))
                for f in range(FIELDS):
                    if f == 0 and j == 0:
                        head = store_ref[0, pl.ds(row, 1), :]
                        continue
                    at = (j * FIELDS + f) * LANES
                    payload_ref[at_row, :, pl.ds(at, LANES)] = store_ref[f, pl.ds(row, 1), :]
            for t, tag in enumerate(tags):
                head = jnp.where(row_lane == sites + t, tag, head)
            payload_ref[at_row, :, pl.ds(0, LANES)] = head


def read_tags(arrived_ref, tag_ref, sem):
    copy = pltpu.make_async_copy(arrived_ref.at[:, :, pl.ds(0, LANES)], tag_ref, sem)
    copy.start()
    copy.wait()


def answer_kernel(sizes, band_ref, arrived_ref, store_ref, reply_ref, tag_ref, sem):
    sites, aux, depth, peers, capacity, tiers = sizes
    band = band_ref[0]
    read_tags(arrived_ref, tag_ref, sem)
    for g in (1, 0):
        origin = jnp.minimum(band + g, tiers - 1)
        for p in range(peers):
            at_row = origin * peers + p
            for j in range(capacity):
                slot = tag_ref[at_row, 0, sites + 2 * j].astype(jnp.int32)
                site = tag_ref[at_row, 0, sites + 2 * j + 1].astype(jnp.int32)
                row = slot * sites + jnp.maximum(site, 0)
                for f in range(FIELDS):
                    at = (j * FIELDS + f) * LANES
                    reply_ref[at_row, :, pl.ds(at, LANES)] = store_ref[f, pl.ds(row, 1), :]


def split(value):
    high = value.astype(jnp.bfloat16)
    low = (value - high.astype(jnp.float32)).astype(jnp.bfloat16)
    return high, low


def local_kernel(
    sizes, quanta_ref, bath_ref, rate_ref, store_ref, coupling_ref, energy_ref, acc_ref, matrix_ref
):
    sites, aux, depth, peers, capacity, tiers = sizes
    row_ids = lax.broadcasted_iota(jnp.int32, (sites, sites), 0)
    col_ids = lax.broadcasted_iota(jnp.int32, (sites, sites), 1)
    coupling = coupling_ref[...]
    hamilton = (coupling + coupling.T) * 0.5 + jnp.where(row_ids == col_ids, energy_ref[...], 0.0)
    matrix_ref[...] = jnp.zeros_like(matrix_ref)
    matrix_ref[pl.ds(0, sites), pl.ds(LANES, sites)] = hamilton
    matrix_ref[pl.ds(LANES, sites), pl.ds(0, sites)] = -hamilton
    high, low = split(matrix_ref[...])
    dot = functools.partial(jnp.dot, preferred_element_type=jnp.float32)
    for a in range(aux):
        damp = jnp.float32(0.0)
        for place in range(depth):
            site = quanta_ref[a, place]
            rate = rate_ref[0, bath_ref[0, jnp.maximum(site, 0)]]
            damp = damp + jnp.where(site >= 0, rate, 0.0)
        here = pl.ds(a * sites, sites)
        for half in range(2):
            real, imag = store_ref[2 * half, here, :], store_ref[2 * half + 1, here, :]
            both = jnp.concatenate([real, imag], axis=1)
            both_high, both_low = split(both)
            product = dot(both_high, high) + (dot(both_low, high) + dot(both_high, low))
            if half == 0:
                product = product - damp * both
            else:
                product = -product
            acc_ref[2 * half, here, :] = product[:, :LANES]
            acc_ref[2 * half + 1, here, :] = product[:, LANES:]
    tail = pl.ds(aux * sites, LANES - sites)
    acc_ref[:, tail, :] = jnp.zeros((4, LANES - sites, LANES), jnp.float32)


def raise_kernel(sizes, band_ref, arrived_ref, acc_ref, sum_ref, work_ref, tag_ref, sem):
    sites, aux, depth, peers, capacity, tiers = sizes
    rows = aux * sites
    band = band_ref[0]
    read_tags(arrived_ref, tag_ref, sem)
    work_ref[...] = acc_ref[...]
    for g in range(2):
        origin = jnp.minimum(band + g, tiers - 1)
        inside = band + g < tiers
        for p in range(peers):
            at_row = origin * peers + p
            for j in range(capacity):
                slot = tag_ref[at_row, 0, sites + 2 * j].astype(jnp.int32)
                site = tag_ref[at_row, 0, sites + 2 * j + 1].astype(jnp.int32)
                usable = (site >= 0) & inside
                row = pl.ds(jnp.where(usable, slot * sites + jnp.maximum(site, 0), rows), 1)
                at = j * FIELDS * LANES
                parts = [
                    arrived_ref[at_row, :, pl.ds(at + f * LANES, LANES)]
                    for f in range(FIELDS)
                ]
                work_ref[0, row, :] = work_ref[0, row, :] + parts[1]
                work_ref[1, row, :] = work_ref[1, row, :] - parts[0]
                work_ref[2, row, :] = work_ref[2, row, :] - parts[3]
                work_ref[3, row, :] = work_ref[3, row, :] + parts[2]
    for a in range(aux):
        here = pl.ds(a * sites, sites)
        for c in range(2):
            turned = work_ref[2 + c, pl.ds(a * sites, LANES), :].T[:sites, :]
            sum_ref[c, here, :] = work_ref[c, here, :] + turned
    tail = pl.ds(rows, LANES - sites)
    sum_ref[:, tail, :] = jnp.zeros((2, LANES - sites, LANES), jnp.float32)


def lower_kernel(
    sizes,
    band_ref,
    send_ref,
    quanta_ref,
    bath_ref,
    rate_ref,
    strength_ref,
    returned_ref,
    sum_ref,
    out_ref,
    work_ref,
):
    sites, aux, depth, peers, capacity, tiers = sizes
    rows = aux * sites
    tiles = 4 * sites // LANES
    pair_blocks = sites // (2 * SUB)
    band = band_ref[0]
    work_ref[pl.ds(0, 2)] = sum_ref[...]
    work_ref[pl.ds(2, 2)] = jnp.zeros((2,) + work_ref.shape[1:], jnp.float32)
    for g in range(2):
        target = jnp.maximum(band - g, 0)
        for q in range(peers):
            at_row = target * peers + q
            for j in range(capacity):
                l = (g * peers + q) * capacity + j
                entry = send_ref[0, l]
                clipped = jnp.maximum(entry, 0)
                source = clipped // depth
                site = quanta_ref[source, clipped % depth]
                usable = (entry >= 0) & (site >= 0) & (band - g >= 0)
                safe = jnp.maximum(site, 0)
                weight = jnp.float32(0.0)
                for place in range(depth):
                    weight = weight + jnp.where(quanta_ref[source, place] == safe, 1.0, 0.0)
                bath = bath_ref[0, safe]
                strength = strength_ref[0, bath]
                turn = weight * (2.0 * thermal * strength)
                shared = -weight * (strength * rate_ref[0, bath])
                row = pl.ds(jnp.where(usable, source * sites + safe, rows), 1)
                at = j * FIELDS * LANES
                row_real, row_imag, col_real, col_imag = (
                    returned_ref[at_row, :, pl.ds(at + f * LANES, LANES)]
                    for f in range(FIELDS)
                )
                work_ref[0, row, :] = work_ref[0, row, :] + (shared * row_real + turn * row_imag)
                work_ref[1, row, :] = work_ref[1, row, :] + (shared * row_imag - turn * row_real)
                work_ref[2, row, :] = work_ref[2, row, :] + (shared * col_real - turn * col_imag)
                work_ref[3, row, :] = work_ref[3, row, :] + (shared * col_imag + turn * col_real)
    for a in range(aux):
        here = pl.ds(a * sites, sites)
        for c in range(2):
            turned = work_ref[2 + c, pl.ds(a * sites, LANES), :].T[:sites, :]
            work_ref[c, here, :] = work_ref[c, here, :] + turned
    lane = lane_index((SUB, LANES))
    for a in range(aux):
        for block in range(pair_blocks):
            base = a * sites + 2 * SUB * block
            even_real, even_imag, odd_real, odd_imag = (
                work_ref[c, pl.ds(base + o, SUB, stride=2), :] for o in (0, 1) for c in (0, 1)
            )
            turned_imag = pltpu.roll(even_imag, 96, 1)
            turned_real = pltpu.roll(odd_real, 64, 1)
            parts = (
                jnp.where(lane < 96, even_real, turned_imag),
                jnp.where(lane < 64, turned_imag, turned_real),
                jnp.where(lane < 32, turned_real, pltpu.roll(odd_imag, 32, 1)),
            )
            for u in range(tiles):
                start = a + aux * (tiles * SUB * block + u)
                out_ref[pl.ds(start, SUB, stride=aux * tiles), :] = parts[u]


def on_device(
    section_state,
    coupling,
    site_energy,
    bath_rate,
    bath_strength,
    bath_of_site,
    quanta,
    send_list,
    dest_slot,
):
    sites = coupling.shape[0]
    aux, flat = section_state.shape
    depth = quanta.shape[1]
    lane_count = send_list.shape[1]
    peers = lax.axis_size("aux")
    tiers = lax.axis_size("tier")
    capacity = lane_count // (2 * peers)
    sizes = (sites, aux, depth, peers, capacity, tiers)
    rows = aux * sites
    padded = rows + LANES - sites
    width = capacity * FIELDS * LANES
    chunks = flat // LANES
    f32 = jnp.float32
    band = lax.axis_index("tier").reshape(1)
    tiled = section_state.reshape(aux, chunks, LANES).transpose(1, 0, 2).reshape(-1, LANES)
    bath_row = bath_of_site.reshape(1, -1)
    rate_row = bath_rate.reshape(1, -1)
    strength_row = bath_strength.reshape(1, -1)

    def call(kernel, in_spaces, outs, scratch, name):
        many = isinstance(outs, list)
        return pl.pallas_call(
            functools.partial(kernel, sizes),
            out_shape=outs,
            in_specs=[spec(space) for space in in_spaces],
            out_specs=[spec(VMEM)] * len(outs) if many else spec(VMEM),
            scratch_shapes=scratch,
            name=name,
            compiler_params=pltpu.CompilerParams(vmem_limit_bytes=24 * 1024 * 1024),
        )

    store_shape = jax.ShapeDtypeStruct((4, padded, LANES), f32)
    wire_shape = jax.ShapeDtypeStruct((tiers * peers, 1, width), f32)
    tag_scratch = [SMEM((tiers * peers, 1, LANES), f32), pltpu.SemaphoreType.DMA(())]
    trade = functools.partial(
        lax.all_to_all, axis_name=("tier", "aux"), split_axis=0, concat_axis=0, tiled=True
    )
    store, payload = call(
        pack_kernel, [SMEM] * 4 + [VMEM], [store_shape, wire_shape], [], "pack"
    )(band, send_list, quanta, dest_slot, tiled)
    arrived = trade(payload)
    acc = call(
        local_kernel,
        [SMEM] * 3 + [VMEM] * 3,
        store_shape,
        [VMEM((2 * LANES, 2 * LANES), f32)],
        "local",
    )(quanta, bath_row, rate_row, store, coupling, site_energy.reshape(1, -1))
    reply = call(answer_kernel, [SMEM, VMEM, VMEM], wire_shape, tag_scratch, "answer")(
        band, arrived, store
    )
    returned = trade(reply)
    total = call(
        raise_kernel,
        [SMEM, VMEM, VMEM],
        jax.ShapeDtypeStruct((2, padded, LANES), f32),
        [VMEM(store_shape.shape, f32)] + tag_scratch,
        "raise",
    )(band, arrived, acc)
    out = call(
        lower_kernel,
        [SMEM] * 6 + [VMEM] * 2,
        jax.ShapeDtypeStruct((aux * chunks, LANES), f32),
        [VMEM(store_shape.shape, f32)],
        "lower",
    )(band, send_list, quanta, bath_row, rate_row, strength_row, returned, total)
    return out.reshape(chunks, aux, LANES).transpose(1, 0, 2).reshape(aux, flat)


def solution(mesh):
    return jax.shard_map(
        on_device,
        mesh=mesh,
        in_specs=(
            P(("tier", "aux"), None),
            P(),
            P(),
            P(),
            P(),
            P(),
            P(("tier", "aux"), None),
            P(("tier", "aux"), None),
            P(("tier", "aux"), None),
        ),
        out_specs=P(("tier", "aux"), None),
        check_vma=False,
    )
```

```python
import functools

import jax
import jax.numpy as jnp
from jax import lax
from jax.experimental import pallas as pl
from jax.experimental.pallas import tpu as pltpu
from jax.sharding import PartitionSpec as P

thermal = 0.5
LANES = 128
SUB = 8
FIELDS = 3
VMEM = pltpu.VMEM
SMEM = pltpu.SMEM


def spec(space):
    return pl.BlockSpec(memory_space=space)


def lane_index(shape):
    return lax.broadcasted_iota(jnp.int32, shape, 1)


def merge(parts, lane, sites):
    spare = LANES - sites
    turned = [pltpu.roll(parts[FIELDS], sites - f * spare, 1) for f in range(FIELDS)]
    return [jnp.where(lane < sites, parts[f], turned[f]) for f in range(FIELDS)]


def unmerge(parts, lane, sites):
    spare = LANES - sites
    last = pltpu.roll(parts[FIELDS - 1], FIELDS * spare, 1)
    for f in reversed(range(FIELDS - 1)):
        last = jnp.where(lane < (f + 1) * spare, pltpu.roll(parts[f], (f + 1) * spare, 1), last)
    return list(parts) + [last]


def pack_kernel(
    sizes,
    band_ref,
    send_hbm,
    quanta_hbm,
    slot_hbm,
    state_hbm,
    store_ref,
    payload_ref,
    state_ref,
    send_ref,
    quanta_ref,
    slot_ref,
    sems,
    table_sems,
):
    sites, aux, depth, peers, capacity, tiers = sizes
    tiles = 4 * sites // LANES
    pair_blocks = sites // (2 * SUB)
    chunk = aux * tiles * SUB
    rows = aux * sites
    copies = [
        pltpu.make_async_copy(
            state_hbm.at[pl.ds(b * chunk, chunk), :],
            state_ref.at[pl.ds(b * chunk, chunk), :],
            sems.at[b],
        )
        for b in range(pair_blocks)
    ]
    tables = [
        pltpu.make_async_copy(source, target, table_sems.at[t])
        for t, (source, target) in enumerate(
            ((send_hbm, send_ref), (quanta_hbm, quanta_ref), (slot_hbm, slot_ref))
        )
    ]
    for copy in copies + tables:
        copy.start()
    lane = lane_index((SUB, LANES))
    store_ref[:, pl.ds(rows, LANES - sites), :] = jnp.zeros((4, LANES - sites, LANES), jnp.float32)
    for block in range(pair_blocks):
        copies[block].wait()
        for a in range(aux):
            first, middle, last = (
                state_ref[pl.ds(a + aux * (tiles * SUB * block + u), SUB, stride=aux * tiles), :]
                for u in range(tiles)
            )
            even_imag = jnp.where(lane < 32, pltpu.roll(first, 32, 1), pltpu.roll(middle, 32, 1))
            odd_real = jnp.where(lane < 64, pltpu.roll(middle, 64, 1), pltpu.roll(last, 64, 1))
            odd_imag = pltpu.roll(last, 96, 1)
            base = a * sites + 2 * SUB * block
            store_ref[0, pl.ds(base, SUB, stride=2), :] = first
            store_ref[1, pl.ds(base, SUB, stride=2), :] = even_imag
            store_ref[0, pl.ds(base + 1, SUB, stride=2), :] = odd_real
            store_ref[1, pl.ds(base + 1, SUB, stride=2), :] = odd_imag
    for a in range(aux):
        for c in range(2):
            block = store_ref[c, pl.ds(a * sites, LANES), :]
            store_ref[2 + c, pl.ds(a * sites, sites), :] = block.T[:sites, :]
    for table in tables:
        table.wait()
    band = band_ref[0]
    row_lane = lane_index((1, LANES))
    for g in (1, 0):
        target = jnp.maximum(band - g, 0)
        inside = band - g >= 0
        for q in range(peers):
            at_row = target * peers + q
            tags = jnp.zeros((1, LANES), jnp.int32)
            for j in range(capacity):
                l = (g * peers + q) * capacity + j
                entry = send_ref[0, l]
                clipped = jnp.maximum(entry, 0)
                source = clipped // depth
                site = quanta_ref[clipped % depth, source]
                usable = (entry >= 0) & (site >= 0) & inside
                site = jnp.maximum(site, 0)
                row = pl.ds(source * sites + site, 1)
                tags = jnp.where(
                    row_lane == 2 * j, jnp.where(usable, slot_ref[0, l] * sites, rows), tags
                )
                tags = jnp.where(row_lane == 2 * j + 1, jnp.where(usable, site, 0), tags)
                fields = merge([store_ref[f, row, :] for f in range(4)], row_lane, sites)
                for f in range(FIELDS):
                    payload_ref[at_row, :, pl.ds((j * FIELDS + f) * LANES, LANES)] = fields[f]
            payload_ref[at_row, :, pl.ds(capacity * FIELDS * LANES, LANES)] = tags.astype(
                jnp.float32
            )


def read_tags(sizes, band, arrived_ref, tag_ref, sems):
    sites, aux, depth, peers, capacity, tiers = sizes
    copies = [
        pltpu.make_async_copy(
            arrived_ref.at[
                pl.ds(jnp.minimum(band + g, tiers - 1) * peers, peers),
                :,
                pl.ds(capacity * FIELDS * LANES, LANES),
            ],
            tag_ref.at[pl.ds(g * peers, peers)],
            sems.at[g],
        )
        for g in range(2)
    ]
    for copy in copies:
        copy.start()
    return copies


def tag_row(tag_ref, g, p, j, peers):
    at = g * peers + p
    return tag_ref[at, 0, 2 * j].astype(jnp.int32) + tag_ref[at, 0, 2 * j + 1].astype(jnp.int32)


def answer_kernel(sizes, band_ref, arrived_ref, store_ref, reply_ref, tag_ref, sems):
    sites, aux, depth, peers, capacity, tiers = sizes
    band = band_ref[0]
    for copy in read_tags(sizes, band, arrived_ref, tag_ref, sems):
        copy.wait()
    for g in (1, 0):
        origin = jnp.minimum(band + g, tiers - 1)
        for p in range(peers):
            at_row = origin * peers + p
            for j in range(capacity):
                row = pl.ds(tag_row(tag_ref, g, p, j, peers), 1)
                for f in range(FIELDS):
                    reply_ref[at_row, :, pl.ds((j * FIELDS + f) * LANES, LANES)] = store_ref[
                        f, row, :
                    ]


def split(value):
    high = value.astype(jnp.bfloat16)
    low = (value - high.astype(jnp.float32)).astype(jnp.bfloat16)
    return high, low


def local_kernel(
    sizes,
    quanta_ref,
    bath_ref,
    rate_ref,
    store_ref,
    coupling_ref,
    energy_ref,
    acc_ref,
    merged_ref,
    matrix_ref,
):
    sites, aux, depth, peers, capacity, tiers = sizes
    row_ids = lax.broadcasted_iota(jnp.int32, (sites, sites), 0)
    col_ids = lax.broadcasted_iota(jnp.int32, (sites, sites), 1)
    coupling = coupling_ref[...]
    hamilton = (coupling + coupling.T) * 0.5 + jnp.where(row_ids == col_ids, energy_ref[...], 0.0)
    matrix_ref[...] = jnp.zeros_like(matrix_ref)
    matrix_ref[pl.ds(0, sites), pl.ds(LANES, sites)] = hamilton
    matrix_ref[pl.ds(LANES, sites), pl.ds(0, sites)] = -hamilton
    high, low = split(matrix_ref[...])
    dot = functools.partial(jnp.dot, preferred_element_type=jnp.float32)
    for a in range(aux):
        damp = jnp.float32(0.0)
        for place in range(depth):
            site = quanta_ref[place, a]
            rate = rate_ref[0, bath_ref[0, jnp.maximum(site, 0)]]
            damp = damp + jnp.where(site >= 0, rate, 0.0)
        here = pl.ds(a * sites, sites)
        for half in range(2):
            real, imag = store_ref[2 * half, here, :], store_ref[2 * half + 1, here, :]
            both = jnp.concatenate([real, imag], axis=1)
            both_high, both_low = split(both)
            product = dot(both_high, high) + (dot(both_low, high) + dot(both_high, low))
            if half == 0:
                product = product - damp * both
            else:
                product = -product
            acc_ref[2 * half, here, :] = product[:, :LANES]
            acc_ref[2 * half + 1, here, :] = product[:, LANES:]
        fields = merge([store_ref[f, here, :] for f in range(4)], lane_index((sites, LANES)), sites)
        for f in range(FIELDS):
            merged_ref[f, here, :] = fields[f]
    tail = pl.ds(aux * sites, LANES - sites)
    acc_ref[:, tail, :] = jnp.zeros((4, LANES - sites, LANES), jnp.float32)
    merged_ref[:, tail, :] = jnp.zeros((FIELDS, LANES - sites, LANES), jnp.float32)


def raise_kernel(
    sizes,
    band_ref,
    send_ref,
    quanta_ref,
    bath_ref,
    rate_ref,
    strength_ref,
    arrived_ref,
    acc_ref,
    sum_ref,
    column_ref,
    place_ref,
    coef_ref,
    work_ref,
    column_work,
    place_work,
    tag_ref,
    sems,
):
    sites, aux, depth, peers, capacity, tiers = sizes
    rows = aux * sites
    band = band_ref[0]
    copies = read_tags(sizes, band, arrived_ref, tag_ref, sems)
    row_lane = lane_index((1, LANES))
    work_ref[...] = acc_ref[...]
    column_work[...] = jnp.zeros_like(column_work)
    place_work[...] = jnp.zeros_like(place_work)
    half = column_work.shape[0] // 2
    for g in range(2):
        inside = band - g >= 0
        for q in range(peers):
            for j in range(capacity):
                l = (g * peers + q) * capacity + j
                at = (g * capacity + j) * peers + q
                entry = send_ref[0, l]
                clipped = jnp.maximum(entry, 0)
                source = clipped // depth
                site = quanta_ref[clipped % depth, source]
                usable = (entry >= 0) & (site >= 0) & inside
                safe = jnp.maximum(site, 0)
                weight = jnp.float32(0.0)
                for place in range(depth):
                    weight = weight + jnp.where(quanta_ref[place, source] == safe, 1.0, 0.0)
                weight = jnp.where(usable, weight, 0.0)
                bath = bath_ref[0, safe]
                strength = strength_ref[0, bath]
                turn = weight * (2.0 * thermal * strength)
                shared = -weight * (strength * rate_ref[0, bath])
                coef_ref[0, pl.ds(at, 1), :] = jnp.full((1, LANES), shared)
                coef_ref[1, pl.ds(at, 1), :] = jnp.full((1, LANES), turn)
                row = pl.ds(jnp.where(usable, source * sites + safe, rows), 1)
                for spot in (at, half + at):
                    slab = spot // LANES
                    place_work[slab, row, :] = jnp.where(
                        row_lane == spot % LANES, 1.0, place_work[slab, row, :]
                    )
                hot = (row_lane == safe).astype(jnp.float32)
                block = jnp.where(usable, source, aux)
                column_work[at, pl.ds(block, 1), :] = hot
                column_work[half + at, pl.ds(block, 1), :] = hot
    for slab in range(place_work.shape[0]):
        place_ref[:, pl.ds(slab * LANES, LANES)] = place_work[slab, pl.ds(0, rows), :].astype(
            jnp.bfloat16
        )
    for a in range(aux):
        column_ref[:, pl.ds(a * LANES, LANES)] = column_work[:, a, :].astype(jnp.bfloat16)
    for copy in copies:
        copy.wait()
    for g in range(2):
        origin = jnp.minimum(band + g, tiers - 1)
        inside = band + g < tiers
        for p in range(peers):
            at_row = origin * peers + p
            for j in range(capacity):
                row = pl.ds(jnp.where(inside, tag_row(tag_ref, g, p, j, peers), rows), 1)
                parts = unmerge(
                    [
                        arrived_ref[at_row, :, pl.ds((j * FIELDS + f) * LANES, LANES)]
                        for f in range(FIELDS)
                    ],
                    row_lane,
                    sites,
                )
                work_ref[0, row, :] = work_ref[0, row, :] + parts[1]
                work_ref[1, row, :] = work_ref[1, row, :] - parts[0]
                work_ref[2, row, :] = work_ref[2, row, :] - parts[3]
                work_ref[3, row, :] = work_ref[3, row, :] + parts[2]
    for a in range(aux):
        here = pl.ds(a * sites, sites)
        for c in range(2):
            turned = work_ref[2 + c, pl.ds(a * sites, LANES), :].T[:sites, :]
            sum_ref[c, here, :] = work_ref[c, here, :] + turned


def lower_kernel(
    sizes,
    band_ref,
    returned_ref,
    sum_ref,
    column_ref,
    place_ref,
    coef_ref,
    out_hbm,
    work_ref,
    edge_ref,
    out_ref,
    sems,
):
    sites, aux, depth, peers, capacity, tiers = sizes
    tiles = 4 * sites // LANES
    pair_blocks = sites // (2 * SUB)
    chunk = aux * tiles * SUB
    slabs = capacity * FIELDS
    used = 2 * capacity * peers
    half = edge_ref.shape[1] // 2
    band = band_ref[0]
    lane = lane_index((peers, LANES))
    if used < half:
        for top in (used, half + used):
            edge_ref[:, pl.ds(top, half - used), :] = jnp.zeros(
                (4, half - used, LANES), jnp.float32
            )
    for g in range(2):
        target = jnp.maximum(band - g, 0)
        for j in range(capacity):
            start = target * (peers * slabs) + j * FIELDS
            parts = [
                returned_ref[pl.ds(start + f, peers, stride=slabs), :] for f in range(FIELDS)
            ]
            row_real, row_imag, col_real, col_imag = unmerge(parts, lane, sites)
            base = (g * capacity + j) * peers
            shared = coef_ref[0, pl.ds(base, peers), :]
            turn = coef_ref[1, pl.ds(base, peers), :]
            values = (
                shared * row_real + turn * row_imag,
                shared * row_imag - turn * row_real,
                shared * col_real - turn * col_imag,
                shared * col_imag + turn * col_real,
            )
            for f, value in enumerate(values):
                high = value.astype(jnp.bfloat16).astype(jnp.float32)
                edge_ref[f, pl.ds(base, peers), :] = high
                edge_ref[f, pl.ds(half + base, peers), :] = value - high
    dot = functools.partial(jnp.dot, preferred_element_type=jnp.float32)
    row_data = jnp.concatenate([edge_ref[0], edge_ref[1]], axis=1).astype(jnp.bfloat16)
    col_data = jnp.concatenate([edge_ref[2].T, edge_ref[3].T], axis=0).astype(jnp.bfloat16)
    for pair in range(aux // 2):
        columns = dot(col_data, column_ref[:, pl.ds(2 * pair * LANES, 2 * LANES)])
        for o in range(2):
            here = pl.ds((2 * pair + o) * sites, sites)
            placed = dot(place_ref[here, :], row_data)
            for c in range(2):
                work_ref[c, here, :] = (
                    sum_ref[c, here, :]
                    + placed[:, c * LANES : (c + 1) * LANES]
                    + columns[c * LANES : c * LANES + sites, o * LANES : (o + 1) * LANES]
                )
    lane = lane_index((SUB, LANES))
    copies = []
    for block in range(pair_blocks):
        for a in range(aux):
            base = a * sites + 2 * SUB * block
            even_real, even_imag, odd_real, odd_imag = (
                work_ref[c, pl.ds(base + o, SUB, stride=2), :] for o in (0, 1) for c in (0, 1)
            )
            turned_imag = pltpu.roll(even_imag, 96, 1)
            turned_real = pltpu.roll(odd_real, 64, 1)
            parts = (
                jnp.where(lane < 96, even_real, turned_imag),
                jnp.where(lane < 64, turned_imag, turned_real),
                jnp.where(lane < 32, turned_real, pltpu.roll(odd_imag, 32, 1)),
            )
            for u in range(tiles):
                start = a + aux * (tiles * SUB * block + u)
                out_ref[pl.ds(start, SUB, stride=aux * tiles), :] = parts[u]
        here = pl.ds(block * chunk, chunk)
        copies.append(pltpu.make_async_copy(out_ref.at[here, :], out_hbm.at[here, :], sems.at[block]))
        copies[-1].start()
    for copy in copies:
        copy.wait()


def on_device(
    section_state,
    coupling,
    site_energy,
    bath_rate,
    bath_strength,
    bath_of_site,
    quanta,
    send_list,
    dest_slot,
):
    sites = coupling.shape[0]
    aux, flat = section_state.shape
    depth = quanta.shape[1]
    lane_count = send_list.shape[1]
    peers = lax.axis_size("aux")
    tiers = lax.axis_size("tier")
    capacity = lane_count // (2 * peers)
    sizes = (sites, aux, depth, peers, capacity, tiers)
    rows = aux * sites
    padded = rows + LANES - sites
    slabs = capacity * FIELDS
    chunks = flat // LANES
    half = -(-lane_count // 64) * 64
    f32 = jnp.float32
    bf16 = jnp.bfloat16
    band = lax.axis_index("tier").reshape(1)
    tiled = section_state.reshape(aux, chunks, LANES).transpose(1, 0, 2).reshape(-1, LANES)
    turned_quanta = quanta.T
    bath_row = bath_of_site.reshape(1, -1)
    rate_row = bath_rate.reshape(1, -1)
    strength_row = bath_strength.reshape(1, -1)
    pair_blocks = sites // (2 * SUB)

    def call(kernel, name, in_spaces, outs, scratch, out_spaces=None):
        return pl.pallas_call(
            functools.partial(kernel, sizes),
            out_shape=[jax.ShapeDtypeStruct(*out) for out in outs],
            in_specs=[spec(space) for space in in_spaces],
            out_specs=[spec(space) for space in out_spaces or [VMEM] * len(outs)],
            scratch_shapes=scratch,
            name=name,
            compiler_params=pltpu.CompilerParams(vmem_limit_bytes=24 * 1024 * 1024),
        )

    dma = pltpu.SemaphoreType.DMA
    store_shape = (4, padded, LANES)
    reply_shape = (tiers * peers, 1, slabs * LANES)
    payload_shape = (tiers * peers, 1, (slabs + 1) * LANES)
    tag_scratch = [SMEM((2 * peers, 1, LANES), f32), dma((2,))]
    flat_shape = (aux * chunks, LANES)
    trade = functools.partial(
        lax.all_to_all, axis_name=("tier", "aux"), split_axis=0, concat_axis=0, tiled=True
    )
    store, payload = call(
        pack_kernel,
        "pack",
        [SMEM] + [pltpu.HBM] * 4,
        [(store_shape, f32), (payload_shape, f32)],
        [
            VMEM(flat_shape, f32),
            SMEM(send_list.shape, jnp.int32),
            SMEM(turned_quanta.shape, jnp.int32),
            SMEM(dest_slot.shape, jnp.int32),
            dma((pair_blocks,)),
            dma((3,)),
        ],
    )(band, send_list, turned_quanta, dest_slot, tiled)
    arrived = trade(payload)
    acc, merged = call(
        local_kernel,
        "local",
        [SMEM] * 3 + [VMEM] * 3,
        [(store_shape, f32), ((FIELDS, padded, LANES), f32)],
        [VMEM((2 * LANES, 2 * LANES), f32)],
    )(turned_quanta, bath_row, rate_row, store, coupling, site_energy.reshape(1, -1))
    (reply,) = call(
        answer_kernel, "answer", [SMEM, VMEM, VMEM], [(reply_shape, f32)], tag_scratch
    )(band, arrived, merged)
    returned = trade(reply)
    total, columns, places, coefs = call(
        raise_kernel,
        "raise",
        [SMEM] * 6 + [VMEM] * 2,
        [
            ((2, rows, LANES), f32),
            ((2 * half, aux * LANES), bf16),
            ((rows, 2 * half), bf16),
            ((2, lane_count, LANES), f32),
        ],
        [VMEM(store_shape, f32), VMEM((2 * half, 2 * SUB, LANES), f32), VMEM((2 * half // LANES, padded, LANES), f32)]
        + tag_scratch,
    )(band, send_list, turned_quanta, bath_row, rate_row, strength_row, arrived, acc)
    (out,) = call(
        lower_kernel,
        "lower",
        [SMEM] + [VMEM] * 5,
        [(flat_shape, f32)],
        [
            VMEM((2, rows, LANES), f32),
            VMEM((4, 2 * half, LANES), f32),
            VMEM(flat_shape, f32),
            dma((pair_blocks,)),
        ],
        [pltpu.HBM],
    )(band, returned.reshape(-1, LANES), total, columns, places, coefs)
    return out.reshape(chunks, aux, LANES).transpose(1, 0, 2).reshape(aux, flat)


def solution(mesh):
    return jax.shard_map(
        on_device,
        mesh=mesh,
        in_specs=(
            P(("tier", "aux"), None),
            P(),
            P(),
            P(),
            P(),
            P(),
            P(("tier", "aux"), None),
            P(("tier", "aux"), None),
            P(("tier", "aux"), None),
        ),
        out_specs=P(("tier", "aux"), None),
        check_vma=False,
    )
```

```python
import functools

import jax
import jax.numpy as jnp
from jax import lax
from jax.experimental import pallas as pl
from jax.experimental.pallas import tpu as pltpu
from jax.sharding import PartitionSpec as P

thermal = 0.5
LANES = 128
SUB = 8
FIELDS = 3
VMEM = pltpu.VMEM
SMEM = pltpu.SMEM


def spec(space):
    return pl.BlockSpec(memory_space=space)


def lane_index(shape):
    return lax.broadcasted_iota(jnp.int32, shape, 1)


def fetch(pairs, sems):
    copies = [
        pltpu.make_async_copy(source, target, sems.at[n]) for n, (source, target) in enumerate(pairs)
    ]
    for copy in copies:
        copy.start()
    return copies


def send_blocks(work_ref, wire_hbm, sems, band, step, tiers, peers):
    def block(g):
        at = jnp.clip(band + g * step, 0, tiers - 1) * peers
        return pltpu.make_async_copy(work_ref.at[g], wire_hbm.at[pl.ds(at, peers)], sems.at[g])

    return block


def merge(parts, lane, sites):
    spare = LANES - sites
    turned = [pltpu.roll(parts[FIELDS], sites - f * spare, 1) for f in range(FIELDS)]
    return [jnp.where(lane < sites, parts[f], turned[f]) for f in range(FIELDS)]


def unmerge(parts, lane, sites):
    spare = LANES - sites
    last = pltpu.roll(parts[FIELDS - 1], FIELDS * spare, 1)
    for f in reversed(range(FIELDS - 1)):
        last = jnp.where(lane < (f + 1) * spare, pltpu.roll(parts[f], (f + 1) * spare, 1), last)
    return list(parts) + [last]


def pack_kernel(
    sizes,
    band_ref,
    send_hbm,
    quanta_hbm,
    slot_hbm,
    state_hbm,
    store_ref,
    payload_hbm,
    state_ref,
    payload_ref,
    send_ref,
    quanta_ref,
    slot_ref,
    sems,
    table_sems,
    wire_sems,
):
    sites, aux, depth, peers, capacity, tiers = sizes
    tiles = 4 * sites // LANES
    pair_blocks = sites // (2 * SUB)
    chunk = aux * tiles * SUB
    rows = aux * sites
    copies = fetch(
        [
            (state_hbm.at[pl.ds(b * chunk, chunk), :], state_ref.at[pl.ds(b * chunk, chunk), :])
            for b in range(pair_blocks)
        ],
        sems,
    )
    tables = fetch(
        [(send_hbm, send_ref), (quanta_hbm, quanta_ref), (slot_hbm, slot_ref)], table_sems
    )
    lane = lane_index((SUB, LANES))
    store_ref[:, pl.ds(rows, LANES - sites), :] = jnp.zeros((4, LANES - sites, LANES), jnp.float32)
    for block in range(pair_blocks):
        copies[block].wait()
        for a in range(aux):
            first, middle, last = (
                state_ref[pl.ds(a + aux * (tiles * SUB * block + u), SUB, stride=aux * tiles), :]
                for u in range(tiles)
            )
            even_imag = jnp.where(lane < 32, pltpu.roll(first, 32, 1), pltpu.roll(middle, 32, 1))
            odd_real = jnp.where(lane < 64, pltpu.roll(middle, 64, 1), pltpu.roll(last, 64, 1))
            odd_imag = pltpu.roll(last, 96, 1)
            base = a * sites + 2 * SUB * block
            store_ref[0, pl.ds(base, SUB, stride=2), :] = first
            store_ref[1, pl.ds(base, SUB, stride=2), :] = even_imag
            store_ref[0, pl.ds(base + 1, SUB, stride=2), :] = odd_real
            store_ref[1, pl.ds(base + 1, SUB, stride=2), :] = odd_imag
    for a in range(aux):
        for c in range(2):
            block = store_ref[c, pl.ds(a * sites, LANES), :]
            store_ref[2 + c, pl.ds(a * sites, sites), :] = block.T[:sites, :]
    for table in tables:
        table.wait()
    band = band_ref[0]
    row_lane = lane_index((1, LANES))
    block = send_blocks(payload_ref, payload_hbm, wire_sems, band, -1, tiers, peers)
    for g in (1, 0):
        inside = band - g >= 0
        for q in range(peers):
            tags = jnp.zeros((1, LANES), jnp.int32)
            for j in range(capacity):
                l = (g * peers + q) * capacity + j
                entry = send_ref[0, l]
                clipped = jnp.maximum(entry, 0)
                source = clipped // depth
                site = quanta_ref[clipped % depth, source]
                usable = (entry >= 0) & (site >= 0) & inside
                site = jnp.maximum(site, 0)
                row = pl.ds(source * sites + site, 1)
                tags = jnp.where(
                    row_lane == 2 * j, jnp.where(usable, slot_ref[0, l] * sites, rows), tags
                )
                tags = jnp.where(row_lane == 2 * j + 1, jnp.where(usable, site, 0), tags)
                fields = merge([store_ref[f, row, :] for f in range(4)], row_lane, sites)
                for f in range(FIELDS):
                    payload_ref[g, q, :, pl.ds((j * FIELDS + f) * LANES, LANES)] = fields[f]
            payload_ref[g, q, :, pl.ds(capacity * FIELDS * LANES, LANES)] = tags.astype(jnp.float32)
        if g == 0:
            block(g).start()
        else:
            pl.when(inside)(block(g).start)
    block(0).wait()
    pl.when(band >= 1)(block(1).wait)


def read_tags(sizes, band, arrived_ref, tag_ref, sems):
    sites, aux, depth, peers, capacity, tiers = sizes
    copies = [
        pltpu.make_async_copy(
            arrived_ref.at[
                pl.ds(jnp.minimum(band + g, tiers - 1) * peers, peers),
                :,
                pl.ds(capacity * FIELDS * LANES, LANES),
            ],
            tag_ref.at[pl.ds(g * peers, peers)],
            sems.at[g],
        )
        for g in range(2)
    ]
    for copy in copies:
        copy.start()
    return copies


def tag_row(tag_ref, g, p, j, peers):
    at = g * peers + p
    return tag_ref[at, 0, 2 * j].astype(jnp.int32) + tag_ref[at, 0, 2 * j + 1].astype(jnp.int32)


def answer_kernel(
    sizes, band_ref, arrived_ref, store_ref, reply_hbm, reply_ref, tag_ref, sems, wire_sems
):
    sites, aux, depth, peers, capacity, tiers = sizes
    band = band_ref[0]
    copies = read_tags(sizes, band, arrived_ref, tag_ref, sems)
    block = send_blocks(reply_ref, reply_hbm, wire_sems, band, 1, tiers, peers)
    for copy in copies:
        copy.wait()
    for g in (1, 0):
        for p in range(peers):
            for j in range(capacity):
                row = pl.ds(tag_row(tag_ref, g, p, j, peers), 1)
                for f in range(FIELDS):
                    reply_ref[g, p, :, pl.ds((j * FIELDS + f) * LANES, LANES)] = store_ref[f, row, :]
        if g == 0:
            block(g).start()
        else:
            pl.when(band + g < tiers)(block(g).start)
    block(0).wait()
    pl.when(band + 1 < tiers)(block(1).wait)


def split(value):
    high = value.astype(jnp.bfloat16)
    low = (value - high.astype(jnp.float32)).astype(jnp.bfloat16)
    return high, low


def local_kernel(
    sizes,
    quanta_hbm,
    bath_hbm,
    rate_hbm,
    coupling_hbm,
    energy_hbm,
    store_ref,
    acc_hbm,
    merged_ref,
    acc_ref,
    matrix_ref,
    coupling_ref,
    energy_ref,
    quanta_ref,
    bath_ref,
    rate_ref,
    sems,
    acc_sems,
):
    sites, aux, depth, peers, capacity, tiers = sizes
    row_ids = lax.broadcasted_iota(jnp.int32, (sites, sites), 0)
    col_ids = lax.broadcasted_iota(jnp.int32, (sites, sites), 1)
    copies = fetch(
        [
            (coupling_hbm, coupling_ref),
            (energy_hbm, energy_ref),
            (quanta_hbm, quanta_ref),
            (bath_hbm, bath_ref),
            (rate_hbm, rate_ref),
        ],
        sems,
    )
    for copy in copies:
        copy.wait()
    coupling = coupling_ref[...]
    hamilton = (coupling + coupling.T) * 0.5 + jnp.where(row_ids == col_ids, energy_ref[...], 0.0)
    matrix_ref[...] = jnp.zeros_like(matrix_ref)
    matrix_ref[pl.ds(0, sites), pl.ds(LANES, sites)] = hamilton
    matrix_ref[pl.ds(LANES, sites), pl.ds(0, sites)] = -hamilton
    high, low = split(matrix_ref[...])
    dot = functools.partial(jnp.dot, preferred_element_type=jnp.float32)
    saves = []
    for a in range(aux):
        damp = jnp.float32(0.0)
        for place in range(depth):
            site = quanta_ref[place, a]
            rate = rate_ref[0, bath_ref[0, jnp.maximum(site, 0)]]
            damp = damp + jnp.where(site >= 0, rate, 0.0)
        here = pl.ds(a * sites, sites)
        for half in range(2):
            real, imag = store_ref[2 * half, here, :], store_ref[2 * half + 1, here, :]
            both = jnp.concatenate([real, imag], axis=1)
            both_high, both_low = split(both)
            product = dot(both_high, high) + (dot(both_low, high) + dot(both_high, low))
            if half == 0:
                product = product - damp * both
            else:
                product = -product
            acc_ref[2 * half, here, :] = product[:, :LANES]
            acc_ref[2 * half + 1, here, :] = product[:, LANES:]
        fields = merge([store_ref[f, here, :] for f in range(4)], lane_index((sites, LANES)), sites)
        for f in range(FIELDS):
            merged_ref[f, here, :] = fields[f]
        saves.append(
            pltpu.make_async_copy(acc_ref.at[:, here, :], acc_hbm.at[:, here, :], acc_sems.at[a])
        )
        saves[-1].start()
    tail = pl.ds(aux * sites, LANES - sites)
    merged_ref[:, tail, :] = jnp.zeros((FIELDS, LANES - sites, LANES), jnp.float32)
    for save in saves:
        save.wait()


def raise_kernel(
    sizes,
    band_ref,
    send_hbm,
    quanta_hbm,
    bath_hbm,
    rate_hbm,
    strength_hbm,
    arrived_ref,
    acc_hbm,
    sum_ref,
    column_ref,
    place_ref,
    coef_ref,
    work_ref,
    column_work,
    place_work,
    send_ref,
    quanta_ref,
    bath_ref,
    rate_ref,
    strength_ref,
    table_sems,
    acc_sems,
    tag_ref,
    sems,
):
    sites, aux, depth, peers, capacity, tiers = sizes
    rows = aux * sites
    band = band_ref[0]
    copies = read_tags(sizes, band, arrived_ref, tag_ref, sems)
    tables = fetch(
        [
            (send_hbm, send_ref),
            (quanta_hbm, quanta_ref),
            (bath_hbm, bath_ref),
            (rate_hbm, rate_ref),
            (strength_hbm, strength_ref),
        ],
        table_sems,
    )
    (load,) = fetch([(acc_hbm, work_ref.at[:, pl.ds(0, rows), :])], acc_sems)
    tail = pl.ds(rows, LANES - sites)
    work_ref[:, tail, :] = jnp.zeros((4, LANES - sites, LANES), jnp.float32)
    row_lane = lane_index((1, LANES))
    column_work[...] = jnp.zeros_like(column_work)
    place_work[...] = jnp.zeros_like(place_work)
    half = column_work.shape[0] // 2
    for table in tables:
        table.wait()
    for g in range(2):
        inside = band - g >= 0
        for q in range(peers):
            for j in range(capacity):
                l = (g * peers + q) * capacity + j
                at = (g * capacity + j) * peers + q
                entry = send_ref[0, l]
                clipped = jnp.maximum(entry, 0)
                source = clipped // depth
                site = quanta_ref[clipped % depth, source]
                usable = (entry >= 0) & (site >= 0) & inside
                safe = jnp.maximum(site, 0)
                weight = jnp.float32(0.0)
                for place in range(depth):
                    weight = weight + jnp.where(quanta_ref[place, source] == safe, 1.0, 0.0)
                weight = jnp.where(usable, weight, 0.0)
                bath = bath_ref[0, safe]
                strength = strength_ref[0, bath]
                turn = weight * (2.0 * thermal * strength)
                shared = -weight * (strength * rate_ref[0, bath])
                coef_ref[0, pl.ds(at, 1), :] = jnp.full((1, LANES), shared)
                coef_ref[1, pl.ds(at, 1), :] = jnp.full((1, LANES), turn)
                row = pl.ds(jnp.where(usable, source * sites + safe, rows), 1)
                for spot in (at, half + at):
                    slab = spot // LANES
                    place_work[slab, row, :] = jnp.where(
                        row_lane == spot % LANES, 1.0, place_work[slab, row, :]
                    )
                hot = (row_lane == safe).astype(jnp.float32)
                block = jnp.where(usable, source, aux)
                column_work[at, pl.ds(block, 1), :] = hot
                column_work[half + at, pl.ds(block, 1), :] = hot
    for slab in range(place_work.shape[0]):
        place_ref[:, pl.ds(slab * LANES, LANES)] = place_work[slab, pl.ds(0, rows), :].astype(
            jnp.bfloat16
        )
    for a in range(aux):
        column_ref[:, pl.ds(a * LANES, LANES)] = column_work[:, a, :].astype(jnp.bfloat16)
    for copy in copies:
        copy.wait()
    load.wait()
    for g in range(2):
        origin = jnp.minimum(band + g, tiers - 1)
        inside = band + g < tiers
        for p in range(peers):
            at_row = origin * peers + p
            for j in range(capacity):
                row = pl.ds(jnp.where(inside, tag_row(tag_ref, g, p, j, peers), rows), 1)
                parts = unmerge(
                    [
                        arrived_ref[at_row, :, pl.ds((j * FIELDS + f) * LANES, LANES)]
                        for f in range(FIELDS)
                    ],
                    row_lane,
                    sites,
                )
                work_ref[0, row, :] = work_ref[0, row, :] + parts[1]
                work_ref[1, row, :] = work_ref[1, row, :] - parts[0]
                work_ref[2, row, :] = work_ref[2, row, :] - parts[3]
                work_ref[3, row, :] = work_ref[3, row, :] + parts[2]
    for a in range(aux):
        here = pl.ds(a * sites, sites)
        for c in range(2):
            turned = work_ref[2 + c, pl.ds(a * sites, LANES), :].T[:sites, :]
            sum_ref[c, here, :] = work_ref[c, here, :] + turned


def lower_kernel(
    sizes,
    band_ref,
    returned_ref,
    sum_ref,
    column_ref,
    place_ref,
    coef_ref,
    out_hbm,
    work_ref,
    edge_ref,
    out_ref,
    sems,
):
    sites, aux, depth, peers, capacity, tiers = sizes
    tiles = 4 * sites // LANES
    pair_blocks = sites // (2 * SUB)
    chunk = aux * tiles * SUB
    slabs = capacity * FIELDS
    used = 2 * capacity * peers
    half = edge_ref.shape[1] // 2
    band = band_ref[0]
    lane = lane_index((peers, LANES))
    if used < half:
        for top in (used, half + used):
            edge_ref[:, pl.ds(top, half - used), :] = jnp.zeros(
                (4, half - used, LANES), jnp.float32
            )
    for g in range(2):
        target = jnp.maximum(band - g, 0)
        for j in range(capacity):
            start = target * (peers * slabs) + j * FIELDS
            parts = [
                returned_ref[pl.ds(start + f, peers, stride=slabs), :] for f in range(FIELDS)
            ]
            row_real, row_imag, col_real, col_imag = unmerge(parts, lane, sites)
            base = (g * capacity + j) * peers
            shared = coef_ref[0, pl.ds(base, peers), :]
            turn = coef_ref[1, pl.ds(base, peers), :]
            values = (
                shared * row_real + turn * row_imag,
                shared * row_imag - turn * row_real,
                shared * col_real - turn * col_imag,
                shared * col_imag + turn * col_real,
            )
            for f, value in enumerate(values):
                high = value.astype(jnp.bfloat16).astype(jnp.float32)
                edge_ref[f, pl.ds(base, peers), :] = high
                edge_ref[f, pl.ds(half + base, peers), :] = value - high
    dot = functools.partial(jnp.dot, preferred_element_type=jnp.float32)
    row_data = jnp.concatenate([edge_ref[0], edge_ref[1]], axis=1).astype(jnp.bfloat16)
    col_data = jnp.concatenate([edge_ref[2].T, edge_ref[3].T], axis=0).astype(jnp.bfloat16)
    for pair in range(aux // 2):
        columns = dot(col_data, column_ref[:, pl.ds(2 * pair * LANES, 2 * LANES)])
        for o in range(2):
            here = pl.ds((2 * pair + o) * sites, sites)
            placed = dot(place_ref[here, :], row_data)
            for c in range(2):
                work_ref[c, here, :] = (
                    sum_ref[c, here, :]
                    + placed[:, c * LANES : (c + 1) * LANES]
                    + columns[c * LANES : c * LANES + sites, o * LANES : (o + 1) * LANES]
                )
    lane = lane_index((SUB, LANES))
    copies = []
    for block in range(pair_blocks):
        for a in range(aux):
            base = a * sites + 2 * SUB * block
            even_real, even_imag, odd_real, odd_imag = (
                work_ref[c, pl.ds(base + o, SUB, stride=2), :] for o in (0, 1) for c in (0, 1)
            )
            turned_imag = pltpu.roll(even_imag, 96, 1)
            turned_real = pltpu.roll(odd_real, 64, 1)
            parts = (
                jnp.where(lane < 96, even_real, turned_imag),
                jnp.where(lane < 64, turned_imag, turned_real),
                jnp.where(lane < 32, turned_real, pltpu.roll(odd_imag, 32, 1)),
            )
            for u in range(tiles):
                start = a + aux * (tiles * SUB * block + u)
                out_ref[pl.ds(start, SUB, stride=aux * tiles), :] = parts[u]
        here = pl.ds(block * chunk, chunk)
        copies.append(pltpu.make_async_copy(out_ref.at[here, :], out_hbm.at[here, :], sems.at[block]))
        copies[-1].start()
    for copy in copies:
        copy.wait()


def on_device(
    section_state,
    coupling,
    site_energy,
    bath_rate,
    bath_strength,
    bath_of_site,
    quanta,
    send_list,
    dest_slot,
):
    sites = coupling.shape[0]
    aux, flat = section_state.shape
    depth = quanta.shape[1]
    lane_count = send_list.shape[1]
    peers = lax.axis_size("aux")
    tiers = lax.axis_size("tier")
    capacity = lane_count // (2 * peers)
    sizes = (sites, aux, depth, peers, capacity, tiers)
    rows = aux * sites
    padded = rows + LANES - sites
    slabs = capacity * FIELDS
    chunks = flat // LANES
    half = -(-lane_count // 64) * 64
    f32 = jnp.float32
    bf16 = jnp.bfloat16
    band = lax.axis_index("tier").reshape(1)
    tiled = section_state.reshape(aux, chunks, LANES).transpose(1, 0, 2).reshape(-1, LANES)
    turned_quanta = quanta.T
    bath_row = bath_of_site.reshape(1, -1)
    rate_row = bath_rate.reshape(1, -1)
    strength_row = bath_strength.reshape(1, -1)
    pair_blocks = sites // (2 * SUB)

    def call(kernel, name, inputs, outs, scratch):
        spaces = [space for space, _ in inputs]
        values = [
            value if space is SMEM else pltpu.with_memory_space_constraint(value, space)
            for space, value in inputs
        ]
        return pl.pallas_call(
            functools.partial(kernel, sizes),
            out_shape=[space(shape, dtype) for space, shape, dtype in outs],
            in_specs=[spec(space) for space in spaces],
            out_specs=[spec(space) for space, _, _ in outs],
            scratch_shapes=scratch,
            name=name,
            compiler_params=pltpu.CompilerParams(vmem_limit_bytes=24 * 1024 * 1024),
        )(*values)

    HBM = pltpu.HBM
    dma = pltpu.SemaphoreType.DMA
    store_shape = (4, padded, LANES)
    acc_shape = (4, rows, LANES)
    reply_shape = (tiers * peers, 1, slabs * LANES)
    payload_shape = (tiers * peers, 1, (slabs + 1) * LANES)
    tag_scratch = [SMEM((2 * peers, 1, LANES), f32), dma((2,))]
    flat_shape = (aux * chunks, LANES)
    send_table = SMEM(send_list.shape, jnp.int32)
    quanta_table = SMEM(turned_quanta.shape, jnp.int32)
    bath_table = SMEM(bath_row.shape, jnp.int32)
    site_table = SMEM(rate_row.shape, f32)
    trade = functools.partial(
        lax.all_to_all, axis_name=("tier", "aux"), split_axis=0, concat_axis=0, tiled=True
    )
    store, payload = call(
        pack_kernel,
        "pack",
        [
            (SMEM, band),
            (HBM, send_list),
            (HBM, turned_quanta),
            (HBM, dest_slot),
            (HBM, tiled),
        ],
        [(VMEM, store_shape, f32), (HBM, payload_shape, f32)],
        [
            VMEM(flat_shape, f32),
            VMEM((2, peers) + payload_shape[1:], f32),
            send_table,
            quanta_table,
            send_table,
            dma((pair_blocks,)),
            dma((3,)),
            dma((2,)),
        ],
    )
    arrived = trade(payload)
    acc, merged = call(
        local_kernel,
        "local",
        [
            (HBM, turned_quanta),
            (HBM, bath_row),
            (HBM, rate_row),
            (HBM, coupling),
            (HBM, site_energy.reshape(1, -1)),
            (VMEM, store),
        ],
        [(HBM, acc_shape, f32), (VMEM, (FIELDS, padded, LANES), f32)],
        [
            VMEM(acc_shape, f32),
            VMEM((2 * LANES, 2 * LANES), f32),
            VMEM(coupling.shape, f32),
            VMEM(rate_row.shape, f32),
            quanta_table,
            bath_table,
            site_table,
            dma((5,)),
            dma((aux,)),
        ],
    )
    (reply,) = call(
        answer_kernel,
        "answer",
        [(SMEM, band), (VMEM, arrived), (VMEM, merged)],
        [(HBM, reply_shape, f32)],
        [VMEM((2, peers) + reply_shape[1:], f32)] + tag_scratch + [dma((2,))],
    )
    returned = trade(reply)
    total, columns, places, coefs = call(
        raise_kernel,
        "raise",
        [
            (SMEM, band),
            (HBM, send_list),
            (HBM, turned_quanta),
            (HBM, bath_row),
            (HBM, rate_row),
            (HBM, strength_row),
            (VMEM, arrived),
            (HBM, acc),
        ],
        [
            (VMEM, (2, rows, LANES), f32),
            (VMEM, (2 * half, aux * LANES), bf16),
            (VMEM, (rows, 2 * half), bf16),
            (VMEM, (2, lane_count, LANES), f32),
        ],
        [
            VMEM(store_shape, f32),
            VMEM((2 * half, 2 * SUB, LANES), f32),
            VMEM((2 * half // LANES, padded, LANES), f32),
            send_table,
            quanta_table,
            bath_table,
            site_table,
            site_table,
            dma((5,)),
            dma((1,)),
        ]
        + tag_scratch,
    )
    (out,) = call(
        lower_kernel,
        "lower",
        [
            (SMEM, band),
            (VMEM, returned.reshape(-1, LANES)),
            (VMEM, total),
            (VMEM, columns),
            (VMEM, places),
            (VMEM, coefs),
        ],
        [(HBM, flat_shape, f32)],
        [
            VMEM((2, rows, LANES), f32),
            VMEM((4, 2 * half, LANES), f32),
            VMEM(flat_shape, f32),
            dma((pair_blocks,)),
        ],
    )
    return out.reshape(chunks, aux, LANES).transpose(1, 0, 2).reshape(aux, flat)


def solution(mesh):
    return jax.shard_map(
        on_device,
        mesh=mesh,
        in_specs=(
            P(("tier", "aux"), None),
            P(),
            P(),
            P(),
            P(),
            P(),
            P(("tier", "aux"), None),
            P(("tier", "aux"), None),
            P(("tier", "aux"), None),
        ),
        out_specs=P(("tier", "aux"), None),
        check_vma=False,
    )
```

```python
import functools

import jax
import jax.numpy as jnp
from jax import lax
from jax.experimental import pallas as pl
from jax.experimental.pallas import tpu as pltpu
from jax.sharding import PartitionSpec as P

thermal = 0.5
LANES = 128
SUB = 8
FIELDS = 3
TAG = 64
VMEM = pltpu.VMEM
SMEM = pltpu.SMEM


def spec(space):
    return pl.BlockSpec(memory_space=space)


def lane_index(shape):
    return lax.broadcasted_iota(jnp.int32, shape, 1)


def fetch(pairs, sems):
    copies = [
        pltpu.make_async_copy(source, target, sems.at[n]) for n, (source, target) in enumerate(pairs)
    ]
    for copy in copies:
        copy.start()
    return copies


def send_blocks(work_ref, wire_hbm, sems, band, step, tiers, peers):
    def block(g):
        at = jnp.clip(band + g * step, 0, tiers - 1) * peers
        return pltpu.make_async_copy(work_ref.at[g], wire_hbm.at[pl.ds(at, peers)], sems.at[g])

    return block


def merge(parts, lane, sites):
    rest = 2 * sites - LANES
    first, second, col_real, col_imag = parts
    return [
        first,
        jnp.where(lane < rest, second, pltpu.roll(col_imag, rest, 1)),
        jnp.where(lane < sites, col_real, pltpu.roll(col_imag, sites + rest - LANES, 1)),
    ]


def imaginary(first, second, lane, sites):
    spare = LANES - sites
    return jnp.where(lane < spare, pltpu.roll(first, spare, 1), pltpu.roll(second, spare, 1))


def unmerge(parts, lane, sites):
    rest = 2 * sites - LANES
    first, second, third = parts
    kept = LANES - rest
    col_imag = jnp.where(
        lane < kept, pltpu.roll(second, kept, 1), pltpu.roll(third, 2 * LANES - sites - rest, 1)
    )
    return first, imaginary(first, second, lane, sites), third, col_imag


def pack_kernel(
    sizes,
    band_ref,
    send_hbm,
    quanta_hbm,
    slot_hbm,
    state_hbm,
    store_ref,
    payload_hbm,
    state_ref,
    payload_ref,
    send_ref,
    quanta_ref,
    slot_ref,
    table_ref,
    sems,
    table_sems,
    wire_sems,
):
    sites, aux, depth, peers, capacity, tiers = sizes
    tiles = 4 * sites // LANES
    pair_blocks = sites // (2 * SUB)
    chunk = aux * tiles * SUB
    rows = aux * sites
    copies = fetch(
        [
            (state_hbm.at[pl.ds(b * chunk, chunk), :], state_ref.at[pl.ds(b * chunk, chunk), :])
            for b in range(pair_blocks)
        ],
        sems,
    )
    tables = fetch(
        [(send_hbm, send_ref), (quanta_hbm, quanta_ref), (slot_hbm, slot_ref)], table_sems
    )
    lane = lane_index((SUB, LANES))
    rest = 2 * sites - LANES
    store_ref[pl.ds(2, 2)] = jnp.zeros((2,) + store_ref.shape[1:], jnp.float32)
    table_ref[...] = jnp.zeros_like(table_ref)
    for block in range(pair_blocks):
        copies[block].wait()
        for a in range(aux):
            first, middle, last = (
                state_ref[pl.ds(a + aux * (tiles * SUB * block + u), SUB, stride=aux * tiles), :]
                for u in range(tiles)
            )
            middle_turned = pltpu.roll(middle, rest, 1)
            last_turned = pltpu.roll(last, rest, 1)
            base = a * sites + 2 * SUB * block
            store_ref[0, pl.ds(base, SUB, stride=2), :] = first
            store_ref[1, pl.ds(base, SUB, stride=2), :] = middle
            store_ref[0, pl.ds(base + 1, SUB, stride=2), :] = jnp.where(
                lane < rest, middle_turned, last_turned
            )
            store_ref[1, pl.ds(base + 1, SUB, stride=2), :] = last_turned
    for table in tables:
        table.wait()
    band = band_ref[0]
    row_lane = lane_index((1, LANES))
    entry = send_ref[...]
    lane_count = entry.shape[1]
    site = jnp.full(entry.shape, -1, jnp.int32)
    base = jnp.zeros(entry.shape, jnp.int32)
    for source in range(aux):
        for place in range(depth):
            here = entry == source * depth + place
            site = jnp.where(here, quanta_ref[place, source], site)
            base = jnp.where(here, source * sites, base)
    group = (lane_index(entry.shape) >= peers * capacity).astype(jnp.int32)
    usable = (entry >= 0) & (site >= 0) & (band - group >= 0)
    site = jnp.maximum(site, 0)
    table_ref[0, :, pl.ds(0, lane_count)] = base + site
    table_ref[1, :, pl.ds(0, lane_count)] = jnp.where(usable, slot_ref[...] * sites, rows)
    table_ref[2, :, pl.ds(0, lane_count)] = jnp.where(usable, site, 0)
    slot_tags, site_tags = table_ref[1], table_ref[2]
    for g in range(2):
        for q in range(peers):
            at = (g * peers + q) * capacity
            tags = jnp.where(
                row_lane < TAG,
                pltpu.roll(slot_tags, (LANES - at) % LANES, 1),
                pltpu.roll(site_tags, (LANES + TAG - at) % LANES, 1),
            )
            payload_ref[g, q, :, pl.ds(capacity * FIELDS * LANES, LANES)] = tags.astype(jnp.float32)
    for a in range(aux):
        here = pl.ds(a * sites, sites)
        turned = store_ref[0, here, :].T
        store_ref[2, here, pl.ds(0, sites)] = turned[:sites, :]
        store_ref[3, pl.ds(a * sites, LANES - sites), pl.ds(0, sites)] = turned[sites:, :]
        turned = store_ref[1, here, :].T
        store_ref[3, pl.ds(a * sites + LANES - sites, rest), pl.ds(0, sites)] = turned[:rest, :]
    block = send_blocks(payload_ref, payload_hbm, wire_sems, band, -1, tiers, peers)
    for g in (1, 0):
        for q in range(peers):
            for j in range(capacity):
                row = pl.ds(table_ref[0, 0, (g * peers + q) * capacity + j], 1)
                fields = merge([store_ref[f, row, :] for f in range(4)], row_lane, sites)
                for f in range(FIELDS):
                    payload_ref[g, q, :, pl.ds((j * FIELDS + f) * LANES, LANES)] = fields[f]
        if g == 0:
            block(g).start()
        else:
            pl.when(band >= g)(block(g).start)
    block(0).wait()
    pl.when(band >= 1)(block(1).wait)


def read_tags(sizes, band, arrived_ref, tag_ref, sems):
    sites, aux, depth, peers, capacity, tiers = sizes
    copies = [
        pltpu.make_async_copy(
            arrived_ref.at[
                pl.ds(jnp.minimum(band + g, tiers - 1) * peers, peers),
                :,
                pl.ds(capacity * FIELDS * LANES, LANES),
            ],
            tag_ref.at[pl.ds(g * peers, peers)],
            sems.at[g],
        )
        for g in range(2)
    ]
    for copy in copies:
        copy.start()
    return copies


def tag_row(tag_ref, g, p, j, peers):
    at = g * peers + p
    return tag_ref[at, 0, j].astype(jnp.int32) + tag_ref[at, 0, TAG + j].astype(jnp.int32)


def answer_kernel(sizes, band_ref, arrived_ref, store_ref, reply_hbm, reply_ref, row_ref, wire_sems):
    sites, aux, depth, peers, capacity, tiers = sizes
    band = band_ref[0]
    block = send_blocks(reply_ref, reply_hbm, wire_sems, band, 1, tiers, peers)
    for g in (1, 0):
        origin = jnp.minimum(band + g, tiers - 1)
        for p in range(peers):
            tags = arrived_ref[origin * peers + p, :, pl.ds(capacity * FIELDS * LANES, LANES)]
            row_ref[g * peers + p] = (tags + pltpu.roll(tags, TAG, 1)).astype(jnp.int32)
    for g in (1, 0):
        for p in range(peers):
            for j in range(capacity):
                row = pl.ds(row_ref[g * peers + p, 0, j], 1)
                for f in range(FIELDS):
                    reply_ref[g, p, :, pl.ds((j * FIELDS + f) * LANES, LANES)] = store_ref[f, row, :]
        if g == 0:
            block(g).start()
        else:
            pl.when(band + g < tiers)(block(g).start)
    block(0).wait()
    pl.when(band + 1 < tiers)(block(1).wait)


def split(value):
    high = value.astype(jnp.bfloat16)
    low = (value - high.astype(jnp.float32)).astype(jnp.bfloat16)
    return high, low


def local_kernel(
    sizes,
    quanta_hbm,
    bath_hbm,
    rate_hbm,
    coupling_hbm,
    energy_hbm,
    store_ref,
    acc_hbm,
    merged_ref,
    acc_ref,
    matrix_ref,
    coupling_ref,
    energy_ref,
    quanta_ref,
    bath_ref,
    rate_ref,
    sems,
    acc_sems,
):
    sites, aux, depth, peers, capacity, tiers = sizes
    row_ids = lax.broadcasted_iota(jnp.int32, (sites, sites), 0)
    col_ids = lax.broadcasted_iota(jnp.int32, (sites, sites), 1)
    copies = fetch(
        [
            (coupling_hbm, coupling_ref),
            (energy_hbm, energy_ref),
            (quanta_hbm, quanta_ref),
            (bath_hbm, bath_ref),
            (rate_hbm, rate_ref),
        ],
        sems,
    )
    for copy in copies:
        copy.wait()
    coupling = coupling_ref[...]
    hamilton = (coupling + coupling.T) * 0.5 + jnp.where(row_ids == col_ids, energy_ref[...], 0.0)
    matrix_ref[...] = jnp.zeros_like(matrix_ref)
    splits = []
    for half, start in enumerate((sites, LANES)):
        matrix_ref[half, pl.ds(0, sites), pl.ds(LANES, sites)] = hamilton
        matrix_ref[half, pl.ds(start, sites), pl.ds(0, sites)] = -hamilton
        splits.append(split(matrix_ref[half]))
    lane = lane_index((sites, LANES))
    dot = functools.partial(jnp.dot, preferred_element_type=jnp.float32)
    saves = []
    for a in range(aux):
        damp = jnp.float32(0.0)
        for place in range(depth):
            site = quanta_ref[place, a]
            rate = rate_ref[0, bath_ref[0, jnp.maximum(site, 0)]]
            damp = damp + jnp.where(site >= 0, rate, 0.0)
        here = pl.ds(a * sites, sites)
        for half in range(2):
            high, low = splits[half]
            first, second = store_ref[2 * half, here, :], store_ref[2 * half + 1, here, :]
            both = jnp.concatenate([first, second], axis=1)
            both_high, both_low = split(both)
            product = dot(both_high, high) + (dot(both_low, high) + dot(both_high, low))
            if half == 0:
                imag = imaginary(first, second, lane, sites)
                product = product - damp * jnp.concatenate([first, imag], axis=1)
            else:
                product = -product
            acc_ref[2 * half, here, :] = product[:, :LANES]
            acc_ref[2 * half + 1, here, :] = product[:, LANES:]
        fields = merge([store_ref[f, here, :] for f in range(4)], lane, sites)
        for f in range(FIELDS):
            merged_ref[f, here, :] = fields[f]
        saves.append(
            pltpu.make_async_copy(acc_ref.at[:, here, :], acc_hbm.at[:, here, :], acc_sems.at[a])
        )
        saves[-1].start()
    tail = pl.ds(aux * sites, LANES - sites)
    merged_ref[:, tail, :] = jnp.zeros((FIELDS, LANES - sites, LANES), jnp.float32)
    for save in saves:
        save.wait()


def raise_kernel(
    sizes,
    band_ref,
    send_hbm,
    quanta_hbm,
    bath_hbm,
    rate_hbm,
    strength_hbm,
    arrived_ref,
    acc_hbm,
    sum_ref,
    column_ref,
    place_ref,
    coef_ref,
    work_ref,
    column_work,
    place_work,
    send_ref,
    quanta_ref,
    bath_ref,
    rate_ref,
    strength_ref,
    table_sems,
    acc_sems,
    tag_ref,
    sems,
):
    sites, aux, depth, peers, capacity, tiers = sizes
    rows = aux * sites
    band = band_ref[0]
    copies = read_tags(sizes, band, arrived_ref, tag_ref, sems)
    tables = fetch(
        [
            (send_hbm, send_ref),
            (quanta_hbm, quanta_ref),
            (bath_hbm, bath_ref),
            (rate_hbm, rate_ref),
            (strength_hbm, strength_ref),
        ],
        table_sems,
    )
    (load,) = fetch([(acc_hbm, work_ref.at[:, pl.ds(0, rows), :])], acc_sems)
    tail = pl.ds(rows, LANES - sites)
    work_ref[:, tail, :] = jnp.zeros((4, LANES - sites, LANES), jnp.float32)
    row_lane = lane_index((1, LANES))
    column_work[...] = jnp.zeros_like(column_work)
    place_work[...] = jnp.zeros_like(place_work)
    half = column_work.shape[0] // 2
    for table in tables:
        table.wait()
    for g in range(2):
        inside = band - g >= 0
        for q in range(peers):
            for j in range(capacity):
                l = (g * peers + q) * capacity + j
                at = (g * capacity + j) * peers + q
                entry = send_ref[0, l]
                clipped = jnp.maximum(entry, 0)
                source = clipped // depth
                site = quanta_ref[clipped % depth, source]
                usable = (entry >= 0) & (site >= 0) & inside
                safe = jnp.maximum(site, 0)
                weight = jnp.float32(0.0)
                for place in range(depth):
                    weight = weight + jnp.where(quanta_ref[place, source] == safe, 1.0, 0.0)
                weight = jnp.where(usable, weight, 0.0)
                bath = bath_ref[0, safe]
                strength = strength_ref[0, bath]
                turn = weight * (2.0 * thermal * strength)
                shared = -weight * (strength * rate_ref[0, bath])
                coef_ref[0, pl.ds(at, 1), :] = jnp.full((1, LANES), shared)
                coef_ref[1, pl.ds(at, 1), :] = jnp.full((1, LANES), turn)
                row = pl.ds(jnp.where(usable, source * sites + safe, rows), 1)
                for spot in (at, half + at):
                    slab = spot // LANES
                    place_work[slab, row, :] = jnp.where(
                        row_lane == spot % LANES, 1.0, place_work[slab, row, :]
                    )
                hot = (row_lane == safe).astype(jnp.float32)
                block = jnp.where(usable, source, aux)
                column_work[at, pl.ds(block, 1), :] = hot
                column_work[half + at, pl.ds(block, 1), :] = hot
    for slab in range(place_work.shape[0]):
        place_ref[:, pl.ds(slab * LANES, LANES)] = place_work[slab, pl.ds(0, rows), :].astype(
            jnp.bfloat16
        )
    for a in range(aux):
        column_ref[:, pl.ds(a * LANES, LANES)] = column_work[:, a, :].astype(jnp.bfloat16)
    for copy in copies:
        copy.wait()
    load.wait()
    for g in range(2):
        origin = jnp.minimum(band + g, tiers - 1)
        inside = band + g < tiers
        for p in range(peers):
            at_row = origin * peers + p
            for j in range(capacity):
                row = pl.ds(jnp.where(inside, tag_row(tag_ref, g, p, j, peers), rows), 1)
                parts = unmerge(
                    [
                        arrived_ref[at_row, :, pl.ds((j * FIELDS + f) * LANES, LANES)]
                        for f in range(FIELDS)
                    ],
                    row_lane,
                    sites,
                )
                work_ref[0, row, :] = work_ref[0, row, :] + parts[1]
                work_ref[1, row, :] = work_ref[1, row, :] - parts[0]
                work_ref[2, row, :] = work_ref[2, row, :] - parts[3]
                work_ref[3, row, :] = work_ref[3, row, :] + parts[2]
    for a in range(aux):
        here = pl.ds(a * sites, sites)
        for c in range(2):
            turned = work_ref[2 + c, pl.ds(a * sites, LANES), :].T[:sites, :]
            sum_ref[c, here, :] = work_ref[c, here, :] + turned


def lower_kernel(
    sizes,
    band_ref,
    returned_ref,
    sum_ref,
    column_ref,
    place_ref,
    coef_ref,
    out_hbm,
    work_ref,
    edge_ref,
    out_ref,
    sems,
):
    sites, aux, depth, peers, capacity, tiers = sizes
    tiles = 4 * sites // LANES
    pair_blocks = sites // (2 * SUB)
    chunk = aux * tiles * SUB
    slabs = capacity * FIELDS
    used = 2 * capacity * peers
    half = edge_ref.shape[1] // 2
    band = band_ref[0]
    lane = lane_index((peers, LANES))
    if used < half:
        for top in (used, half + used):
            edge_ref[:, pl.ds(top, half - used), :] = jnp.zeros(
                (4, half - used, LANES), jnp.float32
            )
    for g in range(2):
        target = jnp.maximum(band - g, 0)
        for j in range(capacity):
            start = target * (peers * slabs) + j * FIELDS
            parts = [
                returned_ref[pl.ds(start + f, peers, stride=slabs), :] for f in range(FIELDS)
            ]
            row_real, row_imag, col_real, col_imag = unmerge(parts, lane, sites)
            base = (g * capacity + j) * peers
            shared = coef_ref[0, pl.ds(base, peers), :]
            turn = coef_ref[1, pl.ds(base, peers), :]
            values = (
                shared * row_real + turn * row_imag,
                shared * row_imag - turn * row_real,
                shared * col_real - turn * col_imag,
                shared * col_imag + turn * col_real,
            )
            for f, value in enumerate(values):
                high = value.astype(jnp.bfloat16).astype(jnp.float32)
                edge_ref[f, pl.ds(base, peers), :] = high
                edge_ref[f, pl.ds(half + base, peers), :] = value - high
    dot = functools.partial(jnp.dot, preferred_element_type=jnp.float32)
    row_data = jnp.concatenate([edge_ref[0], edge_ref[1]], axis=1).astype(jnp.bfloat16)
    col_data = jnp.concatenate([edge_ref[2].T, edge_ref[3].T], axis=0).astype(jnp.bfloat16)
    for pair in range(aux // 2):
        columns = dot(col_data, column_ref[:, pl.ds(2 * pair * LANES, 2 * LANES)])
        for o in range(2):
            here = pl.ds((2 * pair + o) * sites, sites)
            placed = dot(place_ref[here, :], row_data)
            for c in range(2):
                work_ref[c, here, :] = (
                    sum_ref[c, here, :]
                    + placed[:, c * LANES : (c + 1) * LANES]
                    + columns[c * LANES : c * LANES + sites, o * LANES : (o + 1) * LANES]
                )
    lane = lane_index((SUB, LANES))
    copies = []
    for block in range(pair_blocks):
        for a in range(aux):
            base = a * sites + 2 * SUB * block
            even_real, even_imag, odd_real, odd_imag = (
                work_ref[c, pl.ds(base + o, SUB, stride=2), :] for o in (0, 1) for c in (0, 1)
            )
            turned_imag = pltpu.roll(even_imag, 96, 1)
            turned_real = pltpu.roll(odd_real, 64, 1)
            parts = (
                jnp.where(lane < 96, even_real, turned_imag),
                jnp.where(lane < 64, turned_imag, turned_real),
                jnp.where(lane < 32, turned_real, pltpu.roll(odd_imag, 32, 1)),
            )
            for u in range(tiles):
                start = a + aux * (tiles * SUB * block + u)
                out_ref[pl.ds(start, SUB, stride=aux * tiles), :] = parts[u]
        here = pl.ds(block * chunk, chunk)
        copies.append(pltpu.make_async_copy(out_ref.at[here, :], out_hbm.at[here, :], sems.at[block]))
        copies[-1].start()
    for copy in copies:
        copy.wait()


def on_device(
    section_state,
    coupling,
    site_energy,
    bath_rate,
    bath_strength,
    bath_of_site,
    quanta,
    send_list,
    dest_slot,
):
    sites = coupling.shape[0]
    aux, flat = section_state.shape
    depth = quanta.shape[1]
    lane_count = send_list.shape[1]
    peers = lax.axis_size("aux")
    tiers = lax.axis_size("tier")
    capacity = lane_count // (2 * peers)
    sizes = (sites, aux, depth, peers, capacity, tiers)
    rows = aux * sites
    padded = rows + LANES - sites
    slabs = capacity * FIELDS
    chunks = flat // LANES
    half = -(-lane_count // 64) * 64
    f32 = jnp.float32
    bf16 = jnp.bfloat16
    band = lax.axis_index("tier").reshape(1)
    tiled = section_state.reshape(aux, chunks, LANES).transpose(1, 0, 2).reshape(-1, LANES)
    turned_quanta = quanta.T
    bath_row = bath_of_site.reshape(1, -1)
    rate_row = bath_rate.reshape(1, -1)
    strength_row = bath_strength.reshape(1, -1)
    pair_blocks = sites // (2 * SUB)

    def call(kernel, name, inputs, outs, scratch):
        spaces = [space for space, _ in inputs]
        values = [
            value if space is SMEM else pltpu.with_memory_space_constraint(value, space)
            for space, value in inputs
        ]
        return pl.pallas_call(
            functools.partial(kernel, sizes),
            out_shape=[space(shape, dtype) for space, shape, dtype in outs],
            in_specs=[spec(space) for space in spaces],
            out_specs=[spec(space) for space, _, _ in outs],
            scratch_shapes=scratch,
            name=name,
            compiler_params=pltpu.CompilerParams(vmem_limit_bytes=24 * 1024 * 1024),
        )(*values)

    HBM = pltpu.HBM
    dma = pltpu.SemaphoreType.DMA
    store_shape = (4, padded, LANES)
    acc_shape = (4, rows, LANES)
    reply_shape = (tiers * peers, 1, slabs * LANES)
    payload_shape = (tiers * peers, 1, (slabs + 1) * LANES)
    tag_scratch = [SMEM((2 * peers, 1, LANES), f32), dma((2,))]
    flat_shape = (aux * chunks, LANES)
    send_table = SMEM(send_list.shape, jnp.int32)
    quanta_table = SMEM(turned_quanta.shape, jnp.int32)
    bath_table = SMEM(bath_row.shape, jnp.int32)
    site_table = SMEM(rate_row.shape, f32)
    trade = functools.partial(
        lax.all_to_all, axis_name=("tier", "aux"), split_axis=0, concat_axis=0, tiled=True
    )
    store, payload = call(
        pack_kernel,
        "pack",
        [
            (SMEM, band),
            (HBM, send_list),
            (HBM, turned_quanta),
            (HBM, dest_slot),
            (HBM, tiled),
        ],
        [(VMEM, acc_shape, f32), (HBM, payload_shape, f32)],
        [
            VMEM(flat_shape, f32),
            VMEM((2, peers) + payload_shape[1:], f32),
            VMEM(send_list.shape, jnp.int32),
            quanta_table,
            VMEM(dest_slot.shape, jnp.int32),
            VMEM((3, 1, LANES), jnp.int32),
            dma((pair_blocks,)),
            dma((3,)),
            dma((2,)),
        ],
    )
    arrived = trade(payload)
    acc, merged = call(
        local_kernel,
        "local",
        [
            (HBM, turned_quanta),
            (HBM, bath_row),
            (HBM, rate_row),
            (HBM, coupling),
            (HBM, site_energy.reshape(1, -1)),
            (VMEM, store),
        ],
        [(HBM, acc_shape, f32), (VMEM, (FIELDS, padded, LANES), f32)],
        [
            VMEM(acc_shape, f32),
            VMEM((2, 2 * LANES, 2 * LANES), f32),
            VMEM(coupling.shape, f32),
            VMEM(rate_row.shape, f32),
            quanta_table,
            bath_table,
            site_table,
            dma((5,)),
            dma((aux,)),
        ],
    )
    (reply,) = call(
        answer_kernel,
        "answer",
        [(SMEM, band), (VMEM, arrived), (VMEM, merged)],
        [(HBM, reply_shape, f32)],
        [
            VMEM((2, peers) + reply_shape[1:], f32),
            VMEM((2 * peers, 1, LANES), jnp.int32),
            dma((2,)),
        ],
    )
    returned = trade(reply)
    total, columns, places, coefs = call(
        raise_kernel,
        "raise",
        [
            (SMEM, band),
            (HBM, send_list),
            (HBM, turned_quanta),
            (HBM, bath_row),
            (HBM, rate_row),
            (HBM, strength_row),
            (VMEM, arrived),
            (HBM, acc),
        ],
        [
            (VMEM, (2, rows, LANES), f32),
            (VMEM, (2 * half, aux * LANES), bf16),
            (VMEM, (rows, 2 * half), bf16),
            (VMEM, (2, lane_count, LANES), f32),
        ],
        [
            VMEM(store_shape, f32),
            VMEM((2 * half, 2 * SUB, LANES), f32),
            VMEM((2 * half // LANES, padded, LANES), f32),
            send_table,
            quanta_table,
            bath_table,
            site_table,
            site_table,
            dma((5,)),
            dma((1,)),
        ]
        + tag_scratch,
    )
    (out,) = call(
        lower_kernel,
        "lower",
        [
            (SMEM, band),
            (VMEM, returned.reshape(-1, LANES)),
            (VMEM, total),
            (VMEM, columns),
            (VMEM, places),
            (VMEM, coefs),
        ],
        [(HBM, flat_shape, f32)],
        [
            VMEM((2, rows, LANES), f32),
            VMEM((4, 2 * half, LANES), f32),
            VMEM(flat_shape, f32),
            dma((pair_blocks,)),
        ],
    )
    return out.reshape(chunks, aux, LANES).transpose(1, 0, 2).reshape(aux, flat)


def solution(mesh):
    return jax.shard_map(
        on_device,
        mesh=mesh,
        in_specs=(
            P(("tier", "aux"), None),
            P(),
            P(),
            P(),
            P(),
            P(),
            P(("tier", "aux"), None),
            P(("tier", "aux"), None),
            P(("tier", "aux"), None),
        ),
        out_specs=P(("tier", "aux"), None),
        check_vma=False,
    )
```

```python
import functools

import jax
import jax.numpy as jnp
from jax import lax
from jax.experimental import pallas as pl
from jax.experimental.pallas import tpu as pltpu
from jax.sharding import PartitionSpec as P

thermal = 0.5
LANES = 128
SUB = 8
FIELDS = 3
TAG = 64
VMEM = pltpu.VMEM
SMEM = pltpu.SMEM


def spec(space):
    return pl.BlockSpec(memory_space=space)


def lane_index(shape):
    return lax.broadcasted_iota(jnp.int32, shape, 1)


def fetch(pairs, sems):
    copies = [
        pltpu.make_async_copy(source, target, sems.at[n]) for n, (source, target) in enumerate(pairs)
    ]
    for copy in copies:
        copy.start()
    return copies


def send_blocks(work_ref, wire_hbm, sems, band, step, tiers, peers):
    def block(g):
        at = jnp.clip(band + g * step, 0, tiers - 1) * peers
        return pltpu.make_async_copy(work_ref.at[g], wire_hbm.at[pl.ds(at, peers)], sems.at[g])

    return block


def imaginary(first, second, lane, sites):
    spare = LANES - sites
    return jnp.where(lane < spare, pltpu.roll(first, spare, 1), pltpu.roll(second, spare, 1))


def unmerge(parts, lane, sites):
    rest = 2 * sites - LANES
    first, second, third = parts
    kept = LANES - rest
    col_imag = jnp.where(
        lane < kept, pltpu.roll(second, kept, 1), pltpu.roll(third, 2 * LANES - sites - rest, 1)
    )
    return first, imaginary(first, second, lane, sites), third, col_imag


def pack_kernel(
    sizes,
    band_ref,
    send_hbm,
    quanta_hbm,
    slot_hbm,
    state_hbm,
    store_ref,
    payload_ref,
    state_ref,
    send_ref,
    quanta_ref,
    slot_ref,
    table_ref,
    row_ref,
    sems,
    table_sems,
):
    sites, aux, depth, peers, capacity, tiers = sizes
    tiles = 4 * sites // LANES
    pair_blocks = sites // (2 * SUB)
    chunk = aux * tiles * SUB
    rows = aux * sites
    tables = fetch(
        [(send_hbm, send_ref), (quanta_hbm, quanta_ref), (slot_hbm, slot_ref)], table_sems
    )
    copies = fetch(
        [
            (state_hbm.at[pl.ds(b * chunk, chunk), :], state_ref.at[pl.ds(b * chunk, chunk), :])
            for b in range(pair_blocks)
        ],
        sems,
    )
    lane = lane_index((SUB, LANES))
    rest = 2 * sites - LANES
    store_ref[:, pl.ds(rows, LANES - sites), :] = jnp.zeros(
        (FIELDS, LANES - sites, LANES), jnp.float32
    )
    table_ref[...] = jnp.zeros_like(table_ref)
    for table in tables:
        table.wait()
    band = band_ref[0]
    row_lane = lane_index((1, LANES))
    entry = send_ref[...]
    lane_count = entry.shape[1]
    site = jnp.full(entry.shape, -1, jnp.int32)
    base = jnp.zeros(entry.shape, jnp.int32)
    for source in range(aux):
        for place in range(depth):
            here = entry == source * depth + place
            site = jnp.where(here, quanta_ref[place, source], site)
            base = jnp.where(here, source * sites, base)
    group = (lane_index(entry.shape) >= peers * capacity).astype(jnp.int32)
    usable = (entry >= 0) & (site >= 0) & (band - group >= 0)
    site = jnp.maximum(site, 0)
    table_ref[0, :, pl.ds(0, lane_count)] = base + site
    table_ref[1, :, pl.ds(0, lane_count)] = jnp.where(usable, slot_ref[...] * sites, rows)
    table_ref[2, :, pl.ds(0, lane_count)] = jnp.where(usable, site, 0)
    slot_tags, site_tags = table_ref[1], table_ref[2]
    for g in (1, 0):
        for q in range(peers):
            at = (g * peers + q) * capacity
            tags = jnp.where(
                row_lane < TAG,
                pltpu.roll(slot_tags, (LANES - at) % LANES, 1),
                pltpu.roll(site_tags, (LANES + TAG - at) % LANES, 1),
            )
            at_row = jnp.maximum(band - g, 0) * peers + q
            payload_ref[at_row, :, pl.ds(capacity * FIELDS * LANES, LANES)] = tags.astype(
                jnp.float32
            )
    for l in range(lane_count):
        row_ref[l] = table_ref[0, 0, l]
    for block in range(pair_blocks):
        copies[block].wait()
        for a in range(aux):
            first, middle, last = (
                state_ref[pl.ds(a + aux * (tiles * SUB * block + u), SUB, stride=aux * tiles), :]
                for u in range(tiles)
            )
            middle_turned = pltpu.roll(middle, rest, 1)
            last_turned = pltpu.roll(last, rest, 1)
            base = a * sites + 2 * SUB * block
            store_ref[0, pl.ds(base, SUB, stride=2), :] = first
            store_ref[1, pl.ds(base, SUB, stride=2), :] = middle
            store_ref[0, pl.ds(base + 1, SUB, stride=2), :] = jnp.where(
                lane < rest, middle_turned, last_turned
            )
            store_ref[1, pl.ds(base + 1, SUB, stride=2), :] = last_turned
    for a in range(aux):
        here = pl.ds(a * sites, sites)
        first = store_ref[0, here, :].T
        second = store_ref[1, here, :].T
        col_imag = jnp.concatenate([first[sites:, :], second[:rest, :]], axis=0)
        store_ref[2, here, pl.ds(0, sites)] = first[:sites, :]
        store_ref[1, here, pl.ds(rest, LANES - rest)] = col_imag[:, : LANES - rest]
        store_ref[2, here, pl.ds(sites, LANES - sites)] = col_imag[:, LANES - rest :]
    for g in (1, 0):
        for q in range(peers):
            at_row = jnp.maximum(band - g, 0) * peers + q
            for j in range(capacity):
                row = pl.ds(row_ref[(g * peers + q) * capacity + j], 1)
                for f in range(FIELDS):
                    payload_ref[at_row, :, pl.ds((j * FIELDS + f) * LANES, LANES)] = store_ref[
                        f, row, :
                    ]


def read_rows(sizes, band, arrived_ref, row_ref):
    sites, aux, depth, peers, capacity, tiers = sizes
    slabs = capacity * FIELDS + 1
    for g in range(2):
        origin = jnp.minimum(band + g, tiers - 1) * peers
        for p in range(peers):
            tags = arrived_ref[pl.ds((origin + p) * slabs + slabs - 1, 1), :]
            total = (tags + pltpu.roll(tags, TAG, 1)).astype(jnp.int32)
            row_ref[g * peers + p] = jnp.where(band + g < tiers, total, aux * sites)


def answer_kernel(sizes, band_ref, arrived_ref, store_ref, reply_hbm, reply_ref, row_ref, wire_sems):
    sites, aux, depth, peers, capacity, tiers = sizes
    band = band_ref[0]
    block = send_blocks(reply_ref, reply_hbm, wire_sems, band, 1, tiers, peers)
    read_rows(sizes, band, arrived_ref, row_ref)
    for g in (1, 0):
        for p in range(peers):
            for j in range(capacity):
                row = pl.ds(row_ref[g * peers + p, 0, j], 1)
                for f in range(FIELDS):
                    reply_ref[g, p, :, pl.ds((j * FIELDS + f) * LANES, LANES)] = store_ref[f, row, :]
        if g == 0:
            block(g).start()
        else:
            pl.when(band + g < tiers)(block(g).start)
    block(0).wait()
    pl.when(band + 1 < tiers)(block(1).wait)


def split(value):
    high = value.astype(jnp.bfloat16)
    low = (value - high.astype(jnp.float32)).astype(jnp.bfloat16)
    return high, low


def spread(row):
    return jnp.broadcast_to(row, (row.shape[1], row.shape[1])).T


def middle_kernel(
    sizes,
    band_ref,
    send_hbm,
    quanta_hbm,
    bath_hbm,
    rate_hbm,
    strength_hbm,
    coupling_hbm,
    energy_hbm,
    arrived_ref,
    store_ref,
    sum_ref,
    column_ref,
    place_ref,
    coef_ref,
    work_ref,
    matrix_ref,
    edge_ref,
    row_ref,
    coupling_ref,
    vector_ref,
    send_ref,
    bath_row,
    quanta_ref,
    bath_ref,
    rate_ref,
    index_ref,
    sems,
):
    sites, aux, depth, peers, capacity, tiers = sizes
    rows = aux * sites
    rest = 2 * sites - LANES
    f32 = jnp.float32
    band = band_ref[0]
    copies = fetch(
        [
            (coupling_hbm, coupling_ref),
            (energy_hbm, vector_ref.at[0]),
            (rate_hbm, vector_ref.at[1]),
            (strength_hbm, vector_ref.at[2]),
            (send_hbm, send_ref),
            (bath_hbm, bath_row),
            (quanta_hbm, quanta_ref),
            (bath_hbm, bath_ref),
            (rate_hbm, rate_ref),
        ],
        sems,
    )
    read_rows(sizes, band, arrived_ref, row_ref)
    lane = lane_index((peers, LANES))
    for g in range(2):
        origin = jnp.minimum(band + g, tiers - 1) * peers
        for j in range(capacity):
            slabs = capacity * FIELDS + 1
            parts = [
                arrived_ref[pl.ds(origin * slabs + j * FIELDS + f, peers, stride=slabs), :]
                for f in range(FIELDS)
            ]
            row_real, row_imag, col_real, col_imag = unmerge(parts, lane, sites)
            for f, value in enumerate((row_imag, -row_real, -col_imag, col_real)):
                edge_ref[f, pl.ds(g * peers * capacity + j, peers, stride=capacity), :] = value
    matrix_ref[...] = jnp.zeros_like(matrix_ref)
    index_ref[...] = jnp.full(index_ref.shape, -1.0, f32)
    work_ref[:, pl.ds(rows, LANES - sites), :] = jnp.zeros((4, LANES - sites, LANES), f32)
    for copy in copies:
        copy.wait()
    row_ids = lax.broadcasted_iota(jnp.int32, (sites, sites), 0)
    col_ids = lane_index((sites, sites))
    coupling = coupling_ref[...]
    hamilton = (coupling + coupling.T) * 0.5 + jnp.where(row_ids == col_ids, vector_ref[0], 0.0)
    real, imag = pl.ds(0, sites), pl.ds(LANES, sites)
    matrix_ref[0, real, imag] = hamilton
    matrix_ref[0, pl.ds(sites, sites), real] = -hamilton
    matrix_ref[1, pl.ds(LANES, sites), imag] = -hamilton
    matrix_ref[1, pl.ds(rest, LANES - rest), real] = hamilton[: LANES - rest, :]
    matrix_ref[1, pl.ds(LANES + sites, LANES - sites), real] = hamilton[LANES - rest :, :]
    dot = functools.partial(jnp.dot, preferred_element_type=f32)
    splits = [split(matrix_ref[half]) for half in range(2)]
    lane = lane_index((sites, LANES))
    for a in range(aux):
        damp = f32(0.0)
        for place in range(depth):
            site = quanta_ref[place, a]
            rate = rate_ref[0, bath_ref[0, jnp.maximum(site, 0)]]
            damp = damp + jnp.where(site >= 0, rate, 0.0)
        here = pl.ds(a * sites, sites)
        for half in range(2):
            high, low = splits[half]
            first, second = store_ref[half, here, :], store_ref[half + 1, here, :]
            both_high, both_low = split(jnp.concatenate([first, second], axis=1))
            product = dot(both_high, high) + (dot(both_low, high) + dot(both_high, low))
            pair = [product[:, :LANES], product[:, LANES:]]
            if half == 0:
                pair[0] = pair[0] - damp * first
                pair[1] = pair[1] - damp * imaginary(first, second, lane, sites)
            for c in range(2):
                work_ref[2 * half + c, here, :] = pair[c]

    entry = send_ref[...]
    lane_count = entry.shape[1]
    half = index_ref.shape[2] // 2
    site = jnp.full(entry.shape, -1, jnp.int32)
    source = jnp.zeros(entry.shape, jnp.int32)
    for a in range(aux):
        for place in range(depth):
            hit = entry == a * depth + place
            site = jnp.where(hit, quanta_ref[place, a], site)
            source = jnp.where(hit, a, source)
    weight = jnp.zeros(entry.shape, f32)
    for a in range(aux):
        for place in range(depth):
            hit = (source == a) & (site == quanta_ref[place, a])
            weight = weight + jnp.where(hit, 1.0, 0.0)
    group = (lane_index(entry.shape) >= peers * capacity).astype(jnp.int32)
    usable = (entry >= 0) & (site >= 0) & (band - group >= 0)
    weight = jnp.where(usable, weight, 0.0)
    bath_of = spread(bath_row[...].astype(f32)) == col_ids.astype(f32)
    rate_of = jnp.sum(jnp.where(bath_of, vector_ref[1], 0.0), axis=1, keepdims=True)
    strength_of = jnp.sum(jnp.where(bath_of, vector_ref[2], 0.0), axis=1, keepdims=True)
    at_site = lax.broadcasted_iota(jnp.int32, (sites, lane_count), 0) == site
    rate = jnp.sum(jnp.where(at_site, rate_of, 0.0), axis=0, keepdims=True)
    strength = jnp.sum(jnp.where(at_site, strength_of, 0.0), axis=0, keepdims=True)
    lanes = pl.ds(0, lane_count)
    index_ref[2, :, lanes] = -weight * (strength * rate)
    index_ref[3, :, lanes] = weight * (2.0 * thermal * strength)
    for c in range(2):
        coef_ref[c] = spread(index_ref[2 + c, :, pl.ds(0, LANES)])[:lane_count, :]
    row_index = jnp.where(usable, source * sites + site, -1).astype(f32)
    column_index = jnp.where(usable, source * LANES + site, -1).astype(f32)
    for start in (0, half):
        index_ref[0, :, pl.ds(start, lane_count)] = row_index
        index_ref[1, :, pl.ds(start, lane_count)] = column_index
    for slab in range(2 * half // LANES):
        part = pl.ds(slab * LANES, LANES)
        turned = spread(index_ref[1, :, part])
        row_index = index_ref[0, :, part]
        for a in range(aux):
            at = (lane_index((LANES, LANES)) + a * LANES).astype(f32)
            column_ref[part, pl.ds(a * LANES, LANES)] = jnp.where(turned == at, 1.0, 0.0).astype(
                jnp.bfloat16
            )
            at = (lax.broadcasted_iota(jnp.int32, (sites, LANES), 0) + a * sites).astype(f32)
            place_ref[pl.ds(a * sites, sites), part] = jnp.where(row_index == at, 1.0, 0.0).astype(
                jnp.bfloat16
            )

    for g in range(2):
        for p in range(peers):
            for j in range(capacity):
                l = (g * peers + p) * capacity + j
                row = pl.ds(row_ref[g * peers + p, 0, j], 1)
                for c in range(4):
                    work_ref[c, row, :] = work_ref[c, row, :] + edge_ref[c, pl.ds(l, 1), :]
    for a in range(aux):
        here = pl.ds(a * sites, sites)
        for c in range(2):
            turned = work_ref[2 + c, pl.ds(a * sites, LANES), :].T[:sites, :]
            sum_ref[c, here, :] = work_ref[c, here, :] + turned


def lower_kernel(
    sizes,
    band_ref,
    returned_ref,
    sum_ref,
    column_ref,
    place_ref,
    coef_ref,
    out_hbm,
    work_ref,
    edge_ref,
    out_ref,
    sems,
):
    sites, aux, depth, peers, capacity, tiers = sizes
    tiles = 4 * sites // LANES
    pair_blocks = sites // (2 * SUB)
    chunk = aux * tiles * SUB
    slabs = capacity * FIELDS
    used = 2 * capacity * peers
    half = edge_ref.shape[1] // 2
    band = band_ref[0]
    lane = lane_index((peers, LANES))
    if used < half:
        for top in (used, half + used):
            edge_ref[:, pl.ds(top, half - used), :] = jnp.zeros(
                (4, half - used, LANES), jnp.float32
            )
    for g in range(2):
        target = jnp.maximum(band - g, 0)
        for j in range(capacity):
            start = target * (peers * slabs) + j * FIELDS
            parts = [
                returned_ref[pl.ds(start + f, peers, stride=slabs), :] for f in range(FIELDS)
            ]
            row_real, row_imag, col_real, col_imag = unmerge(parts, lane, sites)
            base = g * peers * capacity + j
            shared = coef_ref[0, pl.ds(base, peers, stride=capacity), :]
            turn = coef_ref[1, pl.ds(base, peers, stride=capacity), :]
            values = (
                shared * row_real + turn * row_imag,
                shared * row_imag - turn * row_real,
                shared * col_real - turn * col_imag,
                shared * col_imag + turn * col_real,
            )
            for f, value in enumerate(values):
                high = value.astype(jnp.bfloat16).astype(jnp.float32)
                edge_ref[f, pl.ds(base, peers, stride=capacity), :] = high
                edge_ref[f, pl.ds(half + base, peers, stride=capacity), :] = value - high
    dot = functools.partial(jnp.dot, preferred_element_type=jnp.float32)
    row_data = jnp.concatenate([edge_ref[0], edge_ref[1]], axis=1).astype(jnp.bfloat16)
    col_data = jnp.concatenate([edge_ref[2].T, edge_ref[3].T], axis=0).astype(jnp.bfloat16)
    for pair in range(aux // 2):
        columns = dot(col_data, column_ref[:, pl.ds(2 * pair * LANES, 2 * LANES)])
        for o in range(2):
            here = pl.ds((2 * pair + o) * sites, sites)
            placed = dot(place_ref[here, :], row_data)
            for c in range(2):
                work_ref[c, here, :] = (
                    sum_ref[c, here, :]
                    + placed[:, c * LANES : (c + 1) * LANES]
                    + columns[c * LANES : c * LANES + sites, o * LANES : (o + 1) * LANES]
                )
    lane = lane_index((SUB, LANES))
    copies = []
    for block in range(pair_blocks):
        for a in range(aux):
            base = a * sites + 2 * SUB * block
            even_real, even_imag, odd_real, odd_imag = (
                work_ref[c, pl.ds(base + o, SUB, stride=2), :] for o in (0, 1) for c in (0, 1)
            )
            turned_imag = pltpu.roll(even_imag, 96, 1)
            turned_real = pltpu.roll(odd_real, 64, 1)
            parts = (
                jnp.where(lane < 96, even_real, turned_imag),
                jnp.where(lane < 64, turned_imag, turned_real),
                jnp.where(lane < 32, turned_real, pltpu.roll(odd_imag, 32, 1)),
            )
            for u in range(tiles):
                start = a + aux * (tiles * SUB * block + u)
                out_ref[pl.ds(start, SUB, stride=aux * tiles), :] = parts[u]
        here = pl.ds(block * chunk, chunk)
        copies.append(pltpu.make_async_copy(out_ref.at[here, :], out_hbm.at[here, :], sems.at[block]))
        copies[-1].start()
    for copy in copies:
        copy.wait()


def on_device(
    section_state,
    coupling,
    site_energy,
    bath_rate,
    bath_strength,
    bath_of_site,
    quanta,
    send_list,
    dest_slot,
):
    sites = coupling.shape[0]
    aux, flat = section_state.shape
    depth = quanta.shape[1]
    lane_count = send_list.shape[1]
    peers = lax.axis_size("aux")
    tiers = lax.axis_size("tier")
    capacity = lane_count // (2 * peers)
    sizes = (sites, aux, depth, peers, capacity, tiers)
    rows = aux * sites
    padded = rows + LANES - sites
    slabs = capacity * FIELDS
    chunks = flat // LANES
    half = -(-lane_count // 64) * 64
    f32 = jnp.float32
    bf16 = jnp.bfloat16
    band = lax.axis_index("tier").reshape(1)
    tiled = section_state.reshape(aux, chunks, LANES).transpose(1, 0, 2).reshape(-1, LANES)
    turned_quanta = quanta.T
    bath_row = bath_of_site.reshape(1, -1)
    rate_row = bath_rate.reshape(1, -1)
    strength_row = bath_strength.reshape(1, -1)
    pair_blocks = sites // (2 * SUB)

    def call(kernel, name, inputs, outs, scratch):
        spaces = [space for space, _ in inputs]
        values = [
            value if space is SMEM else pltpu.with_memory_space_constraint(value, space)
            for space, value in inputs
        ]
        return pl.pallas_call(
            functools.partial(kernel, sizes),
            out_shape=[space(shape, dtype) for space, shape, dtype in outs],
            in_specs=[spec(space) for space in spaces],
            out_specs=[spec(space) for space, _, _ in outs],
            scratch_shapes=scratch,
            name=name,
            compiler_params=pltpu.CompilerParams(vmem_limit_bytes=24 * 1024 * 1024),
        )(*values)

    HBM = pltpu.HBM
    dma = pltpu.SemaphoreType.DMA
    i32 = jnp.int32
    store_shape = (FIELDS, padded, LANES)
    reply_shape = (tiers * peers, 1, slabs * LANES)
    payload_shape = (tiers * peers, 1, (slabs + 1) * LANES)
    flat_shape = (aux * chunks, LANES)
    row_scratch = VMEM((2 * peers, 1, LANES), i32)
    trade = functools.partial(
        lax.all_to_all, axis_name=("tier", "aux"), split_axis=0, concat_axis=0, tiled=True
    )
    store, payload = call(
        pack_kernel,
        "pack",
        [(SMEM, band), (HBM, send_list), (HBM, turned_quanta), (HBM, dest_slot), (HBM, tiled)],
        [(VMEM, store_shape, f32), (VMEM, payload_shape, f32)],
        [
            VMEM(flat_shape, f32),
            VMEM(send_list.shape, i32),
            SMEM(turned_quanta.shape, i32),
            VMEM(dest_slot.shape, i32),
            VMEM((3, 1, LANES), i32),
            SMEM((lane_count,), i32),
            dma((pair_blocks,)),
            dma((3,)),
        ],
    )
    arrived = trade(payload).reshape(-1, LANES)
    (reply,) = call(
        answer_kernel,
        "answer",
        [(SMEM, band), (VMEM, arrived), (VMEM, store)],
        [(HBM, reply_shape, f32)],
        [VMEM((2, peers) + reply_shape[1:], f32), row_scratch, dma((2,))],
    )
    returned = trade(reply)
    total, columns, places, coefs = call(
        middle_kernel,
        "middle",
        [
            (SMEM, band),
            (HBM, send_list),
            (HBM, turned_quanta),
            (HBM, bath_row),
            (HBM, rate_row),
            (HBM, strength_row),
            (HBM, coupling),
            (HBM, site_energy.reshape(1, -1)),
            (VMEM, arrived),
            (VMEM, store),
        ],
        [
            (VMEM, (2, rows, LANES), f32),
            (VMEM, (2 * half, aux * LANES), bf16),
            (VMEM, (rows, 2 * half), bf16),
            (VMEM, (2, lane_count, LANES), f32),
        ],
        [
            VMEM((4, padded, LANES), f32),
            VMEM((2, 2 * LANES, 2 * LANES), f32),
            VMEM((4, lane_count, LANES), f32),
            row_scratch,
            VMEM(coupling.shape, f32),
            VMEM((3, 1, sites), f32),
            VMEM(send_list.shape, i32),
            VMEM(bath_row.shape, i32),
            SMEM(turned_quanta.shape, i32),
            SMEM(bath_row.shape, i32),
            SMEM(rate_row.shape, f32),
            VMEM((4, 1, 2 * half), f32),
            dma((9,)),
        ],
    )
    (out,) = call(
        lower_kernel,
        "lower",
        [
            (SMEM, band),
            (VMEM, returned.reshape(-1, LANES)),
            (VMEM, total),
            (VMEM, columns),
            (VMEM, places),
            (VMEM, coefs),
        ],
        [(HBM, flat_shape, f32)],
        [
            VMEM((2, rows, LANES), f32),
            VMEM((4, 2 * half, LANES), f32),
            VMEM(flat_shape, f32),
            dma((pair_blocks,)),
        ],
    )
    return out.reshape(chunks, aux, LANES).transpose(1, 0, 2).reshape(aux, flat)


def solution(mesh):
    return jax.shard_map(
        on_device,
        mesh=mesh,
        in_specs=(
            P(("tier", "aux"), None),
            P(),
            P(),
            P(),
            P(),
            P(),
            P(("tier", "aux"), None),
            P(("tier", "aux"), None),
            P(("tier", "aux"), None),
        ),
        out_specs=P(("tier", "aux"), None),
        check_vma=False,
    )
```

```python
import functools

import jax
import jax.numpy as jnp
from jax import lax
from jax.experimental import pallas as pl
from jax.experimental.pallas import tpu as pltpu
from jax.sharding import PartitionSpec as P

thermal = 0.5
LANES = 128
SUB = 8
FIELDS = 3
TAG = 64
VMEM = pltpu.VMEM
SMEM = pltpu.SMEM


def spec(space):
    return pl.BlockSpec(memory_space=space)


def lane_index(shape):
    return lax.broadcasted_iota(jnp.int32, shape, 1)


def fetch(pairs, sems):
    copies = [
        pltpu.make_async_copy(source, target, sems.at[n]) for n, (source, target) in enumerate(pairs)
    ]
    for copy in copies:
        copy.start()
    return copies


def send_blocks(work_ref, wire_hbm, sems, band, step, tiers, peers):
    def block(g):
        at = jnp.clip(band + g * step, 0, tiers - 1) * peers
        return pltpu.make_async_copy(work_ref.at[g], wire_hbm.at[pl.ds(at, peers)], sems.at[g])

    return block


def imaginary(first, second, lane, sites):
    spare = LANES - sites
    return jnp.where(lane < spare, pltpu.roll(first, spare, 1), pltpu.roll(second, spare, 1))


def unmerge(parts, lane, sites):
    rest = 2 * sites - LANES
    first, second, third = parts
    kept = LANES - rest
    col_imag = jnp.where(
        lane < kept, pltpu.roll(second, kept, 1), pltpu.roll(third, 2 * LANES - sites - rest, 1)
    )
    return first, imaginary(first, second, lane, sites), third, col_imag


def pack_kernel(
    sizes,
    band_ref,
    send_hbm,
    quanta_hbm,
    slot_hbm,
    state_hbm,
    store_ref,
    payload_ref,
    state_ref,
    send_ref,
    quanta_ref,
    slot_ref,
    table_ref,
    row_ref,
    sems,
    table_sems,
):
    sites, aux, depth, peers, capacity, tiers = sizes
    tiles = 4 * sites // LANES
    pair_blocks = sites // (2 * SUB)
    chunk = aux * tiles * SUB
    rows = aux * sites
    tables = fetch(
        [(send_hbm, send_ref), (quanta_hbm, quanta_ref), (slot_hbm, slot_ref)], table_sems
    )
    copies = fetch(
        [(state_hbm, state_ref)],
        sems,
    )
    lane = lane_index((SUB, LANES))
    rest = 2 * sites - LANES
    store_ref[:, pl.ds(rows, LANES - sites), :] = jnp.zeros(
        (FIELDS, LANES - sites, LANES), jnp.float32
    )
    table_ref[...] = jnp.zeros_like(table_ref)
    for table in tables:
        table.wait()
    band = band_ref[0]
    row_lane = lane_index((1, LANES))
    entry = send_ref[...]
    lane_count = entry.shape[1]
    site = jnp.full(entry.shape, -1, jnp.int32)
    base = jnp.zeros(entry.shape, jnp.int32)
    for source in range(aux):
        for place in range(depth):
            here = entry == source * depth + place
            site = jnp.where(here, quanta_ref[place, source], site)
            base = jnp.where(here, source * sites, base)
    group = (lane_index(entry.shape) >= peers * capacity).astype(jnp.int32)
    usable = (entry >= 0) & (site >= 0) & (band - group >= 0)
    site = jnp.maximum(site, 0)
    table_ref[0, :, pl.ds(0, lane_count)] = base + site
    table_ref[1, :, pl.ds(0, lane_count)] = jnp.where(usable, slot_ref[...] * sites, rows)
    table_ref[2, :, pl.ds(0, lane_count)] = jnp.where(usable, site, 0)
    slot_tags, site_tags = table_ref[1], table_ref[2]
    for g in (1, 0):
        for q in range(peers):
            at = (g * peers + q) * capacity
            tags = jnp.where(
                row_lane < TAG,
                pltpu.roll(slot_tags, (LANES - at) % LANES, 1),
                pltpu.roll(site_tags, (LANES + TAG - at) % LANES, 1),
            )
            at_row = jnp.maximum(band - g, 0) * peers + q
            payload_ref[at_row, :, pl.ds(capacity * FIELDS * LANES, LANES)] = tags.astype(
                jnp.float32
            )
    for l in range(lane_count):
        row_ref[l] = table_ref[0, 0, l]
    for copy in copies:
        copy.wait()
    for block in range(pair_blocks):
        for a in range(aux):
            first, middle, last = (
                state_ref[pl.ds(a + aux * (tiles * SUB * block + u), SUB, stride=aux * tiles), :]
                for u in range(tiles)
            )
            middle_turned = pltpu.roll(middle, rest, 1)
            last_turned = pltpu.roll(last, rest, 1)
            base = a * sites + 2 * SUB * block
            store_ref[0, pl.ds(base, SUB, stride=2), :] = first
            store_ref[1, pl.ds(base, SUB, stride=2), :] = middle
            store_ref[0, pl.ds(base + 1, SUB, stride=2), :] = jnp.where(
                lane < rest, middle_turned, last_turned
            )
            store_ref[1, pl.ds(base + 1, SUB, stride=2), :] = last_turned
    for a in range(aux):
        here = pl.ds(a * sites, sites)
        first = store_ref[0, here, :].T
        second = store_ref[1, here, :].T
        col_imag = jnp.concatenate([first[sites:, :], second[:rest, :]], axis=0)
        store_ref[2, here, pl.ds(0, sites)] = first[:sites, :]
        store_ref[1, here, pl.ds(rest, LANES - rest)] = col_imag[:, : LANES - rest]
        store_ref[2, here, pl.ds(sites, LANES - sites)] = col_imag[:, LANES - rest :]
    for g in (1, 0):
        for q in range(peers):
            at_row = jnp.maximum(band - g, 0) * peers + q
            for j in range(capacity):
                row = pl.ds(row_ref[(g * peers + q) * capacity + j], 1)
                for f in range(FIELDS):
                    payload_ref[at_row, :, pl.ds((j * FIELDS + f) * LANES, LANES)] = store_ref[
                        f, row, :
                    ]


def read_rows(sizes, band, arrived_ref, row_ref):
    sites, aux, depth, peers, capacity, tiers = sizes
    slabs = capacity * FIELDS + 1
    for g in range(2):
        origin = jnp.minimum(band + g, tiers - 1) * peers
        for p in range(peers):
            tags = arrived_ref[pl.ds((origin + p) * slabs + slabs - 1, 1), :]
            total = (tags + pltpu.roll(tags, TAG, 1)).astype(jnp.int32)
            row_ref[g * peers + p] = jnp.where(band + g < tiers, total, aux * sites)


def answer_kernel(sizes, band_ref, arrived_ref, store_ref, reply_hbm, reply_ref, row_ref, wire_sems):
    sites, aux, depth, peers, capacity, tiers = sizes
    band = band_ref[0]
    block = send_blocks(reply_ref, reply_hbm, wire_sems, band, 1, tiers, peers)
    read_rows(sizes, band, arrived_ref, row_ref)
    for g in (1, 0):
        for p in range(peers):
            for j in range(capacity):
                row = pl.ds(row_ref[g * peers + p, 0, j], 1)
                for f in range(FIELDS):
                    reply_ref[g, p, :, pl.ds((j * FIELDS + f) * LANES, LANES)] = store_ref[f, row, :]
        if g == 0:
            block(g).start()
        else:
            pl.when(band + g < tiers)(block(g).start)
    block(0).wait()
    pl.when(band + 1 < tiers)(block(1).wait)


def split(value):
    high = value.astype(jnp.bfloat16)
    low = (value - high.astype(jnp.float32)).astype(jnp.bfloat16)
    return high, low


def spread(row):
    return jnp.broadcast_to(row, (row.shape[1], row.shape[1])).T


def middle_kernel(
    sizes,
    band_ref,
    send_hbm,
    quanta_hbm,
    bath_hbm,
    rate_hbm,
    strength_hbm,
    coupling_hbm,
    energy_hbm,
    arrived_ref,
    store_ref,
    sum_ref,
    column_ref,
    place_ref,
    coef_ref,
    work_ref,
    matrix_ref,
    edge_ref,
    row_ref,
    coupling_ref,
    vector_ref,
    send_ref,
    bath_row,
    quanta_ref,
    bath_ref,
    rate_ref,
    index_ref,
    sems,
):
    sites, aux, depth, peers, capacity, tiers = sizes
    rows = aux * sites
    rest = 2 * sites - LANES
    f32 = jnp.float32
    band = band_ref[0]
    copies = fetch(
        [
            (coupling_hbm, coupling_ref),
            (energy_hbm, vector_ref.at[0]),
            (rate_hbm, vector_ref.at[1]),
            (strength_hbm, vector_ref.at[2]),
            (send_hbm, send_ref),
            (bath_hbm, bath_row),
            (quanta_hbm, quanta_ref),
            (bath_hbm, bath_ref),
            (rate_hbm, rate_ref),
        ],
        sems,
    )
    read_rows(sizes, band, arrived_ref, row_ref)
    lane = lane_index((peers, LANES))
    for g in range(2):
        origin = jnp.minimum(band + g, tiers - 1) * peers
        for j in range(capacity):
            slabs = capacity * FIELDS + 1
            parts = [
                arrived_ref[pl.ds(origin * slabs + j * FIELDS + f, peers, stride=slabs), :]
                for f in range(FIELDS)
            ]
            row_real, row_imag, col_real, col_imag = unmerge(parts, lane, sites)
            for f, value in enumerate((row_imag, -row_real, -col_imag, col_real)):
                edge_ref[f, pl.ds(g * peers * capacity + j, peers, stride=capacity), :] = value
    matrix_ref[...] = jnp.zeros_like(matrix_ref)
    index_ref[...] = jnp.full(index_ref.shape, -1.0, f32)
    work_ref[:, pl.ds(rows, LANES - sites), :] = jnp.zeros((4, LANES - sites, LANES), f32)
    for copy in copies:
        copy.wait()
    row_ids = lax.broadcasted_iota(jnp.int32, (sites, sites), 0)
    col_ids = lane_index((sites, sites))
    coupling = coupling_ref[...]
    hamilton = (coupling + coupling.T) * 0.5 + jnp.where(row_ids == col_ids, vector_ref[0], 0.0)
    real, imag = pl.ds(0, sites), pl.ds(LANES, sites)
    matrix_ref[0, real, imag] = hamilton
    matrix_ref[0, pl.ds(sites, sites), real] = -hamilton
    matrix_ref[1, pl.ds(LANES, sites), imag] = -hamilton
    matrix_ref[1, pl.ds(rest, LANES - rest), real] = hamilton[: LANES - rest, :]
    matrix_ref[1, pl.ds(LANES + sites, LANES - sites), real] = hamilton[LANES - rest :, :]
    dot = functools.partial(jnp.dot, preferred_element_type=f32)
    splits = [split(matrix_ref[half]) for half in range(2)]
    lane = lane_index((sites, LANES))
    for a in range(aux):
        damp = f32(0.0)
        for place in range(depth):
            site = quanta_ref[place, a]
            rate = rate_ref[0, bath_ref[0, jnp.maximum(site, 0)]]
            damp = damp + jnp.where(site >= 0, rate, 0.0)
        here = pl.ds(a * sites, sites)
        for half in range(2):
            high, low = splits[half]
            first, second = store_ref[half, here, :], store_ref[half + 1, here, :]
            both_high, both_low = split(jnp.concatenate([first, second], axis=1))
            product = dot(both_high, high) + (dot(both_low, high) + dot(both_high, low))
            pair = [product[:, :LANES], product[:, LANES:]]
            if half == 0:
                pair[0] = pair[0] - damp * first
                pair[1] = pair[1] - damp * imaginary(first, second, lane, sites)
            for c in range(2):
                work_ref[2 * half + c, here, :] = pair[c]

    entry = send_ref[...]
    lane_count = entry.shape[1]
    half = index_ref.shape[2] // 2
    site = jnp.full(entry.shape, -1, jnp.int32)
    source = jnp.zeros(entry.shape, jnp.int32)
    for a in range(aux):
        for place in range(depth):
            hit = entry == a * depth + place
            site = jnp.where(hit, quanta_ref[place, a], site)
            source = jnp.where(hit, a, source)
    weight = jnp.zeros(entry.shape, f32)
    for a in range(aux):
        for place in range(depth):
            hit = (source == a) & (site == quanta_ref[place, a])
            weight = weight + jnp.where(hit, 1.0, 0.0)
    group = (lane_index(entry.shape) >= peers * capacity).astype(jnp.int32)
    usable = (entry >= 0) & (site >= 0) & (band - group >= 0)
    weight = jnp.where(usable, weight, 0.0)
    bath_of = spread(bath_row[...].astype(f32)) == col_ids.astype(f32)
    rate_of = jnp.sum(jnp.where(bath_of, vector_ref[1], 0.0), axis=1, keepdims=True)
    strength_of = jnp.sum(jnp.where(bath_of, vector_ref[2], 0.0), axis=1, keepdims=True)
    at_site = lax.broadcasted_iota(jnp.int32, (sites, lane_count), 0) == site
    rate = jnp.sum(jnp.where(at_site, rate_of, 0.0), axis=0, keepdims=True)
    strength = jnp.sum(jnp.where(at_site, strength_of, 0.0), axis=0, keepdims=True)
    lanes = pl.ds(0, lane_count)
    index_ref[2, :, lanes] = -weight * (strength * rate)
    index_ref[3, :, lanes] = weight * (2.0 * thermal * strength)
    for c in range(2):
        coef_ref[c] = spread(index_ref[2 + c, :, pl.ds(0, LANES)])[:lane_count, :]
    row_index = jnp.where(usable, source * sites + site, -1).astype(f32)
    column_index = jnp.where(usable, source * LANES + site, -1).astype(f32)
    for start in (0, half):
        index_ref[0, :, pl.ds(start, lane_count)] = row_index
        index_ref[1, :, pl.ds(start, lane_count)] = column_index
    for slab in range(2 * half // LANES):
        part = pl.ds(slab * LANES, LANES)
        turned = spread(index_ref[1, :, part])
        row_index = index_ref[0, :, part]
        for a in range(aux):
            at = (lane_index((LANES, LANES)) + a * LANES).astype(f32)
            column_ref[part, pl.ds(a * LANES, LANES)] = jnp.where(turned == at, 1.0, 0.0).astype(
                jnp.bfloat16
            )
            at = (lax.broadcasted_iota(jnp.int32, (sites, LANES), 0) + a * sites).astype(f32)
            place_ref[pl.ds(a * sites, sites), part] = jnp.where(row_index == at, 1.0, 0.0).astype(
                jnp.bfloat16
            )

    for g in range(2):
        for p in range(peers):
            for j in range(capacity):
                l = (g * peers + p) * capacity + j
                row = pl.ds(row_ref[g * peers + p, 0, j], 1)
                for c in range(4):
                    work_ref[c, row, :] = work_ref[c, row, :] + edge_ref[c, pl.ds(l, 1), :]
    for a in range(aux):
        here = pl.ds(a * sites, sites)
        for c in range(2):
            turned = work_ref[2 + c, pl.ds(a * sites, LANES), :].T[:sites, :]
            sum_ref[c, here, :] = work_ref[c, here, :] + turned


def lower_kernel(
    sizes,
    band_ref,
    returned_ref,
    sum_ref,
    column_ref,
    place_ref,
    coef_ref,
    out_hbm,
    work_ref,
    edge_ref,
    out_ref,
    sems,
):
    sites, aux, depth, peers, capacity, tiers = sizes
    tiles = 4 * sites // LANES
    pair_blocks = sites // (2 * SUB)
    chunk = aux * tiles * SUB
    slabs = capacity * FIELDS
    used = 2 * capacity * peers
    half = edge_ref.shape[1] // 2
    band = band_ref[0]
    lane = lane_index((peers, LANES))
    if used < half:
        for top in (used, half + used):
            edge_ref[:, pl.ds(top, half - used), :] = jnp.zeros(
                (4, half - used, LANES), jnp.float32
            )
    for g in range(2):
        target = jnp.maximum(band - g, 0)
        for j in range(capacity):
            start = target * (peers * slabs) + j * FIELDS
            parts = [
                returned_ref[pl.ds(start + f, peers, stride=slabs), :] for f in range(FIELDS)
            ]
            row_real, row_imag, col_real, col_imag = unmerge(parts, lane, sites)
            base = g * peers * capacity + j
            shared = coef_ref[0, pl.ds(base, peers, stride=capacity), :]
            turn = coef_ref[1, pl.ds(base, peers, stride=capacity), :]
            values = (
                shared * row_real + turn * row_imag,
                shared * row_imag - turn * row_real,
                shared * col_real - turn * col_imag,
                shared * col_imag + turn * col_real,
            )
            for f, value in enumerate(values):
                high = value.astype(jnp.bfloat16).astype(jnp.float32)
                edge_ref[f, pl.ds(base, peers, stride=capacity), :] = high
                edge_ref[f, pl.ds(half + base, peers, stride=capacity), :] = value - high
    dot = functools.partial(jnp.dot, preferred_element_type=jnp.float32)
    row_data = jnp.concatenate([edge_ref[0], edge_ref[1]], axis=1).astype(jnp.bfloat16)
    col_data = jnp.concatenate([edge_ref[2].T, edge_ref[3].T], axis=0).astype(jnp.bfloat16)
    for pair in range(aux // 2):
        columns = dot(col_data, column_ref[:, pl.ds(2 * pair * LANES, 2 * LANES)])
        for o in range(2):
            here = pl.ds((2 * pair + o) * sites, sites)
            placed = dot(place_ref[here, :], row_data)
            for c in range(2):
                work_ref[c, here, :] = (
                    sum_ref[c, here, :]
                    + placed[:, c * LANES : (c + 1) * LANES]
                    + columns[c * LANES : c * LANES + sites, o * LANES : (o + 1) * LANES]
                )
    lane = lane_index((SUB, LANES))
    copies = []
    for block in range(pair_blocks):
        for a in range(aux):
            base = a * sites + 2 * SUB * block
            even_real, even_imag, odd_real, odd_imag = (
                work_ref[c, pl.ds(base + o, SUB, stride=2), :] for o in (0, 1) for c in (0, 1)
            )
            turned_imag = pltpu.roll(even_imag, 96, 1)
            turned_real = pltpu.roll(odd_real, 64, 1)
            parts = (
                jnp.where(lane < 96, even_real, turned_imag),
                jnp.where(lane < 64, turned_imag, turned_real),
                jnp.where(lane < 32, turned_real, pltpu.roll(odd_imag, 32, 1)),
            )
            for u in range(tiles):
                start = a + aux * (tiles * SUB * block + u)
                out_ref[pl.ds(start, SUB, stride=aux * tiles), :] = parts[u]
        here = pl.ds(block * chunk, chunk)
        copies.append(pltpu.make_async_copy(out_ref.at[here, :], out_hbm.at[here, :], sems.at[block]))
        copies[-1].start()
    for copy in copies:
        copy.wait()


def on_device(
    section_state,
    coupling,
    site_energy,
    bath_rate,
    bath_strength,
    bath_of_site,
    quanta,
    send_list,
    dest_slot,
):
    sites = coupling.shape[0]
    aux, flat = section_state.shape
    depth = quanta.shape[1]
    lane_count = send_list.shape[1]
    peers = lax.axis_size("aux")
    tiers = lax.axis_size("tier")
    capacity = lane_count // (2 * peers)
    sizes = (sites, aux, depth, peers, capacity, tiers)
    rows = aux * sites
    padded = rows + LANES - sites
    slabs = capacity * FIELDS
    chunks = flat // LANES
    half = -(-lane_count // 64) * 64
    f32 = jnp.float32
    bf16 = jnp.bfloat16
    band = lax.axis_index("tier").reshape(1)
    tiled = section_state.reshape(aux, chunks, LANES).transpose(1, 0, 2).reshape(-1, LANES)
    turned_quanta = quanta.T
    bath_row = bath_of_site.reshape(1, -1)
    rate_row = bath_rate.reshape(1, -1)
    strength_row = bath_strength.reshape(1, -1)
    pair_blocks = sites // (2 * SUB)

    def call(kernel, name, inputs, outs, scratch):
        spaces = [space for space, _ in inputs]
        values = [
            value if space is SMEM else pltpu.with_memory_space_constraint(value, space)
            for space, value in inputs
        ]
        return pl.pallas_call(
            functools.partial(kernel, sizes),
            out_shape=[space(shape, dtype) for space, shape, dtype in outs],
            in_specs=[spec(space) for space in spaces],
            out_specs=[spec(space) for space, _, _ in outs],
            scratch_shapes=scratch,
            name=name,
            compiler_params=pltpu.CompilerParams(vmem_limit_bytes=24 * 1024 * 1024),
        )(*values)

    HBM = pltpu.HBM
    dma = pltpu.SemaphoreType.DMA
    i32 = jnp.int32
    store_shape = (FIELDS, padded, LANES)
    reply_shape = (tiers * peers, 1, slabs * LANES)
    payload_shape = (tiers * peers, 1, (slabs + 1) * LANES)
    flat_shape = (aux * chunks, LANES)
    row_scratch = VMEM((2 * peers, 1, LANES), i32)
    trade = functools.partial(
        lax.all_to_all, axis_name=("tier", "aux"), split_axis=0, concat_axis=0, tiled=True
    )
    store, payload = call(
        pack_kernel,
        "pack",
        [(SMEM, band), (HBM, send_list), (HBM, turned_quanta), (HBM, dest_slot), (HBM, tiled)],
        [(VMEM, store_shape, f32), (VMEM, payload_shape, f32)],
        [
            VMEM(flat_shape, f32),
            VMEM(send_list.shape, i32),
            SMEM(turned_quanta.shape, i32),
            VMEM(dest_slot.shape, i32),
            VMEM((3, 1, LANES), i32),
            SMEM((lane_count,), i32),
            dma((pair_blocks,)),
            dma((3,)),
        ],
    )
    arrived = trade(payload).reshape(-1, LANES)
    (reply,) = call(
        answer_kernel,
        "answer",
        [(SMEM, band), (VMEM, arrived), (VMEM, store)],
        [(HBM, reply_shape, f32)],
        [VMEM((2, peers) + reply_shape[1:], f32), row_scratch, dma((2,))],
    )
    returned = trade(reply)
    total, columns, places, coefs = call(
        middle_kernel,
        "middle",
        [
            (SMEM, band),
            (HBM, send_list),
            (HBM, turned_quanta),
            (HBM, bath_row),
            (HBM, rate_row),
            (HBM, strength_row),
            (HBM, coupling),
            (HBM, site_energy.reshape(1, -1)),
            (VMEM, arrived),
            (VMEM, store),
        ],
        [
            (VMEM, (2, rows, LANES), f32),
            (VMEM, (2 * half, aux * LANES), bf16),
            (VMEM, (rows, 2 * half), bf16),
            (VMEM, (2, lane_count, LANES), f32),
        ],
        [
            VMEM((4, padded, LANES), f32),
            VMEM((2, 2 * LANES, 2 * LANES), f32),
            VMEM((4, lane_count, LANES), f32),
            row_scratch,
            VMEM(coupling.shape, f32),
            VMEM((3, 1, sites), f32),
            VMEM(send_list.shape, i32),
            VMEM(bath_row.shape, i32),
            SMEM(turned_quanta.shape, i32),
            SMEM(bath_row.shape, i32),
            SMEM(rate_row.shape, f32),
            VMEM((4, 1, 2 * half), f32),
            dma((9,)),
        ],
    )
    (out,) = call(
        lower_kernel,
        "lower",
        [
            (SMEM, band),
            (VMEM, returned.reshape(-1, LANES)),
            (VMEM, total),
            (VMEM, columns),
            (VMEM, places),
            (VMEM, coefs),
        ],
        [(HBM, flat_shape, f32)],
        [
            VMEM((2, rows, LANES), f32),
            VMEM((4, 2 * half, LANES), f32),
            VMEM(flat_shape, f32),
            dma((pair_blocks,)),
        ],
    )
    return out.reshape(chunks, aux, LANES).transpose(1, 0, 2).reshape(aux, flat)


def solution(mesh):
    return jax.shard_map(
        on_device,
        mesh=mesh,
        in_specs=(
            P(("tier", "aux"), None),
            P(),
            P(),
            P(),
            P(),
            P(),
            P(("tier", "aux"), None),
            P(("tier", "aux"), None),
            P(("tier", "aux"), None),
        ),
        out_specs=P(("tier", "aux"), None),
        check_vma=False,
    )
```

```python
import functools

import jax
import jax.numpy as jnp
from jax import lax
from jax.experimental import pallas as pl
from jax.experimental.pallas import tpu as pltpu
from jax.sharding import PartitionSpec as P

thermal = 0.5
LANES = 128
SUB = 8
FIELDS = 3
TAG = 64
VMEM = pltpu.VMEM
SMEM = pltpu.SMEM


def spec(space):
    return pl.BlockSpec(memory_space=space)


def lane_index(shape):
    return lax.broadcasted_iota(jnp.int32, shape, 1)


def fetch(pairs, sems):
    copies = [
        pltpu.make_async_copy(source, target, sems.at[n]) for n, (source, target) in enumerate(pairs)
    ]
    for copy in copies:
        copy.start()
    return copies


def send_blocks(work_ref, wire_hbm, sems, band, step, tiers, peers):
    def block(g):
        at = jnp.clip(band + g * step, 0, tiers - 1) * peers
        return pltpu.make_async_copy(work_ref.at[g], wire_hbm.at[pl.ds(at, peers)], sems.at[g])

    return block


def imaginary(first, second, lane, sites):
    spare = LANES - sites
    return jnp.where(lane < spare, pltpu.roll(first, spare, 1), pltpu.roll(second, spare, 1))


def unmerge(parts, lane, sites):
    first, second, third = parts
    kept = 2 * (LANES - sites)
    col_imag = jnp.where(lane < kept, pltpu.roll(second, kept, 1), pltpu.roll(third, kept, 1))
    return first, imaginary(first, second, lane, sites), pltpu.roll(third, sites, 1), col_imag


def pack_kernel(
    sizes,
    band_ref,
    send_hbm,
    quanta_hbm,
    slot_hbm,
    state_hbm,
    store_ref,
    payload_ref,
    state_ref,
    send_ref,
    quanta_ref,
    slot_ref,
    table_ref,
    row_ref,
    sems,
    table_sems,
):
    sites, aux, depth, peers, capacity, tiers = sizes
    tiles = 4 * sites // LANES
    pair_blocks = sites // (2 * SUB)
    chunk = aux * tiles * SUB
    rows = aux * sites
    tables = fetch(
        [(send_hbm, send_ref), (quanta_hbm, quanta_ref), (slot_hbm, slot_ref)], table_sems
    )
    copies = fetch(
        [(state_hbm, state_ref)],
        sems,
    )
    lane = lane_index((SUB, LANES))
    rest = 2 * sites - LANES
    store_ref[:, pl.ds(rows, LANES - sites), :] = jnp.zeros(
        (FIELDS, LANES - sites, LANES), jnp.float32
    )
    table_ref[...] = jnp.zeros_like(table_ref)
    for table in tables:
        table.wait()
    band = band_ref[0]
    row_lane = lane_index((1, LANES))
    entry = send_ref[...]
    lane_count = entry.shape[1]
    site = jnp.full(entry.shape, -1, jnp.int32)
    base = jnp.zeros(entry.shape, jnp.int32)
    for source in range(aux):
        for place in range(depth):
            here = entry == source * depth + place
            site = jnp.where(here, quanta_ref[place, source], site)
            base = jnp.where(here, source * sites, base)
    group = (lane_index(entry.shape) >= peers * capacity).astype(jnp.int32)
    usable = (entry >= 0) & (site >= 0) & (band - group >= 0)
    site = jnp.maximum(site, 0)
    table_ref[0, :, pl.ds(0, lane_count)] = base + site
    table_ref[1, :, pl.ds(0, lane_count)] = jnp.where(usable, slot_ref[...] * sites, rows)
    table_ref[2, :, pl.ds(0, lane_count)] = jnp.where(usable, site, 0)
    slot_tags, site_tags = table_ref[1], table_ref[2]
    for g in (1, 0):
        for q in range(peers):
            at = (g * peers + q) * capacity
            tags = jnp.where(
                row_lane < TAG,
                pltpu.roll(slot_tags, (LANES - at) % LANES, 1),
                pltpu.roll(site_tags, (LANES + TAG - at) % LANES, 1),
            )
            at_row = jnp.maximum(band - g, 0) * peers + q
            payload_ref[at_row, :, pl.ds(capacity * FIELDS * LANES, LANES)] = tags.astype(
                jnp.float32
            )
    for l in range(lane_count):
        row_ref[l] = table_ref[0, 0, l]
    for copy in copies:
        copy.wait()
    for block in range(pair_blocks):
        for a in range(aux):
            first, middle, last = (
                state_ref[pl.ds(a + aux * (tiles * SUB * block + u), SUB, stride=aux * tiles), :]
                for u in range(tiles)
            )
            middle_turned = pltpu.roll(middle, rest, 1)
            last_turned = pltpu.roll(last, rest, 1)
            base = a * sites + 2 * SUB * block
            store_ref[0, pl.ds(base, SUB, stride=2), :] = first
            store_ref[1, pl.ds(base, SUB, stride=2), :] = jnp.where(lane < rest, middle, first)
            store_ref[0, pl.ds(base + 1, SUB, stride=2), :] = jnp.where(
                lane < rest, middle_turned, last_turned
            )
            store_ref[1, pl.ds(base + 1, SUB, stride=2), :] = last_turned
    kept = LANES - rest
    tail = sites - kept
    wide = lane_index((sites, LANES))
    for a in range(aux):
        here = pl.ds(a * sites, sites)
        first, second = store_ref[0, here, :], store_ref[1, here, :]
        columns = jnp.concatenate([first[kept:, :], first], axis=0).T[:sites, :]
        turned = jnp.concatenate([second[kept:, :], second[kept:, :], second[:kept, :]], axis=0).T
        turned = jnp.concatenate([turned[LANES - tail :, :], turned[:rest, :]], axis=0)
        store_ref[1, here, :] = jnp.where(wide < rest, second, turned)
        store_ref[2, here, :] = jnp.where(wide < tail, turned, columns)
    for g in (1, 0):
        for q in range(peers):
            at_row = jnp.maximum(band - g, 0) * peers + q
            for j in range(capacity):
                row = pl.ds(row_ref[(g * peers + q) * capacity + j], 1)
                for f in range(FIELDS):
                    payload_ref[at_row, :, pl.ds((j * FIELDS + f) * LANES, LANES)] = store_ref[
                        f, row, :
                    ]


def read_rows(sizes, band, arrived_ref, row_ref):
    sites, aux, depth, peers, capacity, tiers = sizes
    slabs = capacity * FIELDS + 1
    for g in range(2):
        origin = jnp.minimum(band + g, tiers - 1) * peers
        for p in range(peers):
            tags = arrived_ref[pl.ds((origin + p) * slabs + slabs - 1, 1), :]
            total = (tags + pltpu.roll(tags, TAG, 1)).astype(jnp.int32)
            row_ref[g * peers + p] = jnp.where(band + g < tiers, total, aux * sites)


def answer_kernel(sizes, band_ref, arrived_ref, store_ref, reply_hbm, reply_ref, row_ref, wire_sems):
    sites, aux, depth, peers, capacity, tiers = sizes
    band = band_ref[0]
    block = send_blocks(reply_ref, reply_hbm, wire_sems, band, 1, tiers, peers)
    read_rows(sizes, band, arrived_ref, row_ref)
    for g in (1, 0):
        for p in range(peers):
            for j in range(capacity):
                row = pl.ds(row_ref[g * peers + p, 0, j], 1)
                for f in range(FIELDS):
                    reply_ref[g, p, :, pl.ds((j * FIELDS + f) * LANES, LANES)] = store_ref[f, row, :]
        if g == 0:
            block(g).start()
        else:
            pl.when(band + g < tiers)(block(g).start)
    block(0).wait()
    pl.when(band + 1 < tiers)(block(1).wait)


def split(value):
    high = value.astype(jnp.bfloat16)
    low = (value - high.astype(jnp.float32)).astype(jnp.bfloat16)
    return high, low


def spread(row):
    return jnp.broadcast_to(row, (row.shape[1], row.shape[1])).T


def middle_kernel(
    sizes,
    band_ref,
    send_hbm,
    quanta_hbm,
    bath_hbm,
    rate_hbm,
    strength_hbm,
    coupling_hbm,
    energy_hbm,
    arrived_ref,
    store_ref,
    sum_ref,
    column_ref,
    place_ref,
    coef_ref,
    work_ref,
    matrix_ref,
    edge_ref,
    row_ref,
    coupling_ref,
    vector_ref,
    send_ref,
    bath_row,
    quanta_ref,
    bath_ref,
    rate_ref,
    index_ref,
    sems,
):
    sites, aux, depth, peers, capacity, tiers = sizes
    rows = aux * sites
    rest = 2 * sites - LANES
    f32 = jnp.float32
    band = band_ref[0]
    copies = fetch(
        [
            (coupling_hbm, coupling_ref),
            (energy_hbm, vector_ref.at[0]),
            (rate_hbm, vector_ref.at[1]),
            (strength_hbm, vector_ref.at[2]),
            (send_hbm, send_ref),
            (bath_hbm, bath_row),
            (quanta_hbm, quanta_ref),
            (bath_hbm, bath_ref),
            (rate_hbm, rate_ref),
        ],
        sems,
    )
    read_rows(sizes, band, arrived_ref, row_ref)
    lane = lane_index((peers, LANES))
    for g in range(2):
        origin = jnp.minimum(band + g, tiers - 1) * peers
        for j in range(capacity):
            slabs = capacity * FIELDS + 1
            parts = [
                arrived_ref[pl.ds(origin * slabs + j * FIELDS + f, peers, stride=slabs), :]
                for f in range(FIELDS)
            ]
            row_real, row_imag, col_real, col_imag = unmerge(parts, lane, sites)
            for f, value in enumerate((row_imag, -row_real, -col_imag, col_real)):
                edge_ref[f, pl.ds(g * peers * capacity + j, peers, stride=capacity), :] = value
    matrix_ref[...] = jnp.zeros_like(matrix_ref)
    index_ref[...] = jnp.full(index_ref.shape, -1.0, f32)
    work_ref[:, pl.ds(rows, LANES - sites), :] = jnp.zeros((4, LANES - sites, LANES), f32)
    for copy in copies:
        copy.wait()
    row_ids = lax.broadcasted_iota(jnp.int32, (sites, sites), 0)
    col_ids = lane_index((sites, sites))
    coupling = coupling_ref[...]
    hamilton = (coupling + coupling.T) * 0.5 + jnp.where(row_ids == col_ids, vector_ref[0], 0.0)
    real, imag = pl.ds(0, sites), pl.ds(LANES, sites)
    matrix_ref[0, real, imag] = hamilton
    matrix_ref[0, pl.ds(sites, sites), real] = -hamilton
    matrix_ref[1, pl.ds(rest, sites), real] = hamilton
    matrix_ref[1, pl.ds(2 * LANES - sites, sites), imag] = -hamilton
    dot = functools.partial(jnp.dot, preferred_element_type=f32)
    splits = [split(matrix_ref[half]) for half in range(2)]
    lane = lane_index((sites, LANES))
    for a in range(aux):
        damp = f32(0.0)
        for place in range(depth):
            site = quanta_ref[place, a]
            rate = rate_ref[0, bath_ref[0, jnp.maximum(site, 0)]]
            damp = damp + jnp.where(site >= 0, rate, 0.0)
        here = pl.ds(a * sites, sites)
        for half in range(2):
            high, low = splits[half]
            first, second = store_ref[half, here, :], store_ref[half + 1, here, :]
            both_high, both_low = split(jnp.concatenate([first, second], axis=1))
            product = dot(both_high, high) + (dot(both_low, high) + dot(both_high, low))
            pair = [product[:, :LANES], product[:, LANES:]]
            if half == 0:
                pair[0] = pair[0] - damp * first
                pair[1] = pair[1] - damp * imaginary(first, second, lane, sites)
            for c in range(2):
                work_ref[2 * half + c, here, :] = pair[c]

    entry = send_ref[...]
    lane_count = entry.shape[1]
    half = index_ref.shape[2] // 2
    site = jnp.full(entry.shape, -1, jnp.int32)
    source = jnp.zeros(entry.shape, jnp.int32)
    for a in range(aux):
        for place in range(depth):
            hit = entry == a * depth + place
            site = jnp.where(hit, quanta_ref[place, a], site)
            source = jnp.where(hit, a, source)
    weight = jnp.zeros(entry.shape, f32)
    for a in range(aux):
        for place in range(depth):
            hit = (source == a) & (site == quanta_ref[place, a])
            weight = weight + jnp.where(hit, 1.0, 0.0)
    group = (lane_index(entry.shape) >= peers * capacity).astype(jnp.int32)
    usable = (entry >= 0) & (site >= 0) & (band - group >= 0)
    weight = jnp.where(usable, weight, 0.0)
    bath_of = spread(bath_row[...].astype(f32)) == col_ids.astype(f32)
    rate_of = jnp.sum(jnp.where(bath_of, vector_ref[1], 0.0), axis=1, keepdims=True)
    strength_of = jnp.sum(jnp.where(bath_of, vector_ref[2], 0.0), axis=1, keepdims=True)
    at_site = lax.broadcasted_iota(jnp.int32, (sites, lane_count), 0) == site
    rate = jnp.sum(jnp.where(at_site, rate_of, 0.0), axis=0, keepdims=True)
    strength = jnp.sum(jnp.where(at_site, strength_of, 0.0), axis=0, keepdims=True)
    lanes = pl.ds(0, lane_count)
    index_ref[2, :, lanes] = -weight * (strength * rate)
    index_ref[3, :, lanes] = weight * (2.0 * thermal * strength)
    for c in range(2):
        coef_ref[c] = spread(index_ref[2 + c, :, pl.ds(0, LANES)])[:lane_count, :]
    row_index = jnp.where(usable, source * sites + site, -1).astype(f32)
    column_index = jnp.where(usable, source * LANES + site, -1).astype(f32)
    for start in (0, half):
        index_ref[0, :, pl.ds(start, lane_count)] = row_index
        index_ref[1, :, pl.ds(start, lane_count)] = column_index
    for slab in range(2 * half // LANES):
        part = pl.ds(slab * LANES, LANES)
        turned = spread(index_ref[1, :, part])
        row_index = index_ref[0, :, part]
        for a in range(aux):
            at = (lane_index((LANES, LANES)) + a * LANES).astype(f32)
            column_ref[part, pl.ds(a * LANES, LANES)] = jnp.where(turned == at, 1.0, 0.0).astype(
                jnp.bfloat16
            )
            at = (lax.broadcasted_iota(jnp.int32, (sites, LANES), 0) + a * sites).astype(f32)
            place_ref[pl.ds(a * sites, sites), part] = jnp.where(row_index == at, 1.0, 0.0).astype(
                jnp.bfloat16
            )

    for g in range(2):
        for p in range(peers):
            for j in range(capacity):
                l = (g * peers + p) * capacity + j
                row = pl.ds(row_ref[g * peers + p, 0, j], 1)
                for c in range(4):
                    work_ref[c, row, :] = work_ref[c, row, :] + edge_ref[c, pl.ds(l, 1), :]
    for a in range(aux):
        here = pl.ds(a * sites, sites)
        for c in range(2):
            turned = work_ref[2 + c, pl.ds(a * sites, LANES), :].T[:sites, :]
            sum_ref[c, here, :] = work_ref[c, here, :] + turned


def lower_kernel(
    sizes,
    band_ref,
    returned_ref,
    sum_ref,
    column_ref,
    place_ref,
    coef_ref,
    out_hbm,
    work_ref,
    edge_ref,
    out_ref,
    sems,
):
    sites, aux, depth, peers, capacity, tiers = sizes
    tiles = 4 * sites // LANES
    pair_blocks = sites // (2 * SUB)
    chunk = aux * tiles * SUB
    slabs = capacity * FIELDS
    used = 2 * capacity * peers
    half = edge_ref.shape[1] // 2
    band = band_ref[0]
    lane = lane_index((peers, LANES))
    if used < half:
        for top in (used, half + used):
            edge_ref[:, pl.ds(top, half - used), :] = jnp.zeros(
                (4, half - used, LANES), jnp.float32
            )
    for g in range(2):
        target = jnp.maximum(band - g, 0)
        for j in range(capacity):
            start = target * (peers * slabs) + j * FIELDS
            parts = [
                returned_ref[pl.ds(start + f, peers, stride=slabs), :] for f in range(FIELDS)
            ]
            row_real, row_imag, col_real, col_imag = unmerge(parts, lane, sites)
            base = g * peers * capacity + j
            shared = coef_ref[0, pl.ds(base, peers, stride=capacity), :]
            turn = coef_ref[1, pl.ds(base, peers, stride=capacity), :]
            values = (
                shared * row_real + turn * row_imag,
                shared * row_imag - turn * row_real,
                shared * col_real - turn * col_imag,
                shared * col_imag + turn * col_real,
            )
            for f, value in enumerate(values):
                high = value.astype(jnp.bfloat16).astype(jnp.float32)
                edge_ref[f, pl.ds(base, peers, stride=capacity), :] = high
                edge_ref[f, pl.ds(half + base, peers, stride=capacity), :] = value - high
    dot = functools.partial(jnp.dot, preferred_element_type=jnp.float32)
    row_data = jnp.concatenate([edge_ref[0], edge_ref[1]], axis=1).astype(jnp.bfloat16)
    col_data = jnp.concatenate(
        [edge_ref[2].T[:sites, :], edge_ref[3].T[:sites, :]], axis=0
    ).astype(jnp.bfloat16)
    for a in range(aux):
        here = pl.ds(a * sites, sites)
        placed = dot(place_ref[here, :], row_data)
        for c in range(2):
            work_ref[c, here, :] = sum_ref[c, here, :] + placed[:, c * LANES : (c + 1) * LANES]
    for pair in range(aux // 2):
        columns = dot(col_data, column_ref[:, pl.ds(2 * pair * LANES, 2 * LANES)])
        for o in range(2):
            here = pl.ds((2 * pair + o) * sites, sites)
            for c in range(2):
                work_ref[c, here, :] = (
                    work_ref[c, here, :]
                    + columns[c * sites : (c + 1) * sites, o * LANES : (o + 1) * LANES]
                )
    lane = lane_index((SUB, LANES))
    copies = []
    for block in range(pair_blocks):
        for a in range(aux):
            base = a * sites + 2 * SUB * block
            even_real, even_imag, odd_real, odd_imag = (
                work_ref[c, pl.ds(base + o, SUB, stride=2), :] for o in (0, 1) for c in (0, 1)
            )
            turned_imag = pltpu.roll(even_imag, 96, 1)
            turned_real = pltpu.roll(odd_real, 64, 1)
            parts = (
                jnp.where(lane < 96, even_real, turned_imag),
                jnp.where(lane < 64, turned_imag, turned_real),
                jnp.where(lane < 32, turned_real, pltpu.roll(odd_imag, 32, 1)),
            )
            for u in range(tiles):
                start = a + aux * (tiles * SUB * block + u)
                out_ref[pl.ds(start, SUB, stride=aux * tiles), :] = parts[u]
        here = pl.ds(block * chunk, chunk)
        copies.append(pltpu.make_async_copy(out_ref.at[here, :], out_hbm.at[here, :], sems.at[block]))
        copies[-1].start()
    for copy in copies:
        copy.wait()


def on_device(
    section_state,
    coupling,
    site_energy,
    bath_rate,
    bath_strength,
    bath_of_site,
    quanta,
    send_list,
    dest_slot,
):
    sites = coupling.shape[0]
    aux, flat = section_state.shape
    depth = quanta.shape[1]
    lane_count = send_list.shape[1]
    peers = lax.axis_size("aux")
    tiers = lax.axis_size("tier")
    capacity = lane_count // (2 * peers)
    sizes = (sites, aux, depth, peers, capacity, tiers)
    rows = aux * sites
    padded = rows + LANES - sites
    slabs = capacity * FIELDS
    chunks = flat // LANES
    half = -(-lane_count // 64) * 64
    f32 = jnp.float32
    bf16 = jnp.bfloat16
    band = lax.axis_index("tier").reshape(1)
    tiled = section_state.reshape(aux, chunks, LANES).transpose(1, 0, 2).reshape(-1, LANES)
    turned_quanta = quanta.T
    bath_row = bath_of_site.reshape(1, -1)
    rate_row = bath_rate.reshape(1, -1)
    strength_row = bath_strength.reshape(1, -1)
    pair_blocks = sites // (2 * SUB)

    def call(kernel, name, inputs, outs, scratch):
        spaces = [space for space, _ in inputs]
        values = [
            value if space is SMEM else pltpu.with_memory_space_constraint(value, space)
            for space, value in inputs
        ]
        return pl.pallas_call(
            functools.partial(kernel, sizes),
            out_shape=[space(shape, dtype) for space, shape, dtype in outs],
            in_specs=[spec(space) for space in spaces],
            out_specs=[spec(space) for space, _, _ in outs],
            scratch_shapes=scratch,
            name=name,
            compiler_params=pltpu.CompilerParams(vmem_limit_bytes=24 * 1024 * 1024),
        )(*values)

    HBM = pltpu.HBM
    dma = pltpu.SemaphoreType.DMA
    i32 = jnp.int32
    store_shape = (FIELDS, padded, LANES)
    reply_shape = (tiers * peers, 1, slabs * LANES)
    payload_shape = (tiers * peers, 1, (slabs + 1) * LANES)
    flat_shape = (aux * chunks, LANES)
    row_scratch = VMEM((2 * peers, 1, LANES), i32)
    trade = functools.partial(
        lax.all_to_all, axis_name=("tier", "aux"), split_axis=0, concat_axis=0, tiled=True
    )
    store, payload = call(
        pack_kernel,
        "pack",
        [(SMEM, band), (HBM, send_list), (HBM, turned_quanta), (HBM, dest_slot), (HBM, tiled)],
        [(VMEM, store_shape, f32), (VMEM, payload_shape, f32)],
        [
            VMEM(flat_shape, f32),
            VMEM(send_list.shape, i32),
            SMEM(turned_quanta.shape, i32),
            VMEM(dest_slot.shape, i32),
            VMEM((3, 1, LANES), i32),
            SMEM((lane_count,), i32),
            dma((pair_blocks,)),
            dma((3,)),
        ],
    )
    arrived = trade(payload).reshape(-1, LANES)
    (reply,) = call(
        answer_kernel,
        "answer",
        [(SMEM, band), (VMEM, arrived), (VMEM, store)],
        [(HBM, reply_shape, f32)],
        [VMEM((2, peers) + reply_shape[1:], f32), row_scratch, dma((2,))],
    )
    returned = trade(reply)
    total, columns, places, coefs = call(
        middle_kernel,
        "middle",
        [
            (SMEM, band),
            (HBM, send_list),
            (HBM, turned_quanta),
            (HBM, bath_row),
            (HBM, rate_row),
            (HBM, strength_row),
            (HBM, coupling),
            (HBM, site_energy.reshape(1, -1)),
            (VMEM, arrived),
            (VMEM, store),
        ],
        [
            (VMEM, (2, rows, LANES), f32),
            (VMEM, (2 * half, aux * LANES), bf16),
            (VMEM, (rows, 2 * half), bf16),
            (VMEM, (2, lane_count, LANES), f32),
        ],
        [
            VMEM((4, padded, LANES), f32),
            VMEM((2, 2 * LANES, 2 * LANES), f32),
            VMEM((4, lane_count, LANES), f32),
            row_scratch,
            VMEM(coupling.shape, f32),
            VMEM((3, 1, sites), f32),
            VMEM(send_list.shape, i32),
            VMEM(bath_row.shape, i32),
            SMEM(turned_quanta.shape, i32),
            SMEM(bath_row.shape, i32),
            SMEM(rate_row.shape, f32),
            VMEM((4, 1, 2 * half), f32),
            dma((9,)),
        ],
    )
    (out,) = call(
        lower_kernel,
        "lower",
        [
            (SMEM, band),
            (VMEM, returned.reshape(-1, LANES)),
            (VMEM, total),
            (VMEM, columns),
            (VMEM, places),
            (VMEM, coefs),
        ],
        [(HBM, flat_shape, f32)],
        [
            VMEM((2, rows, LANES), f32),
            VMEM((4, 2 * half, LANES), f32),
            VMEM(flat_shape, f32),
            dma((pair_blocks,)),
        ],
    )
    return out.reshape(chunks, aux, LANES).transpose(1, 0, 2).reshape(aux, flat)


def solution(mesh):
    return jax.shard_map(
        on_device,
        mesh=mesh,
        in_specs=(
            P(("tier", "aux"), None),
            P(),
            P(),
            P(),
            P(),
            P(),
            P(("tier", "aux"), None),
            P(("tier", "aux"), None),
            P(("tier", "aux"), None),
        ),
        out_specs=P(("tier", "aux"), None),
        check_vma=False,
    )
```

```python
import functools

import jax
import jax.numpy as jnp
from jax import lax
from jax.experimental import pallas as pl
from jax.experimental.pallas import tpu as pltpu
from jax.sharding import PartitionSpec as P

thermal = 0.5
LANES = 128
SUB = 8
FIELDS = 3
TAG = 64
VMEM = pltpu.VMEM
SMEM = pltpu.SMEM


def spec(space):
    return pl.BlockSpec(memory_space=space)


def lane_index(shape):
    return lax.broadcasted_iota(jnp.int32, shape, 1)


def fetch(pairs, sems):
    copies = [
        pltpu.make_async_copy(source, target, sems.at[n]) for n, (source, target) in enumerate(pairs)
    ]
    for copy in copies:
        copy.start()
    return copies


def send_blocks(work_ref, wire_hbm, sems, band, step, tiers, peers):
    def block(g):
        at = jnp.clip(band + g * step, 0, tiers - 1) * peers
        return pltpu.make_async_copy(work_ref.at[g], wire_hbm.at[pl.ds(at, peers)], sems.at[g])

    return block


def imaginary(first, second, lane, sites):
    spare = LANES - sites
    return jnp.where(lane < spare, pltpu.roll(first, spare, 1), pltpu.roll(second, spare, 1))


def unmerge(parts, lane, sites):
    first, second, third = parts
    kept = 2 * (LANES - sites)
    col_imag = jnp.where(lane < kept, pltpu.roll(second, kept, 1), pltpu.roll(third, kept, 1))
    return first, imaginary(first, second, lane, sites), pltpu.roll(third, sites, 1), col_imag


def pack_kernel(
    sizes,
    band_ref,
    send_hbm,
    quanta_hbm,
    slot_hbm,
    state_hbm,
    store_ref,
    payload_ref,
    state_ref,
    send_ref,
    quanta_ref,
    slot_ref,
    table_ref,
    row_ref,
    sems,
    table_sems,
):
    sites, aux, depth, peers, capacity, tiers = sizes
    tiles = 4 * sites // LANES
    pair_blocks = sites // (2 * SUB)
    chunk = aux * tiles * SUB
    rows = aux * sites
    tables = fetch(
        [(send_hbm, send_ref), (quanta_hbm, quanta_ref), (slot_hbm, slot_ref)], table_sems
    )
    copies = fetch(
        [(state_hbm, state_ref)],
        sems,
    )
    lane = lane_index((SUB, LANES))
    rest = 2 * sites - LANES
    store_ref[:, pl.ds(rows, LANES - sites), :] = jnp.zeros(
        (FIELDS, LANES - sites, LANES), jnp.float32
    )
    table_ref[...] = jnp.zeros_like(table_ref)
    for table in tables:
        table.wait()
    band = band_ref[0]
    row_lane = lane_index((1, LANES))
    entry = send_ref[...]
    lane_count = entry.shape[1]
    site = jnp.full(entry.shape, -1, jnp.int32)
    base = jnp.zeros(entry.shape, jnp.int32)
    for source in range(aux):
        for place in range(depth):
            here = entry == source * depth + place
            site = jnp.where(here, quanta_ref[place, source], site)
            base = jnp.where(here, source * sites, base)
    group = (lane_index(entry.shape) >= peers * capacity).astype(jnp.int32)
    usable = (entry >= 0) & (site >= 0) & (band - group >= 0)
    site = jnp.maximum(site, 0)
    table_ref[0, :, pl.ds(0, lane_count)] = base + site
    table_ref[1, :, pl.ds(0, lane_count)] = jnp.where(usable, slot_ref[...] * sites, rows)
    table_ref[2, :, pl.ds(0, lane_count)] = jnp.where(usable, site, 0)
    slot_tags, site_tags = table_ref[1], table_ref[2]
    for g in (1, 0):
        for q in range(peers):
            at = (g * peers + q) * capacity
            tags = jnp.where(
                row_lane < TAG,
                pltpu.roll(slot_tags, (LANES - at) % LANES, 1),
                pltpu.roll(site_tags, (LANES + TAG - at) % LANES, 1),
            )
            at_row = jnp.maximum(band - g, 0) * peers + q
            payload_ref[at_row, :, pl.ds(capacity * FIELDS * LANES, LANES)] = tags.astype(
                jnp.float32
            )
    for l in range(lane_count):
        row_ref[l] = table_ref[0, 0, l]
    for copy in copies:
        copy.wait()
    for block in range(pair_blocks):
        for a in range(aux):
            first, middle, last = (
                state_ref[pl.ds(a + aux * (tiles * SUB * block + u), SUB, stride=aux * tiles), :]
                for u in range(tiles)
            )
            middle_turned = pltpu.roll(middle, rest, 1)
            last_turned = pltpu.roll(last, rest, 1)
            base = a * sites + 2 * SUB * block
            store_ref[0, pl.ds(base, SUB, stride=2), :] = first
            store_ref[1, pl.ds(base, SUB, stride=2), :] = jnp.where(lane < rest, middle, first)
            store_ref[0, pl.ds(base + 1, SUB, stride=2), :] = jnp.where(
                lane < rest, middle_turned, last_turned
            )
            store_ref[1, pl.ds(base + 1, SUB, stride=2), :] = last_turned
    kept = LANES - rest
    tail = sites - kept
    wide = lane_index((sites, LANES))
    for a in range(aux):
        here = pl.ds(a * sites, sites)
        first, second = store_ref[0, here, :], store_ref[1, here, :]
        columns = jnp.concatenate([first[kept:, :], first], axis=0).T[:sites, :]
        turned = jnp.concatenate([second[kept:, :], second[kept:, :], second[:kept, :]], axis=0).T
        turned = jnp.concatenate([turned[LANES - tail :, :], turned[:rest, :]], axis=0)
        store_ref[1, here, :] = jnp.where(wide < rest, second, turned)
        store_ref[2, here, :] = jnp.where(wide < tail, turned, columns)
    for g in (1, 0):
        for q in range(peers):
            at_row = jnp.maximum(band - g, 0) * peers + q
            for j in range(capacity):
                row = pl.ds(row_ref[(g * peers + q) * capacity + j], 1)
                for f in range(FIELDS):
                    payload_ref[at_row, :, pl.ds((j * FIELDS + f) * LANES, LANES)] = store_ref[
                        f, row, :
                    ]


def read_rows(sizes, band, arrived_ref, row_ref):
    sites, aux, depth, peers, capacity, tiers = sizes
    slabs = capacity * FIELDS + 1
    for g in range(2):
        origin = jnp.minimum(band + g, tiers - 1) * peers
        for p in range(peers):
            tags = arrived_ref[pl.ds((origin + p) * slabs + slabs - 1, 1), :]
            total = (tags + pltpu.roll(tags, TAG, 1)).astype(jnp.int32)
            row_ref[g * peers + p] = jnp.where(band + g < tiers, total, aux * sites)


def answer_kernel(sizes, band_ref, arrived_ref, store_ref, reply_hbm, reply_ref, row_ref, wire_sems):
    sites, aux, depth, peers, capacity, tiers = sizes
    band = band_ref[0]
    block = send_blocks(reply_ref, reply_hbm, wire_sems, band, 1, tiers, peers)
    read_rows(sizes, band, arrived_ref, row_ref)
    for g in (1, 0):
        for p in range(peers):
            for j in range(capacity):
                row = pl.ds(row_ref[g * peers + p, 0, j], 1)
                for f in range(FIELDS):
                    reply_ref[g, p, :, pl.ds((j * FIELDS + f) * LANES, LANES)] = store_ref[f, row, :]
        if g == 0:
            block(g).start()
        else:
            pl.when(band + g < tiers)(block(g).start)
    block(0).wait()
    pl.when(band + 1 < tiers)(block(1).wait)


def split(value):
    high = value.astype(jnp.bfloat16)
    low = (value - high.astype(jnp.float32)).astype(jnp.bfloat16)
    return high, low


def column_tiles(sites):
    spots = []
    for field in range(4):
        start = field * sites
        first, last = start // LANES, (start + sites - 1) // LANES
        spots += [(start, tile) for tile in range(first, last + 1)]
    return spots


def spread(row):
    return jnp.broadcast_to(row, (row.shape[1], row.shape[1])).T


def middle_kernel(
    sizes,
    band_ref,
    send_hbm,
    quanta_hbm,
    bath_hbm,
    rate_hbm,
    strength_hbm,
    coupling_hbm,
    energy_hbm,
    arrived_ref,
    store_ref,
    sum_ref,
    column_ref,
    place_ref,
    coef_ref,
    mask_ref,
    work_ref,
    matrix_ref,
    edge_ref,
    row_ref,
    coupling_ref,
    vector_ref,
    send_ref,
    bath_row,
    quanta_ref,
    bath_ref,
    rate_ref,
    index_ref,
    sems,
):
    sites, aux, depth, peers, capacity, tiers = sizes
    rows = aux * sites
    rest = 2 * sites - LANES
    f32 = jnp.float32
    band = band_ref[0]
    copies = fetch(
        [
            (coupling_hbm, coupling_ref),
            (energy_hbm, vector_ref.at[0]),
            (rate_hbm, vector_ref.at[1]),
            (strength_hbm, vector_ref.at[2]),
            (send_hbm, send_ref),
            (bath_hbm, bath_row),
            (quanta_hbm, quanta_ref),
            (bath_hbm, bath_ref),
            (rate_hbm, rate_ref),
        ],
        sems,
    )
    read_rows(sizes, band, arrived_ref, row_ref)
    lane = lane_index((peers, LANES))
    for g in range(2):
        origin = jnp.minimum(band + g, tiers - 1) * peers
        for j in range(capacity):
            slabs = capacity * FIELDS + 1
            parts = [
                arrived_ref[pl.ds(origin * slabs + j * FIELDS + f, peers, stride=slabs), :]
                for f in range(FIELDS)
            ]
            row_real, row_imag, col_real, col_imag = unmerge(parts, lane, sites)
            for f, value in enumerate((row_imag, -row_real, -col_imag, col_real)):
                edge_ref[f, pl.ds(g * peers * capacity + j, peers, stride=capacity), :] = value
    matrix_ref[...] = jnp.zeros_like(matrix_ref)
    index_ref[...] = jnp.full(index_ref.shape, -1.0, f32)
    work_ref[:, pl.ds(rows, LANES - sites), :] = jnp.zeros((4, LANES - sites, LANES), f32)
    for copy in copies:
        copy.wait()
    row_ids = lax.broadcasted_iota(jnp.int32, (sites, sites), 0)
    col_ids = lane_index((sites, sites))
    coupling = coupling_ref[...]
    hamilton = (coupling + coupling.T) * 0.5 + jnp.where(row_ids == col_ids, vector_ref[0], 0.0)
    real, imag = pl.ds(0, sites), pl.ds(LANES, sites)
    matrix_ref[0, real, imag] = hamilton
    matrix_ref[0, pl.ds(sites, sites), real] = -hamilton
    matrix_ref[1, pl.ds(rest, sites), real] = hamilton
    matrix_ref[1, pl.ds(2 * LANES - sites, sites), imag] = -hamilton
    dot = functools.partial(jnp.dot, preferred_element_type=f32)
    splits = [split(matrix_ref[half]) for half in range(2)]
    lane = lane_index((sites, LANES))
    for a in range(aux):
        damp = f32(0.0)
        for place in range(depth):
            site = quanta_ref[place, a]
            rate = rate_ref[0, bath_ref[0, jnp.maximum(site, 0)]]
            damp = damp + jnp.where(site >= 0, rate, 0.0)
        here = pl.ds(a * sites, sites)
        for half in range(2):
            high, low = splits[half]
            first, second = store_ref[half, here, :], store_ref[half + 1, here, :]
            both_high, both_low = split(jnp.concatenate([first, second], axis=1))
            product = dot(both_high, high) + (dot(both_low, high) + dot(both_high, low))
            pair = [product[:, :LANES], product[:, LANES:]]
            if half == 0:
                pair[0] = pair[0] - damp * first
                pair[1] = pair[1] - damp * imaginary(first, second, lane, sites)
            for c in range(2):
                work_ref[2 * half + c, here, :] = pair[c]

    entry = send_ref[...]
    lane_count = entry.shape[1]
    half = index_ref.shape[2] // 2
    site = jnp.full(entry.shape, -1, jnp.int32)
    source = jnp.zeros(entry.shape, jnp.int32)
    for a in range(aux):
        for place in range(depth):
            hit = entry == a * depth + place
            site = jnp.where(hit, quanta_ref[place, a], site)
            source = jnp.where(hit, a, source)
    weight = jnp.zeros(entry.shape, f32)
    for a in range(aux):
        for place in range(depth):
            hit = (source == a) & (site == quanta_ref[place, a])
            weight = weight + jnp.where(hit, 1.0, 0.0)
    group = (lane_index(entry.shape) >= peers * capacity).astype(jnp.int32)
    usable = (entry >= 0) & (site >= 0) & (band - group >= 0)
    weight = jnp.where(usable, weight, 0.0)
    bath_of = spread(bath_row[...].astype(f32)) == col_ids.astype(f32)
    rate_of = jnp.sum(jnp.where(bath_of, vector_ref[1], 0.0), axis=1, keepdims=True)
    strength_of = jnp.sum(jnp.where(bath_of, vector_ref[2], 0.0), axis=1, keepdims=True)
    at_site = lax.broadcasted_iota(jnp.int32, (sites, lane_count), 0) == site
    rate = jnp.sum(jnp.where(at_site, rate_of, 0.0), axis=0, keepdims=True)
    strength = jnp.sum(jnp.where(at_site, strength_of, 0.0), axis=0, keepdims=True)
    lanes = pl.ds(0, lane_count)
    index_ref[3, :, lanes] = -weight * (strength * rate)
    index_ref[4, :, lanes] = weight * (2.0 * thermal * strength)
    for c in range(2):
        coef_ref[c] = spread(index_ref[3 + c, :, pl.ds(0, LANES)])[:lane_count, :]
    rows_of = (
        jnp.where(usable, source * sites + site, -1),
        jnp.where(usable, site, -2 * LANES),
        jnp.where(usable, source, -1),
    )
    for start in (0, half):
        for c in range(3):
            index_ref[c, :, pl.ds(start, lane_count)] = rows_of[c].astype(f32)
    tiles = 4 * sites // LANES
    pairs = sites // 2
    for slab in range(2 * half // LANES):
        part = pl.ds(slab * LANES, LANES)
        turned = spread(index_ref[1, :, part])
        here = lane_index((LANES, LANES))
        for n, (offset, tile) in enumerate(column_tiles(sites)):
            hot = turned == (here + (tile * LANES - offset)).astype(f32)
            column_ref[part, pl.ds(n * LANES, LANES)] = jnp.where(hot, 1.0, 0.0).astype(jnp.bfloat16)
        at_aux = lax.broadcasted_iota(jnp.int32, (aux, LANES), 0).astype(f32)
        mask_ref[:, part] = jnp.where(index_ref[2, :, part] == at_aux, 1.0, 0.0)
        for o in range(2):
            shape = (pairs, aux, LANES)
            at = 2 * lax.broadcasted_iota(jnp.int32, shape, 0) + o
            at = at + sites * lax.broadcasted_iota(jnp.int32, shape, 1)
            hot = index_ref[0, :, part] == at.reshape(pairs * aux, LANES).astype(f32)
            place_ref[o, :, part] = jnp.where(hot, 1.0, 0.0).astype(jnp.bfloat16)

    for g in range(2):
        for p in range(peers):
            for j in range(capacity):
                l = (g * peers + p) * capacity + j
                row = pl.ds(row_ref[g * peers + p, 0, j], 1)
                for c in range(4):
                    work_ref[c, row, :] = work_ref[c, row, :] + edge_ref[c, pl.ds(l, 1), :]
    for a in range(aux):
        here = pl.ds(a * sites, sites)
        for c in range(2):
            turned = work_ref[2 + c, pl.ds(a * sites, LANES), :].T[:sites, :]
            work_ref[c, here, :] = work_ref[c, here, :] + turned
    pair_blocks = sites // (2 * SUB)
    lane = lane_index((SUB, LANES))
    for block in range(pair_blocks):
        for a in range(aux):
            base = a * sites + 2 * SUB * block
            even_real, even_imag, odd_real, odd_imag = (
                work_ref[c, pl.ds(base + o, SUB, stride=2), :] for o in (0, 1) for c in (0, 1)
            )
            turned_imag = pltpu.roll(even_imag, 96, 1)
            turned_real = pltpu.roll(odd_real, 64, 1)
            parts = (
                jnp.where(lane < 96, even_real, turned_imag),
                jnp.where(lane < 64, turned_imag, turned_real),
                jnp.where(lane < 32, turned_real, pltpu.roll(odd_imag, 32, 1)),
            )
            for u in range(tiles):
                start = a + aux * (tiles * SUB * block + u)
                sum_ref[pl.ds(start, SUB, stride=aux * tiles), :] = parts[u]


def lower_kernel(
    sizes,
    band_ref,
    returned_ref,
    sum_ref,
    column_ref,
    place_ref,
    coef_ref,
    mask_ref,
    out_hbm,
    edge_ref,
    turned_ref,
    left_ref,
    out_ref,
    sems,
):
    sites, aux, depth, peers, capacity, tiers = sizes
    tiles = 4 * sites // LANES
    pairs = sites // 2
    slabs = capacity * FIELDS
    used = 2 * capacity * peers
    half = edge_ref.shape[1] // 2
    rest = 2 * sites - LANES
    bf16 = jnp.bfloat16
    band = band_ref[0]
    lane = lane_index((peers, LANES))
    if used < half:
        for top in (used, half + used):
            edge_ref[:, pl.ds(top, half - used), :] = jnp.zeros(
                (6, half - used, LANES), jnp.float32
            )
    for g in range(2):
        target = jnp.maximum(band - g, 0)
        for j in range(capacity):
            start = target * (peers * slabs) + j * FIELDS
            parts = [
                returned_ref[pl.ds(start + f, peers, stride=slabs), :] for f in range(FIELDS)
            ]
            row_real, row_imag, col_real, col_imag = unmerge(parts, lane, sites)
            base = g * peers * capacity + j
            shared = coef_ref[0, pl.ds(base, peers, stride=capacity), :]
            turn = coef_ref[1, pl.ds(base, peers, stride=capacity), :]
            real = shared * row_real + turn * row_imag
            imag = pltpu.roll(shared * row_imag - turn * row_real, sites, 1)
            head = jnp.where(lane < sites, real, imag)
            head_turned = pltpu.roll(head, rest, 1)
            values = (
                head,
                jnp.where(lane < rest, imag, 0.0),
                jnp.where(lane < rest, 0.0, head_turned),
                jnp.where(lane < rest, head_turned, pltpu.roll(imag, rest, 1)),
                shared * col_real - turn * col_imag,
                shared * col_imag + turn * col_real,
            )
            for f, value in enumerate(values):
                high = value.astype(bf16).astype(jnp.float32)
                edge_ref[f, pl.ds(base, peers, stride=capacity), :] = high
                edge_ref[f, pl.ds(half + base, peers, stride=capacity), :] = value - high
    for c in range(2):
        turned_ref[c] = edge_ref[4 + c].T
    mask = mask_ref[...]
    for c in range(2):
        for o in range(2):
            for q in range(0, pairs, 2):
                both = [turned_ref[c, pl.ds(2 * (q + d) + o, 1), :] * mask for d in range(2)]
                left_ref[2 * o + c, pl.ds(q * aux, 2 * aux), :] = jnp.concatenate(both, 0).astype(bf16)
    dot = functools.partial(jnp.dot, preferred_element_type=jnp.float32)
    spots = column_tiles(sites)
    hots = [column_ref[:, n * LANES : (n + 1) * LANES] for n in range(len(spots))]
    rights = [edge_ref[f].astype(bf16) for f in range(4)]
    row_spots = ((0, 0, 0), (0, 1, 1), (1, 1, 2), (1, 2, 3))
    terms = [[] for _ in range(tiles)]
    for n, (start, tile) in enumerate(spots):
        terms[tile].append((start // sites, hots[n]))
    for o, tile, f in row_spots:
        terms[tile].append((4 + o, rights[f]))
    parts = 3
    size = pairs // parts
    copies = []
    for part in range(parts):
        here = pl.ds(part * size * aux, size * aux)
        lefts = [left_ref[n, here, :] for n in range(4)]
        lefts += [place_ref[o, here, :] for o in range(2)]
        for tile in range(tiles):
            left = jnp.concatenate([lefts[n] for n, _ in terms[tile]], axis=1)
            right = jnp.concatenate([right for _, right in terms[tile]], axis=0)
            placed = dot(left, right)
            for q in range(size):
                at = pl.ds(((part * size + q) * tiles + tile) * aux, aux)
                out_ref[at, :] = sum_ref[at, :] + placed[q * aux : (q + 1) * aux, :]
        here = pl.ds(part * size * tiles * aux, size * tiles * aux)
        copies.append(pltpu.make_async_copy(out_ref.at[here, :], out_hbm.at[here, :], sems.at[part]))
        copies[-1].start()
    for copy in copies:
        copy.wait()


def on_device(
    section_state,
    coupling,
    site_energy,
    bath_rate,
    bath_strength,
    bath_of_site,
    quanta,
    send_list,
    dest_slot,
):
    sites = coupling.shape[0]
    aux, flat = section_state.shape
    depth = quanta.shape[1]
    lane_count = send_list.shape[1]
    peers = lax.axis_size("aux")
    tiers = lax.axis_size("tier")
    capacity = lane_count // (2 * peers)
    sizes = (sites, aux, depth, peers, capacity, tiers)
    rows = aux * sites
    padded = rows + LANES - sites
    slabs = capacity * FIELDS
    chunks = flat // LANES
    half = -(-lane_count // 64) * 64
    f32 = jnp.float32
    bf16 = jnp.bfloat16
    band = lax.axis_index("tier").reshape(1)
    tiled = section_state.reshape(aux, chunks, LANES).transpose(1, 0, 2).reshape(-1, LANES)
    turned_quanta = quanta.T
    bath_row = bath_of_site.reshape(1, -1)
    rate_row = bath_rate.reshape(1, -1)
    strength_row = bath_strength.reshape(1, -1)
    pair_blocks = sites // (2 * SUB)

    def call(kernel, name, inputs, outs, scratch):
        spaces = [space for space, _ in inputs]
        values = [
            value if space is SMEM else pltpu.with_memory_space_constraint(value, space)
            for space, value in inputs
        ]
        return pl.pallas_call(
            functools.partial(kernel, sizes),
            out_shape=[space(shape, dtype) for space, shape, dtype in outs],
            in_specs=[spec(space) for space in spaces],
            out_specs=[spec(space) for space, _, _ in outs],
            scratch_shapes=scratch,
            name=name,
            compiler_params=pltpu.CompilerParams(vmem_limit_bytes=24 * 1024 * 1024),
        )(*values)

    HBM = pltpu.HBM
    dma = pltpu.SemaphoreType.DMA
    i32 = jnp.int32
    store_shape = (FIELDS, padded, LANES)
    reply_shape = (tiers * peers, 1, slabs * LANES)
    payload_shape = (tiers * peers, 1, (slabs + 1) * LANES)
    flat_shape = (aux * chunks, LANES)
    row_scratch = VMEM((2 * peers, 1, LANES), i32)
    trade = functools.partial(
        lax.all_to_all, axis_name=("tier", "aux"), split_axis=0, concat_axis=0, tiled=True
    )
    store, payload = call(
        pack_kernel,
        "pack",
        [(SMEM, band), (HBM, send_list), (HBM, turned_quanta), (HBM, dest_slot), (HBM, tiled)],
        [(VMEM, store_shape, f32), (VMEM, payload_shape, f32)],
        [
            VMEM(flat_shape, f32),
            VMEM(send_list.shape, i32),
            SMEM(turned_quanta.shape, i32),
            VMEM(dest_slot.shape, i32),
            VMEM((3, 1, LANES), i32),
            SMEM((lane_count,), i32),
            dma((pair_blocks,)),
            dma((3,)),
        ],
    )
    arrived = trade(payload).reshape(-1, LANES)
    (reply,) = call(
        answer_kernel,
        "answer",
        [(SMEM, band), (VMEM, arrived), (VMEM, store)],
        [(HBM, reply_shape, f32)],
        [VMEM((2, peers) + reply_shape[1:], f32), row_scratch, dma((2,))],
    )
    returned = trade(reply)
    total, columns, places, coefs, masks = call(
        middle_kernel,
        "middle",
        [
            (SMEM, band),
            (HBM, send_list),
            (HBM, turned_quanta),
            (HBM, bath_row),
            (HBM, rate_row),
            (HBM, strength_row),
            (HBM, coupling),
            (HBM, site_energy.reshape(1, -1)),
            (VMEM, arrived),
            (VMEM, store),
        ],
        [
            (VMEM, flat_shape, f32),
            (VMEM, (2 * half, len(column_tiles(sites)) * LANES), bf16),
            (VMEM, (2, rows // 2, 2 * half), bf16),
            (VMEM, (2, lane_count, LANES), f32),
            (VMEM, (aux, 2 * half), f32),
        ],
        [
            VMEM((4, padded, LANES), f32),
            VMEM((2, 2 * LANES, 2 * LANES), f32),
            VMEM((4, lane_count, LANES), f32),
            row_scratch,
            VMEM(coupling.shape, f32),
            VMEM((3, 1, sites), f32),
            VMEM(send_list.shape, i32),
            VMEM(bath_row.shape, i32),
            SMEM(turned_quanta.shape, i32),
            SMEM(bath_row.shape, i32),
            SMEM(rate_row.shape, f32),
            VMEM((5, 1, 2 * half), f32),
            dma((9,)),
        ],
    )
    (out,) = call(
        lower_kernel,
        "lower",
        [
            (SMEM, band),
            (VMEM, returned.reshape(-1, LANES)),
            (VMEM, total),
            (VMEM, columns),
            (VMEM, places),
            (VMEM, coefs),
            (VMEM, masks),
        ],
        [(HBM, flat_shape, f32)],
        [
            VMEM((6, 2 * half, LANES), f32),
            VMEM((2, LANES, 2 * half), f32),
            VMEM((4, rows // 2, 2 * half), bf16),
            VMEM(flat_shape, f32),
            dma((pair_blocks,)),
        ],
    )
    return out.reshape(chunks, aux, LANES).transpose(1, 0, 2).reshape(aux, flat)


def solution(mesh):
    return jax.shard_map(
        on_device,
        mesh=mesh,
        in_specs=(
            P(("tier", "aux"), None),
            P(),
            P(),
            P(),
            P(),
            P(),
            P(("tier", "aux"), None),
            P(("tier", "aux"), None),
            P(("tier", "aux"), None),
        ),
        out_specs=P(("tier", "aux"), None),
        check_vma=False,
    )
```

```python
import functools

import jax
import jax.numpy as jnp
from jax import lax
from jax.experimental import pallas as pl
from jax.experimental.pallas import tpu as pltpu
from jax.sharding import PartitionSpec as P

thermal = 0.5
LANES = 128
SUB = 8
FIELDS = 3
TAG = 64
VMEM = pltpu.VMEM
SMEM = pltpu.SMEM


def spec(space):
    return pl.BlockSpec(memory_space=space)


def lane_index(shape):
    return lax.broadcasted_iota(jnp.int32, shape, 1)


def fetch(pairs, sems):
    copies = [
        pltpu.make_async_copy(source, target, sems.at[n]) for n, (source, target) in enumerate(pairs)
    ]
    for copy in copies:
        copy.start()
    return copies


def send_blocks(work_ref, wire_hbm, sems, band, step, tiers, peers):
    def block(g):
        at = jnp.clip(band + g * step, 0, tiers - 1) * peers
        return pltpu.make_async_copy(work_ref.at[g], wire_hbm.at[pl.ds(at, peers)], sems.at[g])

    return block


def imaginary(first, second, lane, sites):
    spare = LANES - sites
    return jnp.where(lane < spare, pltpu.roll(first, spare, 1), pltpu.roll(second, spare, 1))


def unmerge(parts, lane, sites):
    first, second, third = parts
    kept = 2 * (LANES - sites)
    col_imag = jnp.where(lane < kept, pltpu.roll(second, kept, 1), pltpu.roll(third, kept, 1))
    return first, imaginary(first, second, lane, sites), pltpu.roll(third, sites, 1), col_imag


def pack_kernel(
    sizes,
    band_ref,
    send_hbm,
    quanta_hbm,
    slot_hbm,
    state_hbm,
    store_ref,
    payload_ref,
    state_ref,
    send_ref,
    quanta_ref,
    slot_ref,
    table_ref,
    row_ref,
    sems,
    table_sems,
):
    sites, aux, depth, peers, capacity, tiers = sizes
    tiles = 4 * sites // LANES
    pair_blocks = sites // (2 * SUB)
    chunk = aux * tiles * SUB
    rows = aux * sites
    tables = fetch(
        [(send_hbm, send_ref), (quanta_hbm, quanta_ref), (slot_hbm, slot_ref)], table_sems
    )
    copies = fetch(
        [(state_hbm, state_ref)],
        sems,
    )
    lane = lane_index((SUB, LANES))
    rest = 2 * sites - LANES
    store_ref[:, pl.ds(rows, LANES - sites), :] = jnp.zeros(
        (FIELDS, LANES - sites, LANES), jnp.float32
    )
    table_ref[...] = jnp.zeros_like(table_ref)
    for table in tables:
        table.wait()
    band = band_ref[0]
    row_lane = lane_index((1, LANES))
    entry = send_ref[...]
    lane_count = entry.shape[1]
    site = jnp.full(entry.shape, -1, jnp.int32)
    base = jnp.zeros(entry.shape, jnp.int32)
    for source in range(aux):
        for place in range(depth):
            here = entry == source * depth + place
            site = jnp.where(here, quanta_ref[place, source], site)
            base = jnp.where(here, source * sites, base)
    group = (lane_index(entry.shape) >= peers * capacity).astype(jnp.int32)
    usable = (entry >= 0) & (site >= 0) & (band - group >= 0)
    site = jnp.maximum(site, 0)
    table_ref[0, :, pl.ds(0, lane_count)] = base + site
    table_ref[1, :, pl.ds(0, lane_count)] = jnp.where(usable, slot_ref[...] * sites, rows)
    table_ref[2, :, pl.ds(0, lane_count)] = jnp.where(usable, site, 0)
    slot_tags, site_tags = table_ref[1], table_ref[2]
    for g in (1, 0):
        for q in range(peers):
            at = (g * peers + q) * capacity
            tags = jnp.where(
                row_lane < TAG,
                pltpu.roll(slot_tags, (LANES - at) % LANES, 1),
                pltpu.roll(site_tags, (LANES + TAG - at) % LANES, 1),
            )
            at_row = jnp.maximum(band - g, 0) * peers + q
            payload_ref[at_row, :, pl.ds(capacity * FIELDS * LANES, LANES)] = tags.astype(
                jnp.float32
            )
    for l in range(lane_count):
        row_ref[l] = table_ref[0, 0, l]
    for copy in copies:
        copy.wait()
    for block in range(pair_blocks):
        for a in range(aux):
            first, middle, last = (
                state_ref[pl.ds(a + aux * (tiles * SUB * block + u), SUB, stride=aux * tiles), :]
                for u in range(tiles)
            )
            middle_turned = pltpu.roll(middle, rest, 1)
            last_turned = pltpu.roll(last, rest, 1)
            base = a * sites + 2 * SUB * block
            store_ref[0, pl.ds(base, SUB, stride=2), :] = first
            store_ref[1, pl.ds(base, SUB, stride=2), :] = jnp.where(lane < rest, middle, first)
            store_ref[0, pl.ds(base + 1, SUB, stride=2), :] = jnp.where(
                lane < rest, middle_turned, last_turned
            )
            store_ref[1, pl.ds(base + 1, SUB, stride=2), :] = last_turned
    kept = LANES - rest
    tail = sites - kept
    wide = lane_index((sites, LANES))
    for a in range(aux):
        here = pl.ds(a * sites, sites)
        first, second = store_ref[0, here, :], store_ref[1, here, :]
        columns = jnp.concatenate([first[kept:, :], first], axis=0).T[:sites, :]
        turned = jnp.concatenate([second[kept:, :], second[kept:, :], second[:kept, :]], axis=0).T
        turned = jnp.concatenate([turned[LANES - tail :, :], turned[:rest, :]], axis=0)
        store_ref[1, here, :] = jnp.where(wide < rest, second, turned)
        store_ref[2, here, :] = jnp.where(wide < tail, turned, columns)
    for g in (1, 0):
        for q in range(peers):
            at_row = jnp.maximum(band - g, 0) * peers + q
            for j in range(capacity):
                row = pl.ds(row_ref[(g * peers + q) * capacity + j], 1)
                for f in range(FIELDS):
                    payload_ref[at_row, :, pl.ds((j * FIELDS + f) * LANES, LANES)] = store_ref[
                        f, row, :
                    ]


def read_rows(sizes, band, arrived_ref, row_ref):
    sites, aux, depth, peers, capacity, tiers = sizes
    slabs = capacity * FIELDS + 1
    for g in range(2):
        origin = jnp.minimum(band + g, tiers - 1) * peers
        tags = arrived_ref[pl.ds(origin * slabs + slabs - 1, peers, stride=slabs), :]
        total = (tags + pltpu.roll(tags, TAG, 1)).astype(jnp.int32)
        row_ref[pl.ds(g * peers, peers), :] = jnp.where(band + g < tiers, total, aux * sites)


def answer_kernel(sizes, band_ref, arrived_ref, store_ref, reply_hbm, reply_ref, row_ref, wire_sems):
    sites, aux, depth, peers, capacity, tiers = sizes
    band = band_ref[0]
    block = send_blocks(reply_ref, reply_hbm, wire_sems, band, 1, tiers, peers)
    read_rows(sizes, band, arrived_ref, row_ref)
    for g in (1, 0):
        for p in range(peers):
            for j in range(capacity):
                row = pl.ds(row_ref[g * peers + p, j], 1)
                for f in range(FIELDS):
                    reply_ref[g, p, :, pl.ds((j * FIELDS + f) * LANES, LANES)] = store_ref[f, row, :]
        if g == 0:
            block(g).start()
        else:
            pl.when(band + g < tiers)(block(g).start)
    block(0).wait()
    pl.when(band + 1 < tiers)(block(1).wait)


def split(value):
    high = value.astype(jnp.bfloat16)
    low = (value - high.astype(jnp.float32)).astype(jnp.bfloat16)
    return high, low


def column_tiles(sites):
    spots = []
    for field in range(4):
        start = field * sites
        first, last = start // LANES, (start + sites - 1) // LANES
        spots += [(start, tile) for tile in range(first, last + 1)]
    return spots


def spread(row):
    return jnp.broadcast_to(row, (row.shape[1], row.shape[1])).T


def middle_kernel(
    sizes,
    band_ref,
    send_hbm,
    quanta_hbm,
    bath_hbm,
    rate_hbm,
    strength_hbm,
    coupling_hbm,
    energy_hbm,
    arrived_ref,
    store_ref,
    sum_ref,
    column_ref,
    place_ref,
    coef_ref,
    mask_ref,
    work_ref,
    matrix_ref,
    edge_ref,
    row_ref,
    coupling_ref,
    vector_ref,
    send_ref,
    bath_row,
    quanta_ref,
    bath_ref,
    rate_ref,
    index_ref,
    sems,
):
    sites, aux, depth, peers, capacity, tiers = sizes
    rows = aux * sites
    rest = 2 * sites - LANES
    f32 = jnp.float32
    band = band_ref[0]
    copies = fetch(
        [
            (coupling_hbm, coupling_ref),
            (energy_hbm, vector_ref.at[0]),
            (rate_hbm, vector_ref.at[1]),
            (strength_hbm, vector_ref.at[2]),
            (send_hbm, send_ref),
            (bath_hbm, bath_row),
            (quanta_hbm, quanta_ref),
            (bath_hbm, bath_ref),
            (rate_hbm, rate_ref),
        ],
        sems,
    )
    read_rows(sizes, band, arrived_ref, row_ref)
    lane = lane_index((peers, LANES))
    for g in range(2):
        origin = jnp.minimum(band + g, tiers - 1) * peers
        for j in range(capacity):
            slabs = capacity * FIELDS + 1
            parts = [
                arrived_ref[pl.ds(origin * slabs + j * FIELDS + f, peers, stride=slabs), :]
                for f in range(FIELDS)
            ]
            row_real, row_imag, col_real, col_imag = unmerge(parts, lane, sites)
            for f, value in enumerate((row_imag, -row_real, -col_imag, col_real)):
                edge_ref[f, pl.ds(g * peers * capacity + j, peers, stride=capacity), :] = value
    matrix_ref[...] = jnp.zeros_like(matrix_ref)
    index_ref[...] = jnp.full(index_ref.shape, -1.0, f32)
    work_ref[:, pl.ds(rows, LANES - sites), :] = jnp.zeros((4, LANES - sites, LANES), f32)
    for copy in copies:
        copy.wait()
    row_ids = lax.broadcasted_iota(jnp.int32, (sites, sites), 0)
    col_ids = lane_index((sites, sites))
    coupling = coupling_ref[...]
    hamilton = (coupling + coupling.T) * 0.5 + jnp.where(row_ids == col_ids, vector_ref[0], 0.0)
    real, imag = pl.ds(0, sites), pl.ds(LANES, sites)
    matrix_ref[0, real, imag] = hamilton
    matrix_ref[0, pl.ds(sites, sites), real] = -hamilton
    matrix_ref[1, pl.ds(rest, sites), real] = hamilton
    matrix_ref[1, pl.ds(2 * LANES - sites, sites), imag] = -hamilton
    dot = functools.partial(jnp.dot, preferred_element_type=f32)
    splits = [split(matrix_ref[half]) for half in range(2)]
    lane = lane_index((sites, LANES))
    for a in range(aux):
        damp = f32(0.0)
        for place in range(depth):
            site = quanta_ref[place, a]
            rate = rate_ref[0, bath_ref[0, jnp.maximum(site, 0)]]
            damp = damp + jnp.where(site >= 0, rate, 0.0)
        here = pl.ds(a * sites, sites)
        for half in range(2):
            high, low = splits[half]
            first, second = store_ref[half, here, :], store_ref[half + 1, here, :]
            both_high, both_low = split(jnp.concatenate([first, second], axis=1))
            product = dot(both_high, high) + (dot(both_low, high) + dot(both_high, low))
            pair = [product[:, :LANES], product[:, LANES:]]
            if half == 0:
                pair[0] = pair[0] - damp * first
                pair[1] = pair[1] - damp * imaginary(first, second, lane, sites)
            for c in range(2):
                work_ref[2 * half + c, here, :] = pair[c]

    entry = send_ref[...]
    lane_count = entry.shape[1]
    half = index_ref.shape[2] // 2
    site = jnp.full(entry.shape, -1, jnp.int32)
    source = jnp.zeros(entry.shape, jnp.int32)
    for a in range(aux):
        for place in range(depth):
            hit = entry == a * depth + place
            site = jnp.where(hit, quanta_ref[place, a], site)
            source = jnp.where(hit, a, source)
    weight = jnp.zeros(entry.shape, f32)
    for a in range(aux):
        for place in range(depth):
            hit = (source == a) & (site == quanta_ref[place, a])
            weight = weight + jnp.where(hit, 1.0, 0.0)
    group = (lane_index(entry.shape) >= peers * capacity).astype(jnp.int32)
    usable = (entry >= 0) & (site >= 0) & (band - group >= 0)
    weight = jnp.where(usable, weight, 0.0)
    bath_of = spread(bath_row[...].astype(f32)) == col_ids.astype(f32)
    rate_of = jnp.sum(jnp.where(bath_of, vector_ref[1], 0.0), axis=1, keepdims=True)
    strength_of = jnp.sum(jnp.where(bath_of, vector_ref[2], 0.0), axis=1, keepdims=True)
    at_site = lax.broadcasted_iota(jnp.int32, (sites, lane_count), 0) == site
    rate = jnp.sum(jnp.where(at_site, rate_of, 0.0), axis=0, keepdims=True)
    strength = jnp.sum(jnp.where(at_site, strength_of, 0.0), axis=0, keepdims=True)
    lanes = pl.ds(0, lane_count)
    index_ref[3, :, lanes] = -weight * (strength * rate)
    index_ref[4, :, lanes] = weight * (2.0 * thermal * strength)
    for c in range(2):
        coef_ref[c] = spread(index_ref[3 + c, :, pl.ds(0, LANES)])[:lane_count, :]
    rows_of = (
        jnp.where(usable, source * sites + site, -1),
        jnp.where(usable, site, -2 * LANES),
        jnp.where(usable, source, -1),
    )
    for start in (0, half):
        for c in range(3):
            index_ref[c, :, pl.ds(start, lane_count)] = rows_of[c].astype(f32)
    tiles = 4 * sites // LANES
    pairs = sites // 2
    for slab in range(2 * half // LANES):
        part = pl.ds(slab * LANES, LANES)
        turned = spread(index_ref[1, :, part])
        here = lane_index((LANES, LANES))
        for n, (offset, tile) in enumerate(column_tiles(sites)):
            hot = turned == (here + (tile * LANES - offset)).astype(f32)
            column_ref[part, pl.ds(n * LANES, LANES)] = jnp.where(hot, 1.0, 0.0).astype(jnp.bfloat16)
        at_aux = lax.broadcasted_iota(jnp.int32, (aux, LANES), 0).astype(f32)
        mask_ref[:, part] = jnp.where(index_ref[2, :, part] == at_aux, 1.0, 0.0)
        for o in range(2):
            shape = (pairs, aux, LANES)
            at = 2 * lax.broadcasted_iota(jnp.int32, shape, 0) + o
            at = at + sites * lax.broadcasted_iota(jnp.int32, shape, 1)
            hot = index_ref[0, :, part] == at.reshape(pairs * aux, LANES).astype(f32)
            place_ref[o, :, part] = jnp.where(hot, 1.0, 0.0).astype(jnp.bfloat16)

    for g in range(2):
        for p in range(peers):
            for j in range(capacity):
                l = (g * peers + p) * capacity + j
                row = pl.ds(row_ref[g * peers + p, j], 1)
                for c in range(4):
                    work_ref[c, row, :] = work_ref[c, row, :] + edge_ref[c, pl.ds(l, 1), :]
    for a in range(aux):
        here = pl.ds(a * sites, sites)
        for c in range(2):
            turned = work_ref[2 + c, pl.ds(a * sites, LANES), :].T[:sites, :]
            work_ref[c, here, :] = work_ref[c, here, :] + turned
    pair_blocks = sites // (2 * SUB)
    lane = lane_index((SUB, LANES))
    for block in range(pair_blocks):
        for a in range(aux):
            base = a * sites + 2 * SUB * block
            even_real, even_imag, odd_real, odd_imag = (
                work_ref[c, pl.ds(base + o, SUB, stride=2), :] for o in (0, 1) for c in (0, 1)
            )
            turned_imag = pltpu.roll(even_imag, 96, 1)
            turned_real = pltpu.roll(odd_real, 64, 1)
            parts = (
                jnp.where(lane < 96, even_real, turned_imag),
                jnp.where(lane < 64, turned_imag, turned_real),
                jnp.where(lane < 32, turned_real, pltpu.roll(odd_imag, 32, 1)),
            )
            for u in range(tiles):
                start = a + aux * (tiles * SUB * block + u)
                sum_ref[pl.ds(start, SUB, stride=aux * tiles), :] = parts[u]


def lower_kernel(
    sizes,
    band_ref,
    returned_ref,
    sum_ref,
    column_ref,
    place_ref,
    coef_ref,
    mask_ref,
    out_hbm,
    edge_ref,
    turned_ref,
    left_ref,
    out_ref,
    sems,
):
    sites, aux, depth, peers, capacity, tiers = sizes
    tiles = 4 * sites // LANES
    pairs = sites // 2
    slabs = capacity * FIELDS
    used = 2 * capacity * peers
    half = edge_ref.shape[1] // 2
    rest = 2 * sites - LANES
    bf16 = jnp.bfloat16
    band = band_ref[0]
    lane = lane_index((peers, LANES))
    if used < half:
        for top in (used, half + used):
            edge_ref[:, pl.ds(top, half - used), :] = jnp.zeros(
                (6, half - used, LANES), jnp.float32
            )
    for g in range(2):
        target = jnp.maximum(band - g, 0)
        for j in range(capacity):
            start = target * (peers * slabs) + j * FIELDS
            parts = [
                returned_ref[pl.ds(start + f, peers, stride=slabs), :] for f in range(FIELDS)
            ]
            row_real, row_imag, col_real, col_imag = unmerge(parts, lane, sites)
            base = g * peers * capacity + j
            shared = coef_ref[0, pl.ds(base, peers, stride=capacity), :]
            turn = coef_ref[1, pl.ds(base, peers, stride=capacity), :]
            real = shared * row_real + turn * row_imag
            imag = pltpu.roll(shared * row_imag - turn * row_real, sites, 1)
            head = jnp.where(lane < sites, real, imag)
            head_turned = pltpu.roll(head, rest, 1)
            values = (
                head,
                jnp.where(lane < rest, imag, 0.0),
                jnp.where(lane < rest, 0.0, head_turned),
                jnp.where(lane < rest, head_turned, pltpu.roll(imag, rest, 1)),
                shared * col_real - turn * col_imag,
                shared * col_imag + turn * col_real,
            )
            for f, value in enumerate(values):
                high = value.astype(bf16).astype(jnp.float32)
                edge_ref[f, pl.ds(base, peers, stride=capacity), :] = high
                edge_ref[f, pl.ds(half + base, peers, stride=capacity), :] = value - high
    for c in range(2):
        turned_ref[c] = edge_ref[4 + c].T
    mask = mask_ref[...]
    for c in range(2):
        for o in range(2):
            for q in range(0, pairs, 2):
                both = [turned_ref[c, pl.ds(2 * (q + d) + o, 1), :] * mask for d in range(2)]
                left_ref[2 * o + c, pl.ds(q * aux, 2 * aux), :] = jnp.concatenate(both, 0).astype(bf16)
    dot = functools.partial(jnp.dot, preferred_element_type=jnp.float32)
    spots = column_tiles(sites)
    hots = [column_ref[:, n * LANES : (n + 1) * LANES] for n in range(len(spots))]
    rights = [edge_ref[f].astype(bf16) for f in range(4)]
    row_spots = ((0, 0, 0), (0, 1, 1), (1, 1, 2), (1, 2, 3))
    terms = [[] for _ in range(tiles)]
    for n, (start, tile) in enumerate(spots):
        terms[tile].append((start // sites, hots[n]))
    for o, tile, f in row_spots:
        terms[tile].append((4 + o, rights[f]))
    parts = 3
    size = pairs // parts
    copies = []
    for part in range(parts):
        here = pl.ds(part * size * aux, size * aux)
        lefts = [left_ref[n, here, :] for n in range(4)]
        lefts += [place_ref[o, here, :] for o in range(2)]
        for tile in range(tiles):
            left = jnp.concatenate([lefts[n] for n, _ in terms[tile]], axis=1)
            right = jnp.concatenate([right for _, right in terms[tile]], axis=0)
            placed = dot(left, right)
            for q in range(size):
                at = pl.ds(((part * size + q) * tiles + tile) * aux, aux)
                out_ref[at, :] = sum_ref[at, :] + placed[q * aux : (q + 1) * aux, :]
        here = pl.ds(part * size * tiles * aux, size * tiles * aux)
        copies.append(pltpu.make_async_copy(out_ref.at[here, :], out_hbm.at[here, :], sems.at[part]))
        copies[-1].start()
    for copy in copies:
        copy.wait()


def on_device(
    section_state,
    coupling,
    site_energy,
    bath_rate,
    bath_strength,
    bath_of_site,
    quanta,
    send_list,
    dest_slot,
):
    sites = coupling.shape[0]
    aux, flat = section_state.shape
    depth = quanta.shape[1]
    lane_count = send_list.shape[1]
    peers = lax.axis_size("aux")
    tiers = lax.axis_size("tier")
    capacity = lane_count // (2 * peers)
    sizes = (sites, aux, depth, peers, capacity, tiers)
    rows = aux * sites
    padded = rows + LANES - sites
    slabs = capacity * FIELDS
    chunks = flat // LANES
    half = -(-lane_count // 64) * 64
    f32 = jnp.float32
    bf16 = jnp.bfloat16
    band = lax.axis_index("tier").reshape(1)
    tiled = section_state.reshape(aux, chunks, LANES).transpose(1, 0, 2).reshape(-1, LANES)
    turned_quanta = quanta.T
    bath_row = bath_of_site.reshape(1, -1)
    rate_row = bath_rate.reshape(1, -1)
    strength_row = bath_strength.reshape(1, -1)
    pair_blocks = sites // (2 * SUB)

    def call(kernel, name, inputs, outs, scratch):
        spaces = [space for space, _ in inputs]
        values = [
            value if space is SMEM else pltpu.with_memory_space_constraint(value, space)
            for space, value in inputs
        ]
        return pl.pallas_call(
            functools.partial(kernel, sizes),
            out_shape=[space(shape, dtype) for space, shape, dtype in outs],
            in_specs=[spec(space) for space in spaces],
            out_specs=[spec(space) for space, _, _ in outs],
            scratch_shapes=scratch,
            name=name,
            compiler_params=pltpu.CompilerParams(vmem_limit_bytes=24 * 1024 * 1024),
        )(*values)

    HBM = pltpu.HBM
    dma = pltpu.SemaphoreType.DMA
    i32 = jnp.int32
    store_shape = (FIELDS, padded, LANES)
    reply_shape = (tiers * peers, 1, slabs * LANES)
    payload_shape = (tiers * peers, 1, (slabs + 1) * LANES)
    flat_shape = (aux * chunks, LANES)
    row_scratch = VMEM((2 * peers, LANES), i32)
    trade = functools.partial(
        lax.all_to_all, axis_name=("tier", "aux"), split_axis=0, concat_axis=0, tiled=True
    )
    store, payload = call(
        pack_kernel,
        "pack",
        [(SMEM, band), (HBM, send_list), (HBM, turned_quanta), (HBM, dest_slot), (HBM, tiled)],
        [(VMEM, store_shape, f32), (VMEM, payload_shape, f32)],
        [
            VMEM(flat_shape, f32),
            VMEM(send_list.shape, i32),
            SMEM(turned_quanta.shape, i32),
            VMEM(dest_slot.shape, i32),
            VMEM((3, 1, LANES), i32),
            SMEM((lane_count,), i32),
            dma((pair_blocks,)),
            dma((3,)),
        ],
    )
    arrived = trade(payload).reshape(-1, LANES)
    (reply,) = call(
        answer_kernel,
        "answer",
        [(SMEM, band), (VMEM, arrived), (VMEM, store)],
        [(HBM, reply_shape, f32)],
        [VMEM((2, peers) + reply_shape[1:], f32), row_scratch, dma((2,))],
    )
    returned = trade(reply)
    total, columns, places, coefs, masks = call(
        middle_kernel,
        "middle",
        [
            (SMEM, band),
            (HBM, send_list),
            (HBM, turned_quanta),
            (HBM, bath_row),
            (HBM, rate_row),
            (HBM, strength_row),
            (HBM, coupling),
            (HBM, site_energy.reshape(1, -1)),
            (VMEM, arrived),
            (VMEM, store),
        ],
        [
            (VMEM, flat_shape, f32),
            (VMEM, (2 * half, len(column_tiles(sites)) * LANES), bf16),
            (VMEM, (2, rows // 2, 2 * half), bf16),
            (VMEM, (2, lane_count, LANES), f32),
            (VMEM, (aux, 2 * half), f32),
        ],
        [
            VMEM((4, padded, LANES), f32),
            VMEM((2, 2 * LANES, 2 * LANES), f32),
            VMEM((4, lane_count, LANES), f32),
            row_scratch,
            VMEM(coupling.shape, f32),
            VMEM((3, 1, sites), f32),
            VMEM(send_list.shape, i32),
            VMEM(bath_row.shape, i32),
            SMEM(turned_quanta.shape, i32),
            SMEM(bath_row.shape, i32),
            SMEM(rate_row.shape, f32),
            VMEM((5, 1, 2 * half), f32),
            dma((9,)),
        ],
    )
    (out,) = call(
        lower_kernel,
        "lower",
        [
            (SMEM, band),
            (VMEM, returned.reshape(-1, LANES)),
            (VMEM, total),
            (VMEM, columns),
            (VMEM, places),
            (VMEM, coefs),
            (VMEM, masks),
        ],
        [(HBM, flat_shape, f32)],
        [
            VMEM((6, 2 * half, LANES), f32),
            VMEM((2, LANES, 2 * half), f32),
            VMEM((4, rows // 2, 2 * half), bf16),
            VMEM(flat_shape, f32),
            dma((pair_blocks,)),
        ],
    )
    return out.reshape(chunks, aux, LANES).transpose(1, 0, 2).reshape(aux, flat)


def solution(mesh):
    return jax.shard_map(
        on_device,
        mesh=mesh,
        in_specs=(
            P(("tier", "aux"), None),
            P(),
            P(),
            P(),
            P(),
            P(),
            P(("tier", "aux"), None),
            P(("tier", "aux"), None),
            P(("tier", "aux"), None),
        ),
        out_specs=P(("tier", "aux"), None),
        check_vma=False,
    )
```

```python
import functools

import jax
import jax.numpy as jnp
from jax import lax
from jax.experimental import pallas as pl
from jax.experimental.pallas import tpu as pltpu
from jax.sharding import PartitionSpec as P

thermal = 0.5
LANES = 128
SUB = 8
FIELDS = 3
TAG = 64
VMEM = pltpu.VMEM
SMEM = pltpu.SMEM


def spec(space):
    return pl.BlockSpec(memory_space=space)


def lane_index(shape):
    return lax.broadcasted_iota(jnp.int32, shape, 1)


def fetch(pairs, sems):
    copies = [
        pltpu.make_async_copy(source, target, sems.at[n]) for n, (source, target) in enumerate(pairs)
    ]
    for copy in copies:
        copy.start()
    return copies


def send_blocks(work_ref, wire_hbm, sems, band, step, tiers, peers):
    def block(g):
        at = jnp.clip(band + g * step, 0, tiers - 1) * peers
        return pltpu.make_async_copy(work_ref.at[g], wire_hbm.at[pl.ds(at, peers)], sems.at[g])

    return block


def imaginary(first, second, lane, sites):
    spare = LANES - sites
    return jnp.where(lane < spare, pltpu.roll(first, spare, 1), pltpu.roll(second, spare, 1))


def unmerge(parts, lane, sites):
    first, second, third = parts
    kept = 2 * (LANES - sites)
    col_imag = jnp.where(lane < kept, pltpu.roll(second, kept, 1), pltpu.roll(third, kept, 1))
    return first, imaginary(first, second, lane, sites), pltpu.roll(third, sites, 1), col_imag


def pack_kernel(
    sizes,
    band_ref,
    send_hbm,
    quanta_hbm,
    slot_hbm,
    state_hbm,
    store_ref,
    payload_ref,
    state_ref,
    send_ref,
    quanta_ref,
    slot_ref,
    table_ref,
    row_ref,
    sems,
    table_sems,
):
    sites, aux, depth, peers, capacity, tiers = sizes
    tiles = 4 * sites // LANES
    pair_blocks = sites // (2 * SUB)
    chunk = aux * tiles * SUB
    rows = aux * sites
    tables = fetch(
        [(send_hbm, send_ref), (quanta_hbm, quanta_ref), (slot_hbm, slot_ref)], table_sems
    )
    copies = fetch(
        [(state_hbm, state_ref)],
        sems,
    )
    lane = lane_index((SUB, LANES))
    rest = 2 * sites - LANES
    store_ref[:, pl.ds(rows, LANES - sites), :] = jnp.zeros(
        (FIELDS, LANES - sites, LANES), jnp.float32
    )
    table_ref[...] = jnp.zeros_like(table_ref)
    for table in tables:
        table.wait()
    band = band_ref[0]
    row_lane = lane_index((1, LANES))
    entry = send_ref[...]
    lane_count = entry.shape[1]
    site = jnp.full(entry.shape, -1, jnp.int32)
    base = jnp.zeros(entry.shape, jnp.int32)
    for source in range(aux):
        for place in range(depth):
            here = entry == source * depth + place
            site = jnp.where(here, quanta_ref[place, source], site)
            base = jnp.where(here, source * sites, base)
    group = (lane_index(entry.shape) >= peers * capacity).astype(jnp.int32)
    usable = (entry >= 0) & (site >= 0) & (band - group >= 0)
    site = jnp.maximum(site, 0)
    table_ref[0, :, pl.ds(0, lane_count)] = base + site
    table_ref[1, :, pl.ds(0, lane_count)] = jnp.where(usable, slot_ref[...] * sites, rows)
    table_ref[2, :, pl.ds(0, lane_count)] = jnp.where(usable, site, 0)
    slot_tags, site_tags = table_ref[1], table_ref[2]
    for g in (1, 0):
        for q in range(peers):
            at = (g * peers + q) * capacity
            tags = jnp.where(
                row_lane < TAG,
                pltpu.roll(slot_tags, (LANES - at) % LANES, 1),
                pltpu.roll(site_tags, (LANES + TAG - at) % LANES, 1),
            )
            at_row = jnp.maximum(band - g, 0) * peers + q
            payload_ref[at_row, :, pl.ds(capacity * FIELDS * LANES, LANES)] = tags.astype(
                jnp.float32
            )
    for l in range(lane_count):
        row_ref[l] = table_ref[0, 0, l]
    for copy in copies:
        copy.wait()
    for block in range(pair_blocks):
        for a in range(aux):
            first, middle, last = (
                state_ref[pl.ds(a + aux * (tiles * SUB * block + u), SUB, stride=aux * tiles), :]
                for u in range(tiles)
            )
            middle_turned = pltpu.roll(middle, rest, 1)
            last_turned = pltpu.roll(last, rest, 1)
            base = a * sites + 2 * SUB * block
            store_ref[0, pl.ds(base, SUB, stride=2), :] = first
            store_ref[1, pl.ds(base, SUB, stride=2), :] = jnp.where(lane < rest, middle, first)
            store_ref[0, pl.ds(base + 1, SUB, stride=2), :] = jnp.where(
                lane < rest, middle_turned, last_turned
            )
            store_ref[1, pl.ds(base + 1, SUB, stride=2), :] = last_turned
    kept = LANES - rest
    tail = sites - kept
    wide = lane_index((sites, LANES))
    for a in range(aux):
        here = pl.ds(a * sites, sites)
        first, second = store_ref[0, here, :], store_ref[1, here, :]
        columns = jnp.concatenate([first[kept:, :], first], axis=0).T[:sites, :]
        turned = jnp.concatenate([second[kept:, :], second[kept:, :], second[:kept, :]], axis=0).T
        turned = jnp.concatenate([turned[LANES - tail :, :], turned[:rest, :]], axis=0)
        store_ref[1, here, :] = jnp.where(wide < rest, second, turned)
        store_ref[2, here, :] = jnp.where(wide < tail, turned, columns)
    for g in (1, 0):
        for q in range(peers):
            at_row = jnp.maximum(band - g, 0) * peers + q
            for j in range(capacity):
                row = pl.ds(row_ref[(g * peers + q) * capacity + j], 1)
                for f in range(FIELDS):
                    payload_ref[at_row, :, pl.ds((j * FIELDS + f) * LANES, LANES)] = store_ref[
                        f, row, :
                    ]


def read_rows(sizes, band, arrived_ref, row_ref):
    sites, aux, depth, peers, capacity, tiers = sizes
    slabs = capacity * FIELDS + 1
    for g in range(2):
        origin = jnp.minimum(band + g, tiers - 1) * peers
        for p in range(peers):
            tags = arrived_ref[pl.ds((origin + p) * slabs + slabs - 1, 1), :]
            total = (tags + pltpu.roll(tags, TAG, 1)).astype(jnp.int32)
            row_ref[g * peers + p] = jnp.where(band + g < tiers, total, aux * sites)


def answer_kernel(sizes, band_ref, arrived_ref, store_ref, reply_hbm, reply_ref, row_ref, wire_sems):
    sites, aux, depth, peers, capacity, tiers = sizes
    band = band_ref[0]
    block = send_blocks(reply_ref, reply_hbm, wire_sems, band, 1, tiers, peers)
    read_rows(sizes, band, arrived_ref, row_ref)
    for g in (1, 0):
        for p in range(peers):
            for j in range(capacity):
                row = pl.ds(row_ref[g * peers + p, 0, j], 1)
                for f in range(FIELDS):
                    reply_ref[g, p, :, pl.ds((j * FIELDS + f) * LANES, LANES)] = store_ref[f, row, :]
        if g == 0:
            block(g).start()
        else:
            pl.when(band + g < tiers)(block(g).start)
    block(0).wait()
    pl.when(band + 1 < tiers)(block(1).wait)


def split(value):
    high = value.astype(jnp.bfloat16)
    low = (value - high.astype(jnp.float32)).astype(jnp.bfloat16)
    return high, low


def column_tiles(sites):
    spots = []
    for field in range(4):
        start = field * sites
        first, last = start // LANES, (start + sites - 1) // LANES
        spots += [(start, tile) for tile in range(first, last + 1)]
    return spots


def spread(row):
    return jnp.broadcast_to(row, (row.shape[1], row.shape[1])).T


def middle_kernel(
    sizes,
    band_ref,
    send_hbm,
    quanta_hbm,
    bath_hbm,
    rate_hbm,
    strength_hbm,
    coupling_hbm,
    energy_hbm,
    arrived_ref,
    store_ref,
    sum_ref,
    column_ref,
    place_ref,
    coef_ref,
    mask_ref,
    work_ref,
    matrix_ref,
    edge_ref,
    row_ref,
    coupling_ref,
    vector_ref,
    send_ref,
    bath_row,
    quanta_ref,
    bath_ref,
    rate_ref,
    index_ref,
    sems,
):
    sites, aux, depth, peers, capacity, tiers = sizes
    rows = aux * sites
    rest = 2 * sites - LANES
    f32 = jnp.float32
    band = band_ref[0]
    copies = fetch(
        [
            (coupling_hbm, coupling_ref),
            (energy_hbm, vector_ref.at[0]),
            (rate_hbm, vector_ref.at[1]),
            (strength_hbm, vector_ref.at[2]),
            (send_hbm, send_ref),
            (bath_hbm, bath_row),
            (quanta_hbm, quanta_ref),
            (bath_hbm, bath_ref),
            (rate_hbm, rate_ref),
        ],
        sems,
    )
    read_rows(sizes, band, arrived_ref, row_ref)
    lane = lane_index((peers, LANES))
    for g in range(2):
        origin = jnp.minimum(band + g, tiers - 1) * peers
        for j in range(capacity):
            slabs = capacity * FIELDS + 1
            parts = [
                arrived_ref[pl.ds(origin * slabs + j * FIELDS + f, peers, stride=slabs), :]
                for f in range(FIELDS)
            ]
            row_real, row_imag, col_real, col_imag = unmerge(parts, lane, sites)
            for f, value in enumerate((row_imag, -row_real, -col_imag, col_real)):
                edge_ref[f, pl.ds(g * peers * capacity + j, peers, stride=capacity), :] = value
    matrix_ref[...] = jnp.zeros_like(matrix_ref)
    index_ref[...] = jnp.full(index_ref.shape, -1.0, f32)
    work_ref[:, pl.ds(rows, LANES - sites), :] = jnp.zeros((4, LANES - sites, LANES), f32)
    for copy in copies:
        copy.wait()
    row_ids = lax.broadcasted_iota(jnp.int32, (sites, sites), 0)
    col_ids = lane_index((sites, sites))
    coupling = coupling_ref[...]
    hamilton = (coupling + coupling.T) * 0.5 + jnp.where(row_ids == col_ids, vector_ref[0], 0.0)
    real, imag = pl.ds(0, sites), pl.ds(LANES, sites)
    matrix_ref[0, real, imag] = hamilton
    matrix_ref[0, pl.ds(sites, sites), real] = -hamilton
    matrix_ref[1, pl.ds(rest, sites), real] = hamilton
    matrix_ref[1, pl.ds(2 * LANES - sites, sites), imag] = -hamilton
    dot = functools.partial(jnp.dot, preferred_element_type=f32)
    splits = [split(matrix_ref[half]) for half in range(2)]
    lane = lane_index((sites, LANES))
    for a in range(aux):
        damp = f32(0.0)
        for place in range(depth):
            site = quanta_ref[place, a]
            rate = rate_ref[0, bath_ref[0, jnp.maximum(site, 0)]]
            damp = damp + jnp.where(site >= 0, rate, 0.0)
        here = pl.ds(a * sites, sites)
        for half in range(2):
            high, low = splits[half]
            first, second = store_ref[half, here, :], store_ref[half + 1, here, :]
            both_high, both_low = split(jnp.concatenate([first, second], axis=1))
            product = dot(both_high, high) + (dot(both_low, high) + dot(both_high, low))
            pair = [product[:, :LANES], product[:, LANES:]]
            if half == 0:
                pair[0] = pair[0] - damp * first
                pair[1] = pair[1] - damp * imaginary(first, second, lane, sites)
            for c in range(2):
                work_ref[2 * half + c, here, :] = pair[c]

    entry = send_ref[...]
    lane_count = entry.shape[1]
    half = index_ref.shape[2] // 2
    site = jnp.full(entry.shape, -1, jnp.int32)
    source = jnp.zeros(entry.shape, jnp.int32)
    for a in range(aux):
        for place in range(depth):
            hit = entry == a * depth + place
            site = jnp.where(hit, quanta_ref[place, a], site)
            source = jnp.where(hit, a, source)
    weight = jnp.zeros(entry.shape, f32)
    for a in range(aux):
        for place in range(depth):
            hit = (source == a) & (site == quanta_ref[place, a])
            weight = weight + jnp.where(hit, 1.0, 0.0)
    group = (lane_index(entry.shape) >= peers * capacity).astype(jnp.int32)
    usable = (entry >= 0) & (site >= 0) & (band - group >= 0)
    weight = jnp.where(usable, weight, 0.0)
    bath_of = spread(bath_row[...].astype(f32)) == col_ids.astype(f32)
    rate_of = jnp.sum(jnp.where(bath_of, vector_ref[1], 0.0), axis=1, keepdims=True)
    strength_of = jnp.sum(jnp.where(bath_of, vector_ref[2], 0.0), axis=1, keepdims=True)
    at_site = lax.broadcasted_iota(jnp.int32, (sites, lane_count), 0) == site
    rate = jnp.sum(jnp.where(at_site, rate_of, 0.0), axis=0, keepdims=True)
    strength = jnp.sum(jnp.where(at_site, strength_of, 0.0), axis=0, keepdims=True)
    lanes = pl.ds(0, lane_count)
    index_ref[3, :, lanes] = -weight * (strength * rate)
    index_ref[4, :, lanes] = weight * (2.0 * thermal * strength)
    for c in range(2):
        coef_ref[c] = spread(index_ref[3 + c, :, pl.ds(0, LANES)])[:lane_count, :]
    rows_of = (
        jnp.where(usable, source * sites + site, -1),
        jnp.where(usable, site, -2 * LANES),
        jnp.where(usable, source, -1),
    )
    for start in (0, half):
        for c in range(3):
            index_ref[c, :, pl.ds(start, lane_count)] = rows_of[c].astype(f32)
    tiles = 4 * sites // LANES
    pairs = sites // 2
    for slab in range(2 * half // LANES):
        part = pl.ds(slab * LANES, LANES)
        turned = spread(index_ref[1, :, part])
        here = lane_index((LANES, LANES))
        for n, (offset, tile) in enumerate(column_tiles(sites)):
            hot = turned == (here + (tile * LANES - offset)).astype(f32)
            column_ref[part, pl.ds(n * LANES, LANES)] = jnp.where(hot, 1.0, 0.0).astype(jnp.bfloat16)
        at_aux = lax.broadcasted_iota(jnp.int32, (aux, LANES), 0).astype(f32)
        mask_ref[:, part] = jnp.where(index_ref[2, :, part] == at_aux, 1.0, 0.0)
        for o in range(2):
            shape = (pairs, aux, LANES)
            at = 2 * lax.broadcasted_iota(jnp.int32, shape, 0) + o
            at = at + sites * lax.broadcasted_iota(jnp.int32, shape, 1)
            hot = index_ref[0, :, part] == at.reshape(pairs * aux, LANES).astype(f32)
            place_ref[o, :, part] = jnp.where(hot, 1.0, 0.0).astype(jnp.bfloat16)

    for g in range(2):
        for p in range(peers):
            for j in range(capacity):
                l = (g * peers + p) * capacity + j
                row = pl.ds(row_ref[g * peers + p, 0, j], 1)
                for c in range(4):
                    work_ref[c, row, :] = work_ref[c, row, :] + edge_ref[c, pl.ds(l, 1), :]
    for a in range(aux):
        here = pl.ds(a * sites, sites)
        for c in range(2):
            turned = work_ref[2 + c, pl.ds(a * sites, LANES), :].T[:sites, :]
            work_ref[c, here, :] = work_ref[c, here, :] + turned
    pair_blocks = sites // (2 * SUB)
    lane = lane_index((SUB, LANES))
    for block in range(pair_blocks):
        for a in range(aux):
            base = a * sites + 2 * SUB * block
            even_real, even_imag, odd_real, odd_imag = (
                work_ref[c, pl.ds(base + o, SUB, stride=2), :] for o in (0, 1) for c in (0, 1)
            )
            turned_imag = pltpu.roll(even_imag, 96, 1)
            turned_real = pltpu.roll(odd_real, 64, 1)
            parts = (
                jnp.where(lane < 96, even_real, turned_imag),
                jnp.where(lane < 64, turned_imag, turned_real),
                jnp.where(lane < 32, turned_real, pltpu.roll(odd_imag, 32, 1)),
            )
            for u in range(tiles):
                start = a + aux * (tiles * SUB * block + u)
                sum_ref[pl.ds(start, SUB, stride=aux * tiles), :] = parts[u]


def lower_kernel(
    sizes,
    band_ref,
    returned_ref,
    sum_ref,
    column_ref,
    place_ref,
    coef_ref,
    mask_ref,
    out_hbm,
    edge_ref,
    turned_ref,
    left_ref,
    out_ref,
    sems,
):
    sites, aux, depth, peers, capacity, tiers = sizes
    tiles = 4 * sites // LANES
    pairs = sites // 2
    slabs = capacity * FIELDS
    used = 2 * capacity * peers
    half = edge_ref.shape[1] // 2
    rest = 2 * sites - LANES
    bf16 = jnp.bfloat16
    band = band_ref[0]
    lane = lane_index((peers, LANES))
    if used < half:
        for top in (used, half + used):
            edge_ref[:, pl.ds(top, half - used), :] = jnp.zeros(
                (6, half - used, LANES), jnp.float32
            )
    for g in range(2):
        target = jnp.maximum(band - g, 0)
        for j in range(capacity):
            start = target * (peers * slabs) + j * FIELDS
            parts = [
                returned_ref[pl.ds(start + f, peers, stride=slabs), :] for f in range(FIELDS)
            ]
            row_real, row_imag, col_real, col_imag = unmerge(parts, lane, sites)
            base = g * peers * capacity + j
            shared = coef_ref[0, pl.ds(base, peers, stride=capacity), :]
            turn = coef_ref[1, pl.ds(base, peers, stride=capacity), :]
            real = shared * row_real + turn * row_imag
            imag = pltpu.roll(shared * row_imag - turn * row_real, sites, 1)
            head = jnp.where(lane < sites, real, imag)
            head_turned = pltpu.roll(head, rest, 1)
            values = (
                head,
                jnp.where(lane < rest, imag, 0.0),
                jnp.where(lane < rest, 0.0, head_turned),
                jnp.where(lane < rest, head_turned, pltpu.roll(imag, rest, 1)),
                shared * col_real - turn * col_imag,
                shared * col_imag + turn * col_real,
            )
            for f, value in enumerate(values):
                high = value.astype(bf16).astype(jnp.float32)
                edge_ref[f, pl.ds(base, peers, stride=capacity), :] = high
                edge_ref[f, pl.ds(half + base, peers, stride=capacity), :] = value - high
    for c in range(2):
        turned_ref[c] = edge_ref[4 + c].T
    mask = mask_ref[...]
    for c in range(2):
        for o in range(2):
            for q in range(0, pairs, 2):
                both = [turned_ref[c, pl.ds(2 * (q + d) + o, 1), :] * mask for d in range(2)]
                left_ref[2 * o + c, pl.ds(q * aux, 2 * aux), :] = jnp.concatenate(both, 0).astype(bf16)
    dot = functools.partial(jnp.dot, preferred_element_type=jnp.float32)
    spots = column_tiles(sites)
    hots = [column_ref[:, n * LANES : (n + 1) * LANES] for n in range(len(spots))]
    rights = [edge_ref[f].astype(bf16) for f in range(4)]
    row_spots = ((0, 0, 0), (0, 1, 1), (1, 1, 2), (1, 2, 3))
    terms = [[] for _ in range(tiles)]
    for n, (start, tile) in enumerate(spots):
        terms[tile].append((start // sites, hots[n]))
    for o, tile, f in row_spots:
        terms[tile].append((4 + o, rights[f]))
    cuts = [2 * (pairs * n // 16) for n in (0, 4, 7, 8)]
    copies = []
    for part, (low, high) in enumerate(zip(cuts, cuts[1:])):
        size = high - low
        here = pl.ds(low * aux, size * aux)
        lefts = [left_ref[n, here, :] for n in range(4)]
        lefts += [place_ref[o, here, :] for o in range(2)]
        for tile in range(tiles):
            left = jnp.concatenate([lefts[n] for n, _ in terms[tile]], axis=1)
            right = jnp.concatenate([right for _, right in terms[tile]], axis=0)
            placed = dot(left, right)
            for q in range(size):
                at = pl.ds(((low + q) * tiles + tile) * aux, aux)
                out_ref[at, :] = sum_ref[at, :] + placed[q * aux : (q + 1) * aux, :]
        here = pl.ds(low * tiles * aux, size * tiles * aux)
        copies.append(pltpu.make_async_copy(out_ref.at[here, :], out_hbm.at[here, :], sems.at[part]))
        copies[-1].start()
    for copy in copies:
        copy.wait()


def on_device(
    section_state,
    coupling,
    site_energy,
    bath_rate,
    bath_strength,
    bath_of_site,
    quanta,
    send_list,
    dest_slot,
):
    sites = coupling.shape[0]
    aux, flat = section_state.shape
    depth = quanta.shape[1]
    lane_count = send_list.shape[1]
    peers = lax.axis_size("aux")
    tiers = lax.axis_size("tier")
    capacity = lane_count // (2 * peers)
    sizes = (sites, aux, depth, peers, capacity, tiers)
    rows = aux * sites
    padded = rows + LANES - sites
    slabs = capacity * FIELDS
    chunks = flat // LANES
    half = -(-lane_count // 64) * 64
    f32 = jnp.float32
    bf16 = jnp.bfloat16
    band = lax.axis_index("tier").reshape(1)
    tiled = section_state.reshape(aux, chunks, LANES).transpose(1, 0, 2).reshape(-1, LANES)
    turned_quanta = quanta.T
    bath_row = bath_of_site.reshape(1, -1)
    rate_row = bath_rate.reshape(1, -1)
    strength_row = bath_strength.reshape(1, -1)
    pair_blocks = sites // (2 * SUB)

    def call(kernel, name, inputs, outs, scratch):
        spaces = [space for space, _ in inputs]
        values = [
            value if space is SMEM else pltpu.with_memory_space_constraint(value, space)
            for space, value in inputs
        ]
        return pl.pallas_call(
            functools.partial(kernel, sizes),
            out_shape=[space(shape, dtype) for space, shape, dtype in outs],
            in_specs=[spec(space) for space in spaces],
            out_specs=[spec(space) for space, _, _ in outs],
            scratch_shapes=scratch,
            name=name,
            compiler_params=pltpu.CompilerParams(vmem_limit_bytes=24 * 1024 * 1024),
        )(*values)

    HBM = pltpu.HBM
    dma = pltpu.SemaphoreType.DMA
    i32 = jnp.int32
    store_shape = (FIELDS, padded, LANES)
    reply_shape = (tiers * peers, 1, slabs * LANES)
    payload_shape = (tiers * peers, 1, (slabs + 1) * LANES)
    flat_shape = (aux * chunks, LANES)
    row_scratch = VMEM((2 * peers, 1, LANES), i32)
    trade = functools.partial(
        lax.all_to_all, axis_name=("tier", "aux"), split_axis=0, concat_axis=0, tiled=True
    )
    store, payload = call(
        pack_kernel,
        "pack",
        [(SMEM, band), (HBM, send_list), (HBM, turned_quanta), (HBM, dest_slot), (HBM, tiled)],
        [(VMEM, store_shape, f32), (VMEM, payload_shape, f32)],
        [
            VMEM(flat_shape, f32),
            VMEM(send_list.shape, i32),
            SMEM(turned_quanta.shape, i32),
            VMEM(dest_slot.shape, i32),
            VMEM((3, 1, LANES), i32),
            SMEM((lane_count,), i32),
            dma((pair_blocks,)),
            dma((3,)),
        ],
    )
    arrived = trade(payload).reshape(-1, LANES)
    (reply,) = call(
        answer_kernel,
        "answer",
        [(SMEM, band), (VMEM, arrived), (VMEM, store)],
        [(HBM, reply_shape, f32)],
        [VMEM((2, peers) + reply_shape[1:], f32), row_scratch, dma((2,))],
    )
    returned = trade(reply)
    total, columns, places, coefs, masks = call(
        middle_kernel,
        "middle",
        [
            (SMEM, band),
            (HBM, send_list),
            (HBM, turned_quanta),
            (HBM, bath_row),
            (HBM, rate_row),
            (HBM, strength_row),
            (HBM, coupling),
            (HBM, site_energy.reshape(1, -1)),
            (VMEM, arrived),
            (VMEM, store),
        ],
        [
            (VMEM, flat_shape, f32),
            (VMEM, (2 * half, len(column_tiles(sites)) * LANES), bf16),
            (VMEM, (2, rows // 2, 2 * half), bf16),
            (VMEM, (2, lane_count, LANES), f32),
            (VMEM, (aux, 2 * half), f32),
        ],
        [
            VMEM((4, padded, LANES), f32),
            VMEM((2, 2 * LANES, 2 * LANES), f32),
            VMEM((4, lane_count, LANES), f32),
            row_scratch,
            VMEM(coupling.shape, f32),
            VMEM((3, 1, sites), f32),
            VMEM(send_list.shape, i32),
            VMEM(bath_row.shape, i32),
            SMEM(turned_quanta.shape, i32),
            SMEM(bath_row.shape, i32),
            SMEM(rate_row.shape, f32),
            VMEM((5, 1, 2 * half), f32),
            dma((9,)),
        ],
    )
    (out,) = call(
        lower_kernel,
        "lower",
        [
            (SMEM, band),
            (VMEM, returned.reshape(-1, LANES)),
            (VMEM, total),
            (VMEM, columns),
            (VMEM, places),
            (VMEM, coefs),
            (VMEM, masks),
        ],
        [(HBM, flat_shape, f32)],
        [
            VMEM((6, 2 * half, LANES), f32),
            VMEM((2, LANES, 2 * half), f32),
            VMEM((4, rows // 2, 2 * half), bf16),
            VMEM(flat_shape, f32),
            dma((pair_blocks,)),
        ],
    )
    return out.reshape(chunks, aux, LANES).transpose(1, 0, 2).reshape(aux, flat)


def solution(mesh):
    return jax.shard_map(
        on_device,
        mesh=mesh,
        in_specs=(
            P(("tier", "aux"), None),
            P(),
            P(),
            P(),
            P(),
            P(),
            P(("tier", "aux"), None),
            P(("tier", "aux"), None),
            P(("tier", "aux"), None),
        ),
        out_specs=P(("tier", "aux"), None),
        check_vma=False,
    )
```

```python
import functools

import jax
import jax.numpy as jnp
from jax import lax
from jax.experimental import pallas as pl
from jax.experimental.pallas import tpu as pltpu
from jax.sharding import PartitionSpec as P

thermal = 0.5
LANES = 128
SUB = 8
FIELDS = 3
TAG = 64
VMEM = pltpu.VMEM
SMEM = pltpu.SMEM


def spec(space):
    return pl.BlockSpec(memory_space=space)


def lane_index(shape):
    return lax.broadcasted_iota(jnp.int32, shape, 1)


def fetch(pairs, sems):
    copies = [
        pltpu.make_async_copy(source, target, sems.at[n]) for n, (source, target) in enumerate(pairs)
    ]
    for copy in copies:
        copy.start()
    return copies


def send_blocks(work_ref, wire_hbm, sems, band, step, tiers, peers):
    def block(g):
        at = jnp.clip(band + g * step, 0, tiers - 1) * peers
        return pltpu.make_async_copy(work_ref.at[g], wire_hbm.at[pl.ds(at, peers)], sems.at[g])

    return block


def imaginary(first, second, lane, sites):
    spare = LANES - sites
    return jnp.where(lane < spare, pltpu.roll(first, spare, 1), pltpu.roll(second, spare, 1))


def unmerge(parts, lane, sites):
    first, second, third = parts
    kept = 2 * (LANES - sites)
    col_imag = jnp.where(lane < kept, pltpu.roll(second, kept, 1), pltpu.roll(third, kept, 1))
    return first, imaginary(first, second, lane, sites), pltpu.roll(third, sites, 1), col_imag


def pack_kernel(
    sizes,
    band_ref,
    send_hbm,
    quanta_hbm,
    slot_hbm,
    state_hbm,
    store_ref,
    payload_ref,
    state_ref,
    send_ref,
    quanta_ref,
    slot_ref,
    table_ref,
    row_ref,
    sems,
    table_sems,
):
    sites, aux, depth, peers, capacity, tiers = sizes
    tiles = 4 * sites // LANES
    pair_blocks = sites // (2 * SUB)
    chunk = aux * tiles * SUB
    rows = aux * sites
    tables = fetch(
        [(send_hbm, send_ref), (quanta_hbm, quanta_ref), (slot_hbm, slot_ref)], table_sems
    )
    copies = fetch(
        [(state_hbm, state_ref)],
        sems,
    )
    lane = lane_index((SUB, LANES))
    rest = 2 * sites - LANES
    store_ref[:, pl.ds(rows, LANES - sites), :] = jnp.zeros(
        (FIELDS, LANES - sites, LANES), jnp.float32
    )
    table_ref[...] = jnp.zeros_like(table_ref)
    for table in tables:
        table.wait()
    band = band_ref[0]
    row_lane = lane_index((1, LANES))
    entry = send_ref[...]
    lane_count = entry.shape[1]
    site = jnp.full(entry.shape, -1, jnp.int32)
    base = jnp.zeros(entry.shape, jnp.int32)
    for source in range(aux):
        for place in range(depth):
            here = entry == source * depth + place
            site = jnp.where(here, quanta_ref[place, source], site)
            base = jnp.where(here, source * sites, base)
    group = (lane_index(entry.shape) >= peers * capacity).astype(jnp.int32)
    usable = (entry >= 0) & (site >= 0) & (band - group >= 0)
    site = jnp.maximum(site, 0)
    table_ref[0, :, pl.ds(0, lane_count)] = base + site
    table_ref[1, :, pl.ds(0, lane_count)] = jnp.where(usable, slot_ref[...] * sites, rows)
    table_ref[2, :, pl.ds(0, lane_count)] = jnp.where(usable, site, 0)
    slot_tags, site_tags = table_ref[1], table_ref[2]
    for g in (1, 0):
        for q in range(peers):
            at = (g * peers + q) * capacity
            tags = jnp.where(
                row_lane < TAG,
                pltpu.roll(slot_tags, (LANES - at) % LANES, 1),
                pltpu.roll(site_tags, (LANES + TAG - at) % LANES, 1),
            )
            at_row = jnp.maximum(band - g, 0) * peers + q
            payload_ref[at_row, :, pl.ds(capacity * FIELDS * LANES, LANES)] = tags.astype(
                jnp.float32
            )
    for l in range(lane_count):
        row_ref[l] = table_ref[0, 0, l]
    for copy in copies:
        copy.wait()
    for block in range(pair_blocks):
        for a in range(aux):
            first, middle, last = (
                state_ref[pl.ds(a + aux * (tiles * SUB * block + u), SUB, stride=aux * tiles), :]
                for u in range(tiles)
            )
            mixed_turned = pltpu.roll(jnp.where(lane < rest, last, middle), rest, 1)
            last_turned = pltpu.roll(last, rest, 1)
            base = a * sites + 2 * SUB * block
            store_ref[0, pl.ds(base, SUB, stride=2), :] = first
            store_ref[1, pl.ds(base, SUB, stride=2), :] = jnp.where(lane < rest, middle, first)
            store_ref[0, pl.ds(base + 1, SUB, stride=2), :] = mixed_turned
            store_ref[1, pl.ds(base + 1, SUB, stride=2), :] = last_turned
    kept = LANES - rest
    tail = sites - kept
    wide = lane_index((sites, LANES))
    for a in range(aux):
        here = pl.ds(a * sites, sites)
        first, second = store_ref[0, here, :], store_ref[1, here, :]
        columns = jnp.concatenate([first[kept:, :], first], axis=0).T[:sites, :]
        turned = jnp.concatenate([second[kept:, :], second[kept:, :], second[:kept, :]], axis=0).T
        turned = jnp.concatenate([turned[LANES - tail :, :], turned[:rest, :]], axis=0)
        store_ref[1, here, :] = jnp.where(wide < rest, second, turned)
        store_ref[2, here, :] = jnp.where(wide < tail, turned, columns)
    for g in (1, 0):
        for q in range(peers):
            at_row = jnp.maximum(band - g, 0) * peers + q
            for j in range(capacity):
                row = pl.ds(row_ref[(g * peers + q) * capacity + j], 1)
                for f in range(FIELDS):
                    payload_ref[at_row, :, pl.ds((j * FIELDS + f) * LANES, LANES)] = store_ref[
                        f, row, :
                    ]


def read_rows(sizes, band, arrived_ref, row_ref):
    sites, aux, depth, peers, capacity, tiers = sizes
    slabs = capacity * FIELDS + 1
    for g in range(2):
        origin = jnp.minimum(band + g, tiers - 1) * peers
        for p in range(peers):
            tags = arrived_ref[pl.ds((origin + p) * slabs + slabs - 1, 1), :]
            total = (tags + pltpu.roll(tags, TAG, 1)).astype(jnp.int32)
            row_ref[g * peers + p] = jnp.where(band + g < tiers, total, aux * sites)


def answer_kernel(sizes, band_ref, arrived_ref, store_ref, reply_hbm, reply_ref, row_ref, wire_sems):
    sites, aux, depth, peers, capacity, tiers = sizes
    band = band_ref[0]
    block = send_blocks(reply_ref, reply_hbm, wire_sems, band, 1, tiers, peers)
    read_rows(sizes, band, arrived_ref, row_ref)
    for g in (1, 0):
        for p in range(peers):
            for j in range(capacity):
                row = pl.ds(row_ref[g * peers + p, 0, j], 1)
                for f in range(FIELDS):
                    reply_ref[g, p, :, pl.ds((j * FIELDS + f) * LANES, LANES)] = store_ref[f, row, :]
        if g == 0:
            block(g).start()
        else:
            pl.when(band + g < tiers)(block(g).start)
    block(0).wait()
    pl.when(band + 1 < tiers)(block(1).wait)


def split(value):
    high = value.astype(jnp.bfloat16)
    low = (value - high.astype(jnp.float32)).astype(jnp.bfloat16)
    return high, low


def column_tiles(sites):
    spots = []
    for field in range(4):
        start = field * sites
        first, last = start // LANES, (start + sites - 1) // LANES
        spots += [(start, tile) for tile in range(first, last + 1)]
    return spots


def spread(row):
    return jnp.broadcast_to(row, (row.shape[1], row.shape[1])).T


def middle_kernel(
    sizes,
    band_ref,
    send_hbm,
    quanta_hbm,
    bath_hbm,
    rate_hbm,
    strength_hbm,
    coupling_hbm,
    energy_hbm,
    arrived_ref,
    store_ref,
    sum_ref,
    column_ref,
    place_ref,
    coef_ref,
    mask_ref,
    work_ref,
    matrix_ref,
    edge_ref,
    row_ref,
    coupling_ref,
    vector_ref,
    send_ref,
    bath_row,
    quanta_ref,
    bath_ref,
    rate_ref,
    index_ref,
    sems,
):
    sites, aux, depth, peers, capacity, tiers = sizes
    rows = aux * sites
    rest = 2 * sites - LANES
    f32 = jnp.float32
    band = band_ref[0]
    copies = fetch(
        [
            (coupling_hbm, coupling_ref),
            (energy_hbm, vector_ref.at[0]),
            (rate_hbm, vector_ref.at[1]),
            (strength_hbm, vector_ref.at[2]),
            (send_hbm, send_ref),
            (bath_hbm, bath_row),
            (quanta_hbm, quanta_ref),
            (bath_hbm, bath_ref),
            (rate_hbm, rate_ref),
        ],
        sems,
    )
    read_rows(sizes, band, arrived_ref, row_ref)
    lane = lane_index((peers, LANES))
    for g in range(2):
        origin = jnp.minimum(band + g, tiers - 1) * peers
        for j in range(capacity):
            slabs = capacity * FIELDS + 1
            parts = [
                arrived_ref[pl.ds(origin * slabs + j * FIELDS + f, peers, stride=slabs), :]
                for f in range(FIELDS)
            ]
            row_real, row_imag, col_real, col_imag = unmerge(parts, lane, sites)
            for f, value in enumerate((row_imag, -row_real, -col_imag, col_real)):
                edge_ref[f, pl.ds(g * peers * capacity + j, peers, stride=capacity), :] = value
    matrix_ref[...] = jnp.zeros_like(matrix_ref)
    index_ref[...] = jnp.full(index_ref.shape, -1.0, f32)
    work_ref[:, pl.ds(rows, LANES - sites), :] = jnp.zeros((4, LANES - sites, LANES), f32)
    for copy in copies:
        copy.wait()
    row_ids = lax.broadcasted_iota(jnp.int32, (sites, sites), 0)
    col_ids = lane_index((sites, sites))
    coupling = coupling_ref[...]
    hamilton = (coupling + coupling.T) * 0.5 + jnp.where(row_ids == col_ids, vector_ref[0], 0.0)
    real, imag = pl.ds(0, sites), pl.ds(LANES, sites)
    matrix_ref[0, real, imag] = hamilton
    matrix_ref[0, pl.ds(sites, sites), real] = -hamilton
    matrix_ref[1, pl.ds(rest, sites), real] = hamilton
    matrix_ref[1, pl.ds(2 * LANES - sites, sites), imag] = -hamilton
    dot = functools.partial(jnp.dot, preferred_element_type=f32)
    splits = [split(matrix_ref[half]) for half in range(2)]
    lane = lane_index((sites, LANES))
    for a in range(aux):
        damp = f32(0.0)
        for place in range(depth):
            site = quanta_ref[place, a]
            rate = rate_ref[0, bath_ref[0, jnp.maximum(site, 0)]]
            damp = damp + jnp.where(site >= 0, rate, 0.0)
        here = pl.ds(a * sites, sites)
        for half in range(2):
            high, low = splits[half]
            first, second = store_ref[half, here, :], store_ref[half + 1, here, :]
            both_high, both_low = split(jnp.concatenate([first, second], axis=1))
            product = dot(both_high, high) + (dot(both_low, high) + dot(both_high, low))
            pair = [product[:, :LANES], product[:, LANES:]]
            if half == 0:
                pair[0] = pair[0] - damp * first
                pair[1] = pair[1] - damp * imaginary(first, second, lane, sites)
            for c in range(2):
                work_ref[2 * half + c, here, :] = pair[c]

    entry = send_ref[...]
    lane_count = entry.shape[1]
    half = index_ref.shape[2] // 2
    site = jnp.full(entry.shape, -1, jnp.int32)
    source = jnp.zeros(entry.shape, jnp.int32)
    for a in range(aux):
        for place in range(depth):
            hit = entry == a * depth + place
            site = jnp.where(hit, quanta_ref[place, a], site)
            source = jnp.where(hit, a, source)
    weight = jnp.zeros(entry.shape, f32)
    for a in range(aux):
        for place in range(depth):
            hit = (source == a) & (site == quanta_ref[place, a])
            weight = weight + jnp.where(hit, 1.0, 0.0)
    group = (lane_index(entry.shape) >= peers * capacity).astype(jnp.int32)
    usable = (entry >= 0) & (site >= 0) & (band - group >= 0)
    weight = jnp.where(usable, weight, 0.0)
    bath_of = spread(bath_row[...].astype(f32)) == col_ids.astype(f32)
    rate_of = jnp.sum(jnp.where(bath_of, vector_ref[1], 0.0), axis=1, keepdims=True)
    strength_of = jnp.sum(jnp.where(bath_of, vector_ref[2], 0.0), axis=1, keepdims=True)
    at_site = lax.broadcasted_iota(jnp.int32, (sites, lane_count), 0) == site
    rate = jnp.sum(jnp.where(at_site, rate_of, 0.0), axis=0, keepdims=True)
    strength = jnp.sum(jnp.where(at_site, strength_of, 0.0), axis=0, keepdims=True)
    lanes = pl.ds(0, lane_count)
    index_ref[3, :, lanes] = -weight * (strength * rate)
    index_ref[4, :, lanes] = weight * (2.0 * thermal * strength)
    for c in range(2):
        coef_ref[c] = spread(index_ref[3 + c, :, pl.ds(0, LANES)])[:lane_count, :]
    rows_of = (
        jnp.where(usable, source * sites + site, -1),
        jnp.where(usable, site, -2 * LANES),
        jnp.where(usable, source, -1),
    )
    for start in (0, half):
        for c in range(3):
            index_ref[c, :, pl.ds(start, lane_count)] = rows_of[c].astype(f32)
    tiles = 4 * sites // LANES
    pairs = sites // 2
    for slab in range(2 * half // LANES):
        part = pl.ds(slab * LANES, LANES)
        turned = spread(index_ref[1, :, part])
        here = lane_index((LANES, LANES))
        for n, (offset, tile) in enumerate(column_tiles(sites)):
            hot = turned == (here + (tile * LANES - offset)).astype(f32)
            column_ref[part, pl.ds(n * LANES, LANES)] = jnp.where(hot, 1.0, 0.0).astype(jnp.bfloat16)
        at_aux = lax.broadcasted_iota(jnp.int32, (aux, LANES), 0).astype(f32)
        mask_ref[:, part] = jnp.where(index_ref[2, :, part] == at_aux, 1.0, 0.0)
        for o in range(2):
            shape = (pairs, aux, LANES)
            at = 2 * lax.broadcasted_iota(jnp.int32, shape, 0) + o
            at = at + sites * lax.broadcasted_iota(jnp.int32, shape, 1)
            hot = index_ref[0, :, part] == at.reshape(pairs * aux, LANES).astype(f32)
            place_ref[o, :, part] = jnp.where(hot, 1.0, 0.0).astype(jnp.bfloat16)

    for g in range(2):
        for p in range(peers):
            for j in range(capacity):
                l = (g * peers + p) * capacity + j
                row = pl.ds(row_ref[g * peers + p, 0, j], 1)
                for c in range(4):
                    work_ref[c, row, :] = work_ref[c, row, :] + edge_ref[c, pl.ds(l, 1), :]
    for a in range(aux):
        here = pl.ds(a * sites, sites)
        for c in range(2):
            turned = work_ref[2 + c, pl.ds(a * sites, LANES), :].T[:sites, :]
            work_ref[c, here, :] = work_ref[c, here, :] + turned
    pair_blocks = sites // (2 * SUB)
    lane = lane_index((SUB, LANES))
    for block in range(pair_blocks):
        for a in range(aux):
            base = a * sites + 2 * SUB * block
            even_real, even_imag, odd_real, odd_imag = (
                work_ref[c, pl.ds(base + o, SUB, stride=2), :] for o in (0, 1) for c in (0, 1)
            )
            turned_imag = pltpu.roll(even_imag, 96, 1)
            turned_real = pltpu.roll(odd_real, 64, 1)
            parts = (
                jnp.where(lane < 96, even_real, turned_imag),
                jnp.where(lane < 64, turned_imag, turned_real),
                jnp.where(lane < 32, turned_real, pltpu.roll(odd_imag, 32, 1)),
            )
            for u in range(tiles):
                start = a + aux * (tiles * SUB * block + u)
                sum_ref[pl.ds(start, SUB, stride=aux * tiles), :] = parts[u]


def lower_kernel(
    sizes,
    band_ref,
    returned_ref,
    sum_ref,
    column_ref,
    place_ref,
    coef_ref,
    mask_ref,
    out_hbm,
    edge_ref,
    turned_ref,
    left_ref,
    out_ref,
    sems,
):
    sites, aux, depth, peers, capacity, tiers = sizes
    tiles = 4 * sites // LANES
    pairs = sites // 2
    slabs = capacity * FIELDS
    used = 2 * capacity * peers
    half = edge_ref.shape[1] // 2
    rest = 2 * sites - LANES
    bf16 = jnp.bfloat16
    band = band_ref[0]
    lane = lane_index((peers, LANES))
    if used < half:
        for top in (used, half + used):
            edge_ref[:, pl.ds(top, half - used), :] = jnp.zeros(
                (6, half - used, LANES), jnp.float32
            )
    for g in range(2):
        target = jnp.maximum(band - g, 0)
        for j in range(capacity):
            start = target * (peers * slabs) + j * FIELDS
            parts = [
                returned_ref[pl.ds(start + f, peers, stride=slabs), :] for f in range(FIELDS)
            ]
            row_real, row_imag, col_real, col_imag = unmerge(parts, lane, sites)
            base = g * peers * capacity + j
            shared = coef_ref[0, pl.ds(base, peers, stride=capacity), :]
            turn = coef_ref[1, pl.ds(base, peers, stride=capacity), :]
            real = shared * row_real + turn * row_imag
            imag = pltpu.roll(shared * row_imag - turn * row_real, sites, 1)
            head = jnp.where(lane < sites, real, imag)
            head_turned = pltpu.roll(head, rest, 1)
            values = (
                head,
                jnp.where(lane < rest, imag, 0.0),
                jnp.where(lane < rest, 0.0, head_turned),
                jnp.where(lane < rest, head_turned, pltpu.roll(imag, rest, 1)),
                shared * col_real - turn * col_imag,
                shared * col_imag + turn * col_real,
            )
            for f, value in enumerate(values):
                high = value.astype(bf16).astype(jnp.float32)
                edge_ref[f, pl.ds(base, peers, stride=capacity), :] = high
                edge_ref[f, pl.ds(half + base, peers, stride=capacity), :] = value - high
    for c in range(2):
        turned_ref[c] = edge_ref[4 + c].T
    mask = mask_ref[...]
    for c in range(2):
        for o in range(2):
            for q in range(0, pairs, 2):
                both = [turned_ref[c, pl.ds(2 * (q + d) + o, 1), :] * mask for d in range(2)]
                left_ref[2 * o + c, pl.ds(q * aux, 2 * aux), :] = jnp.concatenate(both, 0).astype(bf16)
    dot = functools.partial(jnp.dot, preferred_element_type=jnp.float32)
    spots = column_tiles(sites)
    hots = [column_ref[:, n * LANES : (n + 1) * LANES] for n in range(len(spots))]
    rights = [edge_ref[f].astype(bf16) for f in range(4)]
    row_spots = ((0, 0, 0), (0, 1, 1), (1, 1, 2), (1, 2, 3))
    terms = [[] for _ in range(tiles)]
    for n, (start, tile) in enumerate(spots):
        terms[tile].append((start // sites, hots[n]))
    for o, tile, f in row_spots:
        terms[tile].append((4 + o, rights[f]))
    parts = 3
    size = pairs // parts
    copies = []
    for part in range(parts):
        here = pl.ds(part * size * aux, size * aux)
        lefts = [left_ref[n, here, :] for n in range(4)]
        lefts += [place_ref[o, here, :] for o in range(2)]
        for tile in range(tiles):
            left = jnp.concatenate([lefts[n] for n, _ in terms[tile]], axis=1)
            right = jnp.concatenate([right for _, right in terms[tile]], axis=0)
            placed = dot(left, right)
            for q in range(size):
                at = pl.ds(((part * size + q) * tiles + tile) * aux, aux)
                out_ref[at, :] = sum_ref[at, :] + placed[q * aux : (q + 1) * aux, :]
        here = pl.ds(part * size * tiles * aux, size * tiles * aux)
        copies.append(pltpu.make_async_copy(out_ref.at[here, :], out_hbm.at[here, :], sems.at[part]))
        copies[-1].start()
    for copy in copies:
        copy.wait()


def on_device(
    section_state,
    coupling,
    site_energy,
    bath_rate,
    bath_strength,
    bath_of_site,
    quanta,
    send_list,
    dest_slot,
):
    sites = coupling.shape[0]
    aux, flat = section_state.shape
    depth = quanta.shape[1]
    lane_count = send_list.shape[1]
    peers = lax.axis_size("aux")
    tiers = lax.axis_size("tier")
    capacity = lane_count // (2 * peers)
    sizes = (sites, aux, depth, peers, capacity, tiers)
    rows = aux * sites
    padded = rows + LANES - sites
    slabs = capacity * FIELDS
    chunks = flat // LANES
    half = -(-lane_count // 64) * 64
    f32 = jnp.float32
    bf16 = jnp.bfloat16
    band = lax.axis_index("tier").reshape(1)
    tiled = section_state.reshape(aux, chunks, LANES).transpose(1, 0, 2).reshape(-1, LANES)
    turned_quanta = quanta.T
    bath_row = bath_of_site.reshape(1, -1)
    rate_row = bath_rate.reshape(1, -1)
    strength_row = bath_strength.reshape(1, -1)
    pair_blocks = sites // (2 * SUB)

    def call(kernel, name, inputs, outs, scratch):
        spaces = [space for space, _ in inputs]
        values = [
            value if space is SMEM else pltpu.with_memory_space_constraint(value, space)
            for space, value in inputs
        ]
        return pl.pallas_call(
            functools.partial(kernel, sizes),
            out_shape=[space(shape, dtype) for space, shape, dtype in outs],
            in_specs=[spec(space) for space in spaces],
            out_specs=[spec(space) for space, _, _ in outs],
            scratch_shapes=scratch,
            name=name,
            compiler_params=pltpu.CompilerParams(vmem_limit_bytes=24 * 1024 * 1024),
        )(*values)

    HBM = pltpu.HBM
    dma = pltpu.SemaphoreType.DMA
    i32 = jnp.int32
    store_shape = (FIELDS, padded, LANES)
    reply_shape = (tiers * peers, 1, slabs * LANES)
    payload_shape = (tiers * peers, 1, (slabs + 1) * LANES)
    flat_shape = (aux * chunks, LANES)
    row_scratch = VMEM((2 * peers, 1, LANES), i32)
    trade = functools.partial(
        lax.all_to_all, axis_name=("tier", "aux"), split_axis=0, concat_axis=0, tiled=True
    )
    store, payload = call(
        pack_kernel,
        "pack",
        [(SMEM, band), (HBM, send_list), (HBM, turned_quanta), (HBM, dest_slot), (HBM, tiled)],
        [(VMEM, store_shape, f32), (VMEM, payload_shape, f32)],
        [
            VMEM(flat_shape, f32),
            VMEM(send_list.shape, i32),
            SMEM(turned_quanta.shape, i32),
            VMEM(dest_slot.shape, i32),
            VMEM((3, 1, LANES), i32),
            SMEM((lane_count,), i32),
            dma((pair_blocks,)),
            dma((3,)),
        ],
    )
    arrived = trade(payload).reshape(-1, LANES)
    (reply,) = call(
        answer_kernel,
        "answer",
        [(SMEM, band), (VMEM, arrived), (VMEM, store)],
        [(HBM, reply_shape, f32)],
        [VMEM((2, peers) + reply_shape[1:], f32), row_scratch, dma((2,))],
    )
    returned = trade(reply)
    total, columns, places, coefs, masks = call(
        middle_kernel,
        "middle",
        [
            (SMEM, band),
            (HBM, send_list),
            (HBM, turned_quanta),
            (HBM, bath_row),
            (HBM, rate_row),
            (HBM, strength_row),
            (HBM, coupling),
            (HBM, site_energy.reshape(1, -1)),
            (VMEM, arrived),
            (VMEM, store),
        ],
        [
            (VMEM, flat_shape, f32),
            (VMEM, (2 * half, len(column_tiles(sites)) * LANES), bf16),
            (VMEM, (2, rows // 2, 2 * half), bf16),
            (VMEM, (2, lane_count, LANES), f32),
            (VMEM, (aux, 2 * half), f32),
        ],
        [
            VMEM((4, padded, LANES), f32),
            VMEM((2, 2 * LANES, 2 * LANES), f32),
            VMEM((4, lane_count, LANES), f32),
            row_scratch,
            VMEM(coupling.shape, f32),
            VMEM((3, 1, sites), f32),
            VMEM(send_list.shape, i32),
            VMEM(bath_row.shape, i32),
            SMEM(turned_quanta.shape, i32),
            SMEM(bath_row.shape, i32),
            SMEM(rate_row.shape, f32),
            VMEM((5, 1, 2 * half), f32),
            dma((9,)),
        ],
    )
    (out,) = call(
        lower_kernel,
        "lower",
        [
            (SMEM, band),
            (VMEM, returned.reshape(-1, LANES)),
            (VMEM, total),
            (VMEM, columns),
            (VMEM, places),
            (VMEM, coefs),
            (VMEM, masks),
        ],
        [(HBM, flat_shape, f32)],
        [
            VMEM((6, 2 * half, LANES), f32),
            VMEM((2, LANES, 2 * half), f32),
            VMEM((4, rows // 2, 2 * half), bf16),
            VMEM(flat_shape, f32),
            dma((pair_blocks,)),
        ],
    )
    return out.reshape(chunks, aux, LANES).transpose(1, 0, 2).reshape(aux, flat)


def solution(mesh):
    return jax.shard_map(
        on_device,
        mesh=mesh,
        in_specs=(
            P(("tier", "aux"), None),
            P(),
            P(),
            P(),
            P(),
            P(),
            P(("tier", "aux"), None),
            P(("tier", "aux"), None),
            P(("tier", "aux"), None),
        ),
        out_specs=P(("tier", "aux"), None),
        check_vma=False,
    )
```
